32 devices in a mesh: sens: 2 (over x), src: 16 (over z, y, core).
Axes of the slice: x: 2, y: 2, z: 4, core: 2. Of those that a mesh axis runs over, the one named last changes fastest.
Arguments:
- slip_param: float32 [1024, 384], P(('src', 'sens')), may hold values from -4 to 4
- rigidity: float32 [1024], P(('src', 'sens')), may hold values from 1 to 36
- kernel: bfloat16 [2, 512, 1024, 384], P(None, 'sens', 'src'), may hold values from -0.08984375 to 0.08984375
- observed: float32 [512, 384], P('sens'), may hold values from -6 to 6
Outputs:
- final_param: float32 [1024, 384], P(('src', 'sens'))
- misfit: float32 [512, 384], P(('sens', 'src'))
The draws below stay inside these ranges and needn't reach their ends.
All inputs are finite; a program needn't handle non-finite values.
Results may differ from the reference program's by a relative error of at most 0.0003.
Values sent between devices are 32-bit elements; how exact they have to be, the bound alone decides.
No kernel may reach another device: no remote copies, remote signals or barrier semaphores. Data moves between devices by JAX's collectives and lax.ppermute only.
A program may use at most 64 MiB of HBM per device.

```python
import math
import jax
import jax.numpy as jnp
from jax import lax

SOURCES = 1024
SENSORS = 512
TIMES = 384
ITERS = 3
FREQS = 384


def draw_rigidity(key, part):
    position = jnp.arange(SOURCES, dtype=jnp.float32) / (SOURCES - 1)
    rough = jax.random.uniform(key, (SOURCES,), jnp.float32, 0.0, math.log(4.0))
    rise = math.log(3.0)
    return jnp.exp(rise * position + rough)


def spiked(entries, own_key, source, target, shards_of, factor):
    def block_of(dim):
        return (jnp.arange(entries.shape[dim]) // (entries.shape[dim] // shards_of)).reshape((-1,) + (1,) * (entries.ndim - 1 - dim))

    first = jax.random.permutation(own_key, shards_of)[block_of(target)]
    other_side = (block_of(target) + shards_of // 2) % shards_of
    return jnp.where((block_of(source) == first) | (block_of(source) == other_side), factor * entries, entries)


def block_scale(own_key, extent, pieces, smallest, top_value):
    def one(dim, shards_of):
        steps = jax.random.uniform(jax.random.fold_in(jax.random.fold_in(own_key, 6), dim), (shards_of,), jnp.float32, smallest / len(pieces), top_value / len(pieces))
        return jnp.repeat(jnp.exp(steps), extent[dim] // shards_of).reshape((-1,) + (1,) * (len(extent) - dim - 1))

    gain = one(*pieces[0])
    for cut in pieces[1:]:
        gain = gain * one(*cut)
    return gain


def bell_draw(own_key, dims, width, bound, pieces=(), kind=jnp.bfloat16):
    gain = block_scale(own_key, dims, pieces, -0.22, 0.18) if pieces else 1.0
    entries = jax.random.normal(own_key, dims, jnp.float32) * width * gain
    return jnp.minimum(jnp.maximum(entries, -bound), bound).astype(kind)


def heavy_noise(rng, extent, width, most, cuts, heavy, kind=jnp.bfloat16):
    result = width * jax.random.normal(rng, extent, jnp.float32)
    if cuts:
        result = result * block_scale(rng, extent, cuts, -0.22, 0.18)
    return jnp.clip(spiked(result, jax.random.fold_in(rng, 3), *heavy), -most, most).astype(kind)


def setup_inputs(seed: int = 0) -> dict:
    splits = jax.random.split(jax.random.key(seed), 5)
    return {
        "slip_param": bell_draw(splits[0], (SOURCES, TIMES), 1.0, 4.0, ((0, 32),), jnp.float32),
        "rigidity": draw_rigidity(jax.random.fold_in(splits[4], 71), 0),
        "kernel": heavy_noise(splits[2], (2, SENSORS, SOURCES, FREQS), 0.015, 0.08984375, ((1, 2), (2, 16)), (2, 1, 16, 2.0)),
        "observed": bell_draw(splits[3], (SENSORS, TIMES), 1.0, 6.0, ((0, 2),), jnp.float32),
    }


highest = lax.Precision.HIGHEST
step_rate = 0.3
epsilon = 1e-06

def forward_table(length):
    padded = 2 * length
    sample_index = jnp.arange(length, dtype=jnp.int32)[:, None]
    freq_index = jnp.arange(length, dtype=jnp.int32)[None, :]
    phases = (sample_index * freq_index % padded).astype(jnp.float32) * (2.0 * math.pi / padded)
    return jnp.concatenate([jnp.cos(phases), -jnp.sin(phases)], axis=1)

def spectral_weights(length):
    padded = 2 * length
    column = jnp.arange(2 * length, dtype=jnp.int32) % length
    return jnp.where(column == 0, 1.0 / padded, 2.0 / padded).astype(jnp.float32)

def forward_terms(kernel, spectra):
    freqs = kernel.shape[-1]
    real_part = spectra[:, :freqs][None]
    imag_part = spectra[:, freqs:][None]
    kernel_real = kernel[0].astype(jnp.float32)
    kernel_imag = kernel[1].astype(jnp.float32)
    out_real = lax.optimization_barrier(jnp.sum(kernel_real * real_part - kernel_imag * imag_part, axis=1))
    out_imag = lax.optimization_barrier(jnp.sum(kernel_real * imag_part + kernel_imag * real_part, axis=1))
    return jnp.concatenate([out_real, out_imag], axis=1)

def adjoint_terms(kernel, spectra):
    freqs = kernel.shape[-1]
    real_part = spectra[:, :freqs][:, None]
    imag_part = spectra[:, freqs:][:, None]
    kernel_real = kernel[0].astype(jnp.float32)
    kernel_imag = kernel[1].astype(jnp.float32)
    back_real = lax.optimization_barrier(jnp.sum(kernel_real * real_part + kernel_imag * imag_part, axis=0))
    back_imag = lax.optimization_barrier(jnp.sum(kernel_real * imag_part - kernel_imag * real_part, axis=0))
    return jnp.concatenate([back_real, back_imag], axis=1)

def forward_all(kernel, spectra):

    def one_block(index):
        piece = lax.dynamic_slice_in_dim(kernel, (index * 32).astype(jnp.int32), 32, 1)
        return forward_terms(piece, spectra)
    stacked = lax.map(one_block, jnp.arange(SENSORS // 32, dtype=jnp.int32))
    return stacked.reshape(SENSORS, -1)

def adjoint_all(kernel, spectra):

    def one_block(index):
        piece = lax.dynamic_slice_in_dim(kernel, (index * 32).astype(jnp.int32), 32, 2)
        return adjoint_terms(piece, spectra)
    stacked = lax.map(one_block, jnp.arange(SOURCES // 32, dtype=jnp.int32))
    return stacked.reshape(SOURCES, -1)

def reference(slip_param, rigidity, kernel, observed):
    table = forward_table(TIMES)
    weighted = table * spectral_weights(TIMES)[None, :]
    scale_rows = rigidity[:, None]
    param = slip_param
    misfit = observed
    for iteration in range(ITERS):
        slip = scale_rows * jax.nn.softplus(param)
        spectra = jnp.dot(slip, table, precision=highest)
        pred_spectra = forward_all(kernel, spectra)
        prediction = jnp.dot(pred_spectra, weighted.T, precision=highest)
        misfit = prediction - observed
        adjoint_spec = jnp.dot(misfit, weighted, precision=highest)
        back = adjoint_all(kernel, adjoint_spec)
        gradient = jnp.dot(back, table.T, precision=highest) * scale_rows * jax.nn.sigmoid(param)
        root_mean = jnp.sqrt(jnp.mean(gradient * gradient) + epsilon)
        param = param - step_rate * gradient / root_mean
    return (param, misfit)
```

```python
import math

import jax
import jax.numpy as jnp
from jax import lax
from jax.sharding import Mesh, PartitionSpec as P

ITERS = 3

highest = lax.Precision.HIGHEST
step_rate = 0.3
epsilon = 1e-06


def forward_table(length):
    padded = 2 * length
    sample_index = jnp.arange(length, dtype=jnp.int32)[:, None]
    freq_index = jnp.arange(length, dtype=jnp.int32)[None, :]
    phases = (sample_index * freq_index % padded).astype(jnp.float32) * (2.0 * math.pi / padded)
    return jnp.concatenate([jnp.cos(phases), -jnp.sin(phases)], axis=1)


def spectral_weights(length):
    padded = 2 * length
    column = jnp.arange(2 * length, dtype=jnp.int32) % length
    return jnp.where(column == 0, 1.0 / padded, 2.0 / padded).astype(jnp.float32)


def forward_terms(kernel, spectra):
    freqs = kernel.shape[-1]
    real_part = spectra[:, :freqs][None]
    imag_part = spectra[:, freqs:][None]
    kernel_real = kernel[0].astype(jnp.float32)
    kernel_imag = kernel[1].astype(jnp.float32)
    out_real = jnp.sum(kernel_real * real_part - kernel_imag * imag_part, axis=1)
    out_imag = jnp.sum(kernel_real * imag_part + kernel_imag * real_part, axis=1)
    return jnp.concatenate([out_real, out_imag], axis=1)


def adjoint_terms(kernel, spectra):
    freqs = kernel.shape[-1]
    real_part = spectra[:, :freqs][:, None]
    imag_part = spectra[:, freqs:][:, None]
    kernel_real = kernel[0].astype(jnp.float32)
    kernel_imag = kernel[1].astype(jnp.float32)
    back_real = jnp.sum(kernel_real * real_part + kernel_imag * imag_part, axis=0)
    back_imag = jnp.sum(kernel_real * imag_part - kernel_imag * real_part, axis=0)
    return jnp.concatenate([back_real, back_imag], axis=1)


def swap_cores(x):
    return lax.ppermute(x, "core", [(0, 1), (1, 0)])


def gather_sens(x):
    if lax.axis_size("sens") == 2:
        first = lax.axis_index("sens") == 0
        other = lax.ppermute(x, "sens", [(0, 1), (1, 0)])
        return jnp.concatenate([jnp.where(first, x, other), jnp.where(first, other, x)], axis=0)
    return lax.all_gather(x, "sens", axis=0, tiled=True)


def sum_sens(x):
    if lax.axis_size("sens") == 2:
        return x + lax.ppermute(x, "sens", [(0, 1), (1, 0)])
    return lax.psum(x, "sens")


def scatter_sum_src(x):
    chips, cores = lax.axis_size("chip"), lax.axis_size("core")
    x = x.reshape(chips, cores, -1, x.shape[-1])
    if cores == 2:
        first = lax.axis_index("core") == 0
        keep = jnp.where(first, x[:, 0], x[:, 1])
        send = jnp.where(first, x[:, 1], x[:, 0])
        x = keep + swap_cores(send)
    else:
        x = x[:, 0]
    return jnp.sum(lax.all_to_all(x, "chip", 0, 0), axis=0)


def gather_src(x):
    chips, cores = lax.axis_size("chip"), lax.axis_size("core")
    rows, width = x.shape
    mine = lax.all_to_all(jnp.broadcast_to(x[None], (chips, rows, width)), "chip", 0, 0)
    if cores == 2:
        first = lax.axis_index("core") == 0
        other = swap_cores(mine)
        mine = jnp.stack([jnp.where(first, mine, other), jnp.where(first, other, mine)], axis=1)
    return mine.reshape(chips * cores * rows, width)


def sum_src_scalar(value):
    count = lax.axis_size("chip") * lax.axis_size("core")
    sent = jnp.broadcast_to(value.reshape(1, 1), (count, 128))
    return jnp.sum(lax.all_to_all(sent, ("chip", "core"), 0, 0)[:, 0])


def local(slip_param, rigidity, kernel, observed):
    length = slip_param.shape[1]
    own_sources = slip_param.shape[0]
    table = forward_table(length)
    weighted = table * spectral_weights(length)[None, :]
    src = lax.axis_size("chip") * lax.axis_size("core")
    src_index = lax.axis_index("chip") * lax.axis_size("core") + lax.axis_index("core")
    own_count = kernel.shape[1] // src
    own_observed = lax.dynamic_slice_in_dim(observed, src_index * own_count, own_count, 0)
    entry_count = own_sources * lax.axis_size("sens") * src * length
    packed = gather_sens(jnp.concatenate([slip_param, jnp.broadcast_to(rigidity[:, None], (own_sources, 128))], axis=1))
    param, scale_rows = packed[:, :length], packed[:, length:length + 1]
    misfit = own_observed
    for iteration in range(ITERS):
        slip = scale_rows * jax.nn.softplus(param)
        spectra = jnp.dot(slip, table, precision=highest)
        terms = forward_terms(kernel, spectra)
        terms = jnp.dot(terms, weighted.T, precision=highest)
        misfit = scatter_sum_src(terms) - own_observed
        residual = gather_src(misfit)
        adjoint_spec = jnp.dot(residual, weighted, precision=highest)
        back_terms = adjoint_terms(kernel, adjoint_spec)
        back_terms = jnp.dot(back_terms, table.T, precision=highest)
        gradient = sum_sens(back_terms) * scale_rows * jax.nn.sigmoid(param)
        square_sum = sum_src_scalar(jnp.sum(gradient * gradient))
        root_mean = jnp.sqrt(square_sum / entry_count + epsilon)
        param = param - step_rate * gradient / root_mean
    own_param = lax.dynamic_slice_in_dim(param, lax.axis_index("sens") * own_sources, own_sources, 0)
    return (own_param, misfit)


def solution(mesh):
    sens, src = mesh.shape["sens"], mesh.shape["src"]
    cores = 2 if src % 2 == 0 else 1
    split = Mesh(mesh.devices.reshape(sens, src // cores, cores), ("sens", "chip", "core"))
    in_specs = (
        P(("chip", "core", "sens"), None),
        P(("chip", "core", "sens")),
        P(None, "sens", ("chip", "core"), None),
        P("sens", None),
    )
    out_specs = (P(("chip", "core", "sens"), None), P(("sens", "chip", "core"), None))
    return jax.shard_map(local, mesh=split, in_specs=in_specs, out_specs=out_specs, check_vma=False)
```

```python
import functools
import math

import jax
import jax.numpy as jnp
import numpy as np
from jax import lax
from jax.experimental import pallas as pl
from jax.experimental.pallas import tpu as pltpu
from jax.sharding import Mesh, PartitionSpec as P

ITERS = 3

highest = lax.Precision.HIGHEST
step_rate = 0.3
epsilon = 1e-06
f32, bf16 = jnp.float32, jnp.bfloat16
LANES = 128
HALF = LANES // 2
NN, NT = ((1,), (0,)), ((1,), (1,))
VM = pl.BlockSpec(memory_space=pltpu.VMEM)
SM = pl.BlockSpec(memory_space=pltpu.SMEM)
ROWS = 16
UNROLL = 24


def table_parts(length):
    padded = 2 * length
    phases = np.outer(np.arange(length), np.arange(length)) % padded * (2.0 * math.pi / padded)
    table = np.concatenate([np.cos(phases), -np.sin(phases)], axis=0).astype(np.float32)
    high = table.astype(jnp.bfloat16)
    return jnp.asarray(np.stack([high, (table - high.astype(np.float32)).astype(jnp.bfloat16)]))


def row_weights(length):
    row = lax.broadcasted_iota(jnp.int32, (length, 1), 0)
    return jnp.where(row == 0, 0.5 / length, 1.0 / length).astype(f32)


def params(mib):
    return pltpu.CompilerParams(vmem_limit_bytes=mib << 20)


def mm(a, b, dims):
    return lax.dot_general(a, b, (dims, ((), ())), preferred_element_type=f32)


def split(x):
    high = x.astype(bf16)
    return high, (x - high.astype(f32)).astype(bf16)


def mm3(a, b, dims):
    return mm(a[0], b[0], dims) + (mm(a[0], b[1], dims) + mm(a[1], b[0], dims))


def relayout_body(k_hbm, out_ref, buf, stage, sem):
    freqs = k_hbm.shape[3]
    steps = k_hbm.shape[1] // ROWS
    same = lax.broadcasted_iota(jnp.int32, (LANES, LANES), 0) == lax.broadcasted_iota(jnp.int32, (LANES, LANES), 1)
    eye = same.astype(f32).astype(bf16)

    def copy(i, slot):
        return pltpu.make_async_copy(k_hbm.at[:, pl.ds(i * ROWS, ROWS)], buf.at[slot], sem.at[slot])

    copy(0, 0).start()

    def step(i, carry):
        slot = lax.rem(i, 2)
        copy(i, slot).wait()

        @pl.when(i + 1 < steps)
        def _():
            copy(i + 1, 1 - slot).start()

        for r in range(0, ROWS, 2):
            x = jnp.concatenate([buf[slot, c, r + j] for j in range(2) for c in range(2)], axis=0)
            for chunk in range(freqs // LANES):
                o = mm(eye, x[:, chunk * LANES:(chunk + 1) * LANES], NT)
                for j in range(2):
                    for h in range(2):
                        rows = pl.ds(chunk * HALF * ROWS + r + j, HALF, stride=ROWS)
                        stage[h, rows, :] = o[h * HALF:(h + 1) * HALF, j * LANES:(j + 1) * LANES]
        rows = pl.ds(pl.multiple_of(i * ROWS, ROWS), ROWS)
        for h in range(2):
            out_ref[:, rows, h * LANES:(h + 1) * LANES] = stage[h].reshape(freqs // 2, ROWS, LANES).astype(bf16)
        return carry

    lax.fori_loop(0, steps, step, 0)


def relayout(kernel):
    _, sensors, sources, freqs = kernel.shape
    return pl.pallas_call(
        relayout_body,
        in_specs=[pl.BlockSpec(memory_space=pl.ANY)],
        out_specs=VM,
        out_shape=pltpu.VMEM((freqs // 2, sensors, 4 * sources), bf16),
        scratch_shapes=[
            pltpu.VMEM((2, 2, ROWS, sources, freqs), bf16),
            pltpu.VMEM((2, freqs // 2 * ROWS, LANES), f32),
            pltpu.SemaphoreType.DMA((2,)),
        ],
        compiler_params=params(10),
        name="relayout",
    )(kernel)


def pair_row(chunk, h, m):
    return pl.ds(chunk * HALF * 8 + 4 * h + m, HALF, stride=8)


def contract(k_ref, lhs, res, dims):
    pairs = k_ref.shape[0]

    def step(i, carry):
        for u in range(UNROLL):
            pair = i * UNROLL + u
            rows = pl.ds(pl.multiple_of(pair * 8, 8), 8)
            a = jnp.concatenate([lhs[0, rows, :], lhs[1, rows, :]], axis=1).astype(bf16)
            o = mm(a, k_ref[pair], dims)
            res[0, rows, :] = o[:, :LANES]
            res[1, rows, :] = o[:, LANES:]
        return carry

    lax.fori_loop(0, pairs // UNROLL, step, 0)


def forward_core(param, k_ref, rig_ref, t_ref, core_ref, keep_ref, send_ref, lhs, res, terms):
    freqs, sources = param.shape[1], param.shape[0]
    slip = rig_ref[...] * jax.nn.softplus(param)
    z = mm3((t_ref[0], t_ref[1]), split(jnp.concatenate([slip, slip], axis=0)), NT)
    low = lax.broadcasted_iota(jnp.int32, (freqs, LANES), 1) < sources
    real, imag = z[:freqs], z[freqs:]
    zero = jnp.zeros((HALF, LANES), f32)
    for m, x in enumerate((jnp.where(low, real, -imag), jnp.where(low, imag, real))):
        high = x.astype(bf16).astype(f32)
        for n, v in enumerate((high, x - high)):
            for chunk in range(freqs // LANES):
                for h in range(2):
                    first = chunk * LANES + h * HALF
                    lhs[h, pair_row(chunk, h, 2 * n + m), :] = v[first:first + HALF]
                    lhs[1 - h, pair_row(chunk, h, 2 * n + m), :] = zero
    contract(k_ref, lhs, res, NT)
    w = row_weights(freqs)
    halves = []
    for m in range(2):
        parts = []
        for chunk in range(freqs // LANES):
            for h in range(2):
                high, rest = pair_row(chunk, h, m), pair_row(chunk, h, 2 + m)
                parts.append(jnp.concatenate([res[c, high, :] + res[c, rest, :] for c in range(2)], axis=1))
        halves.append(jnp.concatenate(parts, axis=0) * w)
    spectrum = jnp.concatenate(halves, axis=0).T
    terms[...] = mm3(split(spectrum), (t_ref[0], t_ref[1]), NN).reshape(terms.shape)
    core = core_ref[0]
    keep_ref[...] = terms[:, core]
    send_ref[...] = terms[:, terms.shape[1] - 1 - core]


def forward_first_body(k_ref, p_ref, rig_ref, t_ref, core_ref, keep_ref, send_ref, lhs, res, terms):
    forward_core(p_ref[...], k_ref, rig_ref, t_ref, core_ref, keep_ref, send_ref, lhs, res, terms)


def moved(param, gradient, sums, entries):
    square_sum = jnp.sum(sums[:, 0:1], axis=0, keepdims=True)
    root_mean = jnp.sqrt(square_sum / entries + epsilon)
    return param - step_rate * gradient / root_mean


def forward_next_body(entries, k_ref, p_ref, g_ref, q_ref, rig_ref, t_ref, core_ref, new_ref, keep_ref, send_ref, lhs, res, terms):
    param = moved(p_ref[...], g_ref[...], q_ref[...], entries)
    new_ref[...] = param
    forward_core(param, k_ref, rig_ref, t_ref, core_ref, keep_ref, send_ref, lhs, res, terms)


def forward(k2, param, update, scale_rows, table, core, grid_shape, entries):
    pairs, sensors, _ = k2.shape
    length = param.shape[1]
    chips, cores = grid_shape
    rows = sensors // (chips * cores)
    outs = [jax.ShapeDtypeStruct((chips, rows, length), f32)] * 2
    scratch = [
        pltpu.VMEM((2, pairs * 8, LANES), f32),
        pltpu.VMEM((2, pairs * 8, LANES), f32),
        pltpu.VMEM((chips, cores, rows, length), f32),
    ]
    if update is None:
        keep, send = pl.pallas_call(
            forward_first_body, in_specs=[VM] * 4 + [SM], out_specs=[VM] * 2, out_shape=outs,
            scratch_shapes=scratch, compiler_params=params(12), name="forward_first",
        )(k2, param, scale_rows, table, core)
        return param, keep, send
    return pl.pallas_call(
        functools.partial(forward_next_body, entries), in_specs=[VM] * 6 + [SM], out_specs=[VM] * 3,
        out_shape=[jax.ShapeDtypeStruct(param.shape, f32)] + outs,
        scratch_shapes=scratch, compiler_params=params(12), name="forward_next",
    )(k2, param, *update, scale_rows, table, core)


def adjoint_body(k_ref, mine_ref, other_ref, t_ref, core_ref, o_ref, lhs, res, full):
    freqs, sources = t_ref.shape[2], k_ref.shape[2] // 4
    core = core_ref[0]
    full[:, core] = mine_ref[...]
    full[:, full.shape[1] - 1 - core] = other_ref[...]
    misfit = full[...].reshape(k_ref.shape[1], freqs)
    spectrum = mm3((t_ref[0], t_ref[1]), split(misfit), NT)
    w = row_weights(freqs)
    for m in range(2):
        x = spectrum[m * freqs:(m + 1) * freqs] * w
        high = x.astype(bf16).astype(f32)
        for n, v in enumerate((high, x - high)):
            for chunk in range(freqs // LANES):
                for h in range(2):
                    first = chunk * LANES + h * HALF
                    for c in range(2):
                        lhs[c, pair_row(chunk, h, 2 * n + m), :] = v[first:first + HALF, c * LANES:(c + 1) * LANES]
    contract(k_ref, lhs, res, NN)
    low = lax.broadcasted_iota(jnp.int32, (HALF, LANES), 1) < sources
    parts = []
    for chunk in range(freqs // LANES):
        for h in range(2):
            real, imag = [res[h, pair_row(chunk, h, m), :] + res[h, pair_row(chunk, h, 2 + m), :] for m in range(2)]
            parts.append(jnp.where(low, real, -real) + pltpu.roll(imag, sources, 1))
    back = jnp.concatenate(parts, axis=0).T
    o_ref[...] = mm3(split(back[:sources]), (t_ref[0, :freqs], t_ref[1, :freqs]), NN) + mm3(
        split(back[sources:]), (t_ref[0, freqs:], t_ref[1, freqs:]), NN
    )


def adjoint(k2, mine, other, table, core):
    pairs, sensors, width = k2.shape
    chips, rows, length = mine.shape
    return pl.pallas_call(
        adjoint_body, in_specs=[VM] * 4 + [SM], out_specs=VM,
        out_shape=jax.ShapeDtypeStruct((width // 4, length), f32),
        scratch_shapes=[
            pltpu.VMEM((2, pairs * 8, LANES), f32),
            pltpu.VMEM((2, pairs * 8, LANES), f32),
            pltpu.VMEM((chips, sensors // (chips * rows), rows, length), f32),
        ],
        compiler_params=params(12), name="adjoint",
    )(k2, mine, other, table, core)


def gradient_body(a_ref, b_ref, p_ref, rig_ref, g_ref, q_ref):
    gradient = (a_ref[...] + b_ref[...]) * rig_ref[...] * jax.nn.sigmoid(p_ref[...])
    g_ref[...] = gradient
    total = jnp.sum(jnp.sum(gradient * gradient, axis=0, keepdims=True), axis=1, keepdims=True)
    q_ref[...] = jnp.broadcast_to(total, q_ref.shape)


def gradient_and_square(own, received, param, scale_rows, peers):
    return pl.pallas_call(
        gradient_body, in_specs=[VM] * 4, out_specs=[VM] * 2,
        out_shape=[jax.ShapeDtypeStruct(param.shape, f32), jax.ShapeDtypeStruct((peers, LANES), f32)],
        compiler_params=params(4), name="gradient",
    )(own, received, param, scale_rows)


def swap(x, axis):
    return lax.ppermute(x, axis, [(0, 1), (1, 0)])


def gather_sens(x):
    if lax.axis_size("sens") == 2:
        first = lax.axis_index("sens") == 0
        other = swap(x, "sens")
        return jnp.concatenate([jnp.where(first, x, other), jnp.where(first, other, x)], axis=0)
    return lax.all_gather(x, "sens", axis=0, tiled=True)


def to_chips(x):
    return lax.all_to_all(x, "chip", 0, 0)


def own_misfit(partial, own_observed):
    return jnp.sum(to_chips(partial), axis=0) - own_observed


def from_chips(misfit):
    return to_chips(jnp.broadcast_to(misfit[None], (lax.axis_size("chip"), *misfit.shape)))


def exchange_scalars(sums):
    return lax.all_to_all(sums, ("chip", "core"), 0, 0, tiled=True)


def plain_forward(kernel, slip):
    length = slip.shape[1]
    table = sum(table_parts(length).astype(f32))
    spectra = lax.dot_general(slip, table, (NT, ((), ())), precision=highest)
    real, imag = spectra[None, :, :length], spectra[None, :, length:]
    k_real, k_imag = kernel[0].astype(f32), kernel[1].astype(f32)
    out_real = jnp.sum(k_real * real - k_imag * imag, axis=1)
    out_imag = jnp.sum(k_real * imag + k_imag * real, axis=1)
    w = jnp.tile(row_weights(length), (2, 1))
    return jnp.dot(jnp.concatenate([out_real, out_imag], axis=1), table * w, precision=highest)


def plain_adjoint(kernel, residual):
    length = residual.shape[1]
    table = sum(table_parts(length).astype(f32))
    w = jnp.tile(row_weights(length), (2, 1))
    spectrum = lax.dot_general(residual, table * w, (NT, ((), ())), precision=highest)
    real, imag = spectrum[:, None, :length], spectrum[:, None, length:]
    k_real, k_imag = kernel[0].astype(f32), kernel[1].astype(f32)
    back_real = jnp.sum(k_real * real + k_imag * imag, axis=0)
    back_imag = jnp.sum(k_real * imag - k_imag * real, axis=0)
    return jnp.dot(jnp.concatenate([back_real, back_imag], axis=1), table, precision=highest)


def plain_iterations(param, scale_rows, kernel, own_observed, entries):
    chips, cores = lax.axis_size("chip"), lax.axis_size("core")
    length = param.shape[1]
    misfit = own_observed
    for _ in range(ITERS):
        terms = plain_forward(kernel, scale_rows * jax.nn.softplus(param)).reshape(chips, cores, -1, length)
        partial = lax.psum_scatter(terms, "core", scatter_dimension=1, tiled=False)
        misfit = own_misfit(partial, own_observed)
        residual = lax.all_gather(from_chips(misfit), "core", axis=1, tiled=False)
        back = plain_adjoint(kernel, residual.reshape(-1, length))
        gradient = lax.psum(back, "sens") * scale_rows * jax.nn.sigmoid(param)
        sums = jnp.broadcast_to(jnp.sum(gradient * gradient), (chips * cores, LANES))
        param = moved(param, gradient, exchange_scalars(sums), entries)
    return param, misfit


def iterations(param, scale_rows, kernel, own_observed, entries):
    chips, cores = lax.axis_size("chip"), lax.axis_size("core")
    core = lax.axis_index("core").reshape(1)
    table = table_parts(param.shape[1])
    k2 = relayout(kernel)
    update = None
    misfit = own_observed
    for _ in range(ITERS):
        param, keep, send = forward(k2, param, update, scale_rows, table, core, (chips, cores), entries)
        misfit = own_misfit(keep + swap(send, "core"), own_observed)
        mine = from_chips(misfit)
        back = adjoint(k2, mine, swap(mine, "core"), table, core)
        gradient, sums = gradient_and_square(back, swap(back, "sens"), param, scale_rows, chips * cores)
        update = gradient, exchange_scalars(sums)
    return moved(param, *update, entries), misfit


def local(slip_param, rigidity, kernel, observed):
    own_sources, length = slip_param.shape
    chips, cores, sens = lax.axis_size("chip"), lax.axis_size("core"), lax.axis_size("sens")
    own_count = kernel.shape[1] // (chips * cores)
    src_index = lax.axis_index("chip") * cores + lax.axis_index("core")
    own_observed = lax.dynamic_slice_in_dim(observed, src_index * own_count, own_count, 0)
    entries = own_sources * sens * chips * cores * length
    packed = gather_sens(jnp.concatenate([slip_param, jnp.broadcast_to(rigidity[:, None], (own_sources, LANES))], axis=1))
    param, scale_rows = packed[:, :length], packed[:, length:length + 1]
    fits = (
        sens == 2 and cores == 2 and kernel.shape[2] == HALF and kernel.shape[1] == 2 * LANES
        and length % LANES == 0 and (length // 2) % UNROLL == 0 and own_count % 8 == 0
    )
    run = iterations if fits else plain_iterations
    param, misfit = run(param, scale_rows, kernel, own_observed, entries)
    own_param = lax.dynamic_slice_in_dim(param, lax.axis_index("sens") * own_sources, own_sources, 0)
    return (own_param, misfit)


def solution(mesh):
    sens, src = mesh.shape["sens"], mesh.shape["src"]
    cores = 2 if src % 2 == 0 else 1
    split_mesh = Mesh(mesh.devices.reshape(sens, src // cores, cores), ("sens", "chip", "core"))
    in_specs = (
        P(("chip", "core", "sens"), None),
        P(("chip", "core", "sens")),
        P(None, "sens", ("chip", "core"), None),
        P("sens", None),
    )
    out_specs = (P(("chip", "core", "sens"), None), P(("sens", "chip", "core"), None))
    return jax.shard_map(local, mesh=split_mesh, in_specs=in_specs, out_specs=out_specs, check_vma=False)
```

```python
import functools
import math

import jax
import jax.numpy as jnp
import numpy as np
from jax import lax
from jax.experimental import pallas as pl
from jax.experimental.pallas import tpu as pltpu
from jax.sharding import Mesh, PartitionSpec as P

ITERS = 3

highest = lax.Precision.HIGHEST
step_rate = 0.3
epsilon = 1e-06
f32, bf16 = jnp.float32, jnp.bfloat16
LANES = 128
HALF = LANES // 2
NN, NT = ((1,), (0,)), ((1,), (1,))
VM = pl.BlockSpec(memory_space=pltpu.VMEM)
ROWS = 16
UNROLL = 24


def table_parts(length):
    padded = 2 * length
    phases = np.outer(np.arange(length), np.arange(length)) % padded * (2.0 * math.pi / padded)
    table = np.concatenate([np.cos(phases), -np.sin(phases)], axis=0).astype(np.float32)
    high = table.astype(jnp.bfloat16)
    return jnp.asarray(np.stack([high, (table - high.astype(np.float32)).astype(jnp.bfloat16)]))


def row_weights(length):
    row = lax.broadcasted_iota(jnp.int32, (length, 1), 0)
    return jnp.where(row == 0, 0.5 / length, 1.0 / length).astype(f32)


def params(mib):
    return pltpu.CompilerParams(vmem_limit_bytes=mib << 20)


def mm(a, b, dims):
    return lax.dot_general(a, b, (dims, ((), ())), preferred_element_type=f32)


def split(x):
    high = x.astype(bf16)
    return high, (x - high.astype(f32)).astype(bf16)


def mm3(a, b, dims):
    return mm(a[0], b[0], dims) + (mm(a[0], b[1], dims) + mm(a[1], b[0], dims))


def relayout_body(k_hbm, out_ref, buf, stage, sem):
    freqs = k_hbm.shape[3]
    steps = k_hbm.shape[1] // ROWS
    same = lax.broadcasted_iota(jnp.int32, (LANES, LANES), 0) == lax.broadcasted_iota(jnp.int32, (LANES, LANES), 1)
    eye = same.astype(f32).astype(bf16)

    def copy(i, slot):
        return pltpu.make_async_copy(k_hbm.at[:, pl.ds(i * ROWS, ROWS)], buf.at[slot], sem.at[slot])

    copy(0, 0).start()

    def step(i, carry):
        slot = lax.rem(i, 2)
        copy(i, slot).wait()

        @pl.when(i + 1 < steps)
        def _():
            copy(i + 1, 1 - slot).start()

        for r in range(0, ROWS, 2):
            x = jnp.concatenate([buf[slot, c, r + j] for j in range(2) for c in range(2)], axis=0)
            for chunk in range(freqs // LANES):
                o = mm(eye, x[:, chunk * LANES:(chunk + 1) * LANES], NT)
                for j in range(2):
                    for h in range(2):
                        rows = pl.ds(chunk * HALF * ROWS + r + j, HALF, stride=ROWS)
                        stage[h, rows, :] = o[h * HALF:(h + 1) * HALF, j * LANES:(j + 1) * LANES]
        rows = pl.ds(pl.multiple_of(i * ROWS, ROWS), ROWS)
        for h in range(2):
            out_ref[:, rows, h * LANES:(h + 1) * LANES] = stage[h].reshape(freqs // 2, ROWS, LANES).astype(bf16)
        return carry

    lax.fori_loop(0, steps, step, 0)


def relayout(kernel):
    _, sensors, sources, freqs = kernel.shape
    return pl.pallas_call(
        relayout_body,
        in_specs=[pl.BlockSpec(memory_space=pl.ANY)],
        out_specs=VM,
        out_shape=pltpu.VMEM((freqs // 2, sensors, 4 * sources), bf16),
        scratch_shapes=[
            pltpu.VMEM((2, 2, ROWS, sources, freqs), bf16),
            pltpu.VMEM((2, freqs // 2 * ROWS, LANES), f32),
            pltpu.SemaphoreType.DMA((2,)),
        ],
        compiler_params=params(10),
        name="relayout",
    )(kernel)


def pair_row(chunk, h, m):
    return pl.ds(chunk * HALF * 8 + 4 * h + m, HALF, stride=8)


def contract(k_ref, lhs, res, dims):
    pairs = k_ref.shape[0]

    def step(i, carry):
        for u in range(UNROLL):
            pair = i * UNROLL + u
            rows = pl.ds(pl.multiple_of(pair * 8, 8), 8)
            a = jnp.concatenate([lhs[0, rows, :], lhs[1, rows, :]], axis=1).astype(bf16)
            o = mm(a, k_ref[pair], dims)
            res[0, rows, :] = o[:, :LANES]
            res[1, rows, :] = o[:, LANES:]
        return carry

    lax.fori_loop(0, pairs // UNROLL, step, 0)


def forward_core(param, scale_rows, k_ref, t_ref, keep_ref, send_ref, lhs, res, terms):
    freqs, sources = param.shape[1], param.shape[0]
    slip = scale_rows * jax.nn.softplus(param)
    z = mm3((t_ref[0], t_ref[1]), split(jnp.concatenate([slip, slip], axis=0)), NT)
    low = lax.broadcasted_iota(jnp.int32, (freqs, LANES), 1) < sources
    real, imag = z[:freqs], z[freqs:]
    zero = jnp.zeros((HALF, LANES), f32)
    for m, x in enumerate((jnp.where(low, real, -imag), jnp.where(low, imag, real))):
        high = x.astype(bf16).astype(f32)
        for n, v in enumerate((high, x - high)):
            for chunk in range(freqs // LANES):
                for h in range(2):
                    first = chunk * LANES + h * HALF
                    lhs[h, pair_row(chunk, h, 2 * n + m), :] = v[first:first + HALF]
                    lhs[1 - h, pair_row(chunk, h, 2 * n + m), :] = zero
    contract(k_ref, lhs, res, NT)
    w = row_weights(freqs)
    halves = []
    for m in range(2):
        parts = []
        for chunk in range(freqs // LANES):
            for h in range(2):
                high, rest = pair_row(chunk, h, m), pair_row(chunk, h, 2 + m)
                parts.append(jnp.concatenate([res[c, high, :] + res[c, rest, :] for c in range(2)], axis=1))
        halves.append(jnp.concatenate(parts, axis=0) * w)
    spectrum = jnp.concatenate(halves, axis=0).T
    terms[...] = mm3(split(spectrum), (t_ref[0], t_ref[1]), NN).reshape(terms.shape)
    core = lax.axis_index("core")
    keep_ref[...] = terms[:, core]
    send_ref[...] = terms[:, terms.shape[1] - 1 - core]


def forward_first_body(k_ref, mine_ref, other_ref, t_ref, new_ref, rig_ref, keep_ref, send_ref, lhs, res, terms, both):
    sens = lax.axis_index("sens")
    both[sens] = mine_ref[...]
    both[1 - sens] = other_ref[...]
    packed = both[...].reshape(-1, both.shape[2])
    length = new_ref.shape[1]
    new_ref[...] = packed[:, :length]
    rig_ref[...] = packed[:, length:]
    forward_core(packed[:, :length], packed[:, length:length + 1], k_ref, t_ref, keep_ref, send_ref, lhs, res, terms)


def moved(param, gradient, sums, entries):
    square_sum = jnp.sum(sums[:, 0:1], axis=0, keepdims=True)
    root_mean = jnp.sqrt(square_sum / entries + epsilon)
    return param - step_rate * gradient / root_mean


def forward_next_body(entries, k_ref, p_ref, g_ref, q_ref, rig_ref, t_ref, new_ref, keep_ref, send_ref, lhs, res, terms):
    param = moved(p_ref[...], g_ref[...], q_ref[...], entries)
    new_ref[...] = param
    forward_core(param, rig_ref[:, 0:1], k_ref, t_ref, keep_ref, send_ref, lhs, res, terms)


def forward_spaces(k2, length, chips, cores):
    pairs, sensors, _ = k2.shape
    rows = sensors // (chips * cores)
    outs = [jax.ShapeDtypeStruct((chips, rows, length), f32)] * 2
    scratch = [
        pltpu.VMEM((2, pairs * 8, LANES), f32),
        pltpu.VMEM((2, pairs * 8, LANES), f32),
        pltpu.VMEM((chips, cores, rows, length), f32),
    ]
    return outs, scratch


def forward_first(k2, mine, other, table, chips, cores):
    sources, length = 2 * mine.shape[0], table.shape[2]
    outs, scratch = forward_spaces(k2, length, chips, cores)
    return pl.pallas_call(
        forward_first_body, in_specs=[VM] * 4, out_specs=[VM] * 4,
        out_shape=[jax.ShapeDtypeStruct((sources, length), f32), jax.ShapeDtypeStruct((sources, LANES), f32)] + outs,
        scratch_shapes=scratch + [pltpu.VMEM((2, *mine.shape), f32)],
        compiler_params=params(12), name="forward_first",
    )(k2, mine, other, table)


def forward_next(k2, param, gradient, sums, scale_rows, table, chips, cores, entries):
    outs, scratch = forward_spaces(k2, param.shape[1], chips, cores)
    return pl.pallas_call(
        functools.partial(forward_next_body, entries), in_specs=[VM] * 6, out_specs=[VM] * 3,
        out_shape=[jax.ShapeDtypeStruct(param.shape, f32)] + outs,
        scratch_shapes=scratch, compiler_params=params(12), name="forward_next",
    )(k2, param, gradient, sums, scale_rows, table)


def misfit_body(parts_ref, obs_ref, m_ref, spread_ref):
    chips, rows, _ = parts_ref.shape
    first = (lax.axis_index("chip") * lax.axis_size("core") + lax.axis_index("core")) * rows
    total = parts_ref[0]
    for c in range(1, chips):
        total = total + parts_ref[c]
    misfit = total - obs_ref[pl.ds(pl.multiple_of(first, 8), rows), :]
    m_ref[...] = misfit
    for c in range(chips):
        spread_ref[c] = misfit


def misfit_and_spread(parts, observed):
    return pl.pallas_call(
        misfit_body, in_specs=[VM] * 2, out_specs=[VM] * 2,
        out_shape=[jax.ShapeDtypeStruct(parts.shape[1:], f32), jax.ShapeDtypeStruct(parts.shape, f32)],
        compiler_params=params(4), name="misfit",
    )(parts, observed)


def finish_body(entries, p_ref, g_ref, q_ref, o_ref):
    rows = o_ref.shape[0]
    own = pl.ds(pl.multiple_of(lax.axis_index("sens") * rows, 8), rows)
    o_ref[...] = moved(p_ref[own, :], g_ref[own, :], q_ref[...], entries)


def finish(param, gradient, sums, entries):
    return pl.pallas_call(
        functools.partial(finish_body, entries), in_specs=[VM] * 3, out_specs=VM,
        out_shape=jax.ShapeDtypeStruct((param.shape[0] // 2, param.shape[1]), f32),
        compiler_params=params(4), name="finish",
    )(param, gradient, sums)


def adjoint_body(k_ref, mine_ref, other_ref, t_ref, o_ref, lhs, res, full):
    freqs, sources = t_ref.shape[2], k_ref.shape[2] // 4
    core = lax.axis_index("core")
    full[:, core] = mine_ref[...]
    full[:, full.shape[1] - 1 - core] = other_ref[...]
    misfit = full[...].reshape(k_ref.shape[1], freqs)
    spectrum = mm3((t_ref[0], t_ref[1]), split(misfit), NT)
    w = row_weights(freqs)
    for m in range(2):
        x = spectrum[m * freqs:(m + 1) * freqs] * w
        high = x.astype(bf16).astype(f32)
        for n, v in enumerate((high, x - high)):
            for chunk in range(freqs // LANES):
                for h in range(2):
                    first = chunk * LANES + h * HALF
                    for c in range(2):
                        lhs[c, pair_row(chunk, h, 2 * n + m), :] = v[first:first + HALF, c * LANES:(c + 1) * LANES]
    contract(k_ref, lhs, res, NN)
    low = lax.broadcasted_iota(jnp.int32, (HALF, LANES), 1) < sources
    parts = []
    for chunk in range(freqs // LANES):
        for h in range(2):
            real, imag = [res[h, pair_row(chunk, h, m), :] + res[h, pair_row(chunk, h, 2 + m), :] for m in range(2)]
            parts.append(jnp.where(low, real, -real) + pltpu.roll(imag, sources, 1))
    back = jnp.concatenate(parts, axis=0).T
    o_ref[...] = mm3(split(back[:sources]), (t_ref[0, :freqs], t_ref[1, :freqs]), NN) + mm3(
        split(back[sources:]), (t_ref[0, freqs:], t_ref[1, freqs:]), NN
    )


def adjoint(k2, mine, other, table):
    pairs, sensors, width = k2.shape
    chips, rows, length = mine.shape
    return pl.pallas_call(
        adjoint_body, in_specs=[VM] * 4, out_specs=VM,
        out_shape=jax.ShapeDtypeStruct((width // 4, length), f32),
        scratch_shapes=[
            pltpu.VMEM((2, pairs * 8, LANES), f32),
            pltpu.VMEM((2, pairs * 8, LANES), f32),
            pltpu.VMEM((chips, sensors // (chips * rows), rows, length), f32),
        ],
        compiler_params=params(12), name="adjoint",
    )(k2, mine, other, table)


def gradient_body(a_ref, b_ref, p_ref, rig_ref, g_ref, q_ref):
    gradient = (a_ref[...] + b_ref[...]) * rig_ref[:, 0:1] * jax.nn.sigmoid(p_ref[...])
    g_ref[...] = gradient
    total = jnp.sum(jnp.sum(gradient * gradient, axis=0, keepdims=True), axis=1, keepdims=True)
    q_ref[...] = jnp.broadcast_to(total, q_ref.shape)


def gradient_and_square(own, received, param, scale_rows, peers):
    return pl.pallas_call(
        gradient_body, in_specs=[VM] * 4, out_specs=[VM] * 2,
        out_shape=[jax.ShapeDtypeStruct(param.shape, f32), jax.ShapeDtypeStruct((peers, LANES), f32)],
        compiler_params=params(4), name="gradient",
    )(own, received, param, scale_rows)


def swap(x, axis):
    return lax.ppermute(x, axis, [(0, 1), (1, 0)])


def to_chips(x):
    return lax.all_to_all(x, "chip", 0, 0)


def exchange_scalars(sums):
    return lax.all_to_all(sums, ("chip", "core"), 0, 0, tiled=True)


def plain_forward(kernel, slip):
    length = slip.shape[1]
    table = sum(table_parts(length).astype(f32))
    spectra = lax.dot_general(slip, table, (NT, ((), ())), precision=highest)
    real, imag = spectra[None, :, :length], spectra[None, :, length:]
    k_real, k_imag = kernel[0].astype(f32), kernel[1].astype(f32)
    out_real = jnp.sum(k_real * real - k_imag * imag, axis=1)
    out_imag = jnp.sum(k_real * imag + k_imag * real, axis=1)
    w = jnp.tile(row_weights(length), (2, 1))
    return jnp.dot(jnp.concatenate([out_real, out_imag], axis=1), table * w, precision=highest)


def plain_adjoint(kernel, residual):
    length = residual.shape[1]
    table = sum(table_parts(length).astype(f32))
    w = jnp.tile(row_weights(length), (2, 1))
    spectrum = lax.dot_general(residual, table * w, (NT, ((), ())), precision=highest)
    real, imag = spectrum[:, None, :length], spectrum[:, None, length:]
    k_real, k_imag = kernel[0].astype(f32), kernel[1].astype(f32)
    back_real = jnp.sum(k_real * real + k_imag * imag, axis=0)
    back_imag = jnp.sum(k_real * imag - k_imag * real, axis=0)
    return jnp.dot(jnp.concatenate([back_real, back_imag], axis=1), table, precision=highest)


def plain_iterations(slip_param, rigidity, kernel, observed, entries):
    chips, cores = lax.axis_size("chip"), lax.axis_size("core")
    own_sources, length = slip_param.shape
    own_count = kernel.shape[1] // (chips * cores)
    src_index = lax.axis_index("chip") * cores + lax.axis_index("core")
    own_observed = lax.dynamic_slice_in_dim(observed, src_index * own_count, own_count, 0)
    param = lax.all_gather(slip_param, "sens", axis=0, tiled=True)
    scale_rows = lax.all_gather(rigidity[:, None], "sens", axis=0, tiled=True)
    misfit = own_observed
    for _ in range(ITERS):
        terms = plain_forward(kernel, scale_rows * jax.nn.softplus(param)).reshape(chips, cores, -1, length)
        partial = lax.psum_scatter(terms, "core", scatter_dimension=1, tiled=False)
        misfit = jnp.sum(to_chips(partial), axis=0) - own_observed
        spread = to_chips(jnp.broadcast_to(misfit[None], (chips, *misfit.shape)))
        residual = lax.all_gather(spread, "core", axis=1, tiled=False)
        back = plain_adjoint(kernel, residual.reshape(-1, length))
        gradient = lax.psum(back, "sens") * scale_rows * jax.nn.sigmoid(param)
        sums = jnp.broadcast_to(jnp.sum(gradient * gradient), (chips * cores, LANES))
        param = moved(param, gradient, exchange_scalars(sums), entries)
    return lax.dynamic_slice_in_dim(param, lax.axis_index("sens") * own_sources, own_sources, 0), misfit


def iterations(slip_param, rigidity, kernel, observed, entries):
    chips, cores = lax.axis_size("chip"), lax.axis_size("core")
    own_sources, length = slip_param.shape
    table = table_parts(length)
    mine = jnp.concatenate([slip_param, jnp.broadcast_to(rigidity[:, None], (own_sources, LANES))], axis=1)
    other = swap(mine, "sens")
    k2 = relayout(kernel)
    param, scale_rows, keep, send = forward_first(k2, mine, other, table, chips, cores)
    for iteration in range(ITERS):
        if iteration:
            param, keep, send = forward_next(k2, param, gradient, sums, scale_rows, table, chips, cores, entries)
        misfit, spread = misfit_and_spread(to_chips(keep + swap(send, "core")), observed)
        near = to_chips(spread)
        back = adjoint(k2, near, swap(near, "core"), table)
        gradient, sums = gradient_and_square(back, swap(back, "sens"), param, scale_rows, chips * cores)
        sums = exchange_scalars(sums)
    return finish(param, gradient, sums, entries), misfit


def local(slip_param, rigidity, kernel, observed):
    own_sources, length = slip_param.shape
    chips, cores, sens = lax.axis_size("chip"), lax.axis_size("core"), lax.axis_size("sens")
    own_count = kernel.shape[1] // (chips * cores)
    entries = own_sources * sens * chips * cores * length
    fits = (
        sens == 2 and cores == 2 and kernel.shape[2] == HALF and kernel.shape[1] == 2 * LANES
        and length % LANES == 0 and (length // 2) % UNROLL == 0 and own_count % 8 == 0
    )
    run = iterations if fits else plain_iterations
    return run(slip_param, rigidity, kernel, observed, entries)


def solution(mesh):
    sens, src = mesh.shape["sens"], mesh.shape["src"]
    cores = 2 if src % 2 == 0 else 1
    split_mesh = Mesh(mesh.devices.reshape(sens, src // cores, cores), ("sens", "chip", "core"))
    in_specs = (
        P(("chip", "core", "sens"), None),
        P(("chip", "core", "sens")),
        P(None, "sens", ("chip", "core"), None),
        P("sens", None),
    )
    out_specs = (P(("chip", "core", "sens"), None), P(("sens", "chip", "core"), None))
    return jax.shard_map(local, mesh=split_mesh, in_specs=in_specs, out_specs=out_specs, check_vma=False)
```

```python
import functools
import math

import jax
import jax.numpy as jnp
import numpy as np
from jax import lax
from jax.experimental import pallas as pl
from jax.experimental.pallas import tpu as pltpu
from jax.sharding import Mesh, PartitionSpec as P

ITERS = 3

highest = lax.Precision.HIGHEST
step_rate = 0.3
epsilon = 1e-06
f32, bf16 = jnp.float32, jnp.bfloat16
LANES = 128
HALF = LANES // 2
NN, NT = ((1,), (0,)), ((1,), (1,))
VM = pl.BlockSpec(memory_space=pltpu.VMEM)
ROWS = 16
PITCH = 24
BUFFERS = 3
UNROLL = 96


def table_parts(length):
    padded = 2 * length
    phases = np.outer(np.arange(length), np.arange(length)) % padded * (2.0 * math.pi / padded)
    table = np.concatenate([np.cos(phases), -np.sin(phases)], axis=0).astype(np.float32)
    high = table.astype(jnp.bfloat16)
    return jnp.asarray(np.stack([high, (table - high.astype(np.float32)).astype(jnp.bfloat16)]))


def row_weights(length):
    row = lax.broadcasted_iota(jnp.int32, (length, 1), 0)
    return jnp.where(row == 0, 0.5 / length, 1.0 / length).astype(f32)


def params(mib):
    return pltpu.CompilerParams(vmem_limit_bytes=mib << 20)


def mm(a, b, dims):
    return lax.dot_general(a, b, (dims, ((), ())), preferred_element_type=f32)


def split(x):
    high = x.astype(bf16)
    return high, (x - high.astype(f32)).astype(bf16)


def mm3(a, b, dims):
    return mm(a[0], b[0], dims) + (mm(a[0], b[1], dims) + mm(a[1], b[0], dims))


def relayout_body(k_hbm, out_ref, buf, stage, sem):
    freqs = k_hbm.shape[3]
    steps = k_hbm.shape[1] // ROWS

    def copy(i):
        slot = lax.rem(i, BUFFERS)
        return pltpu.make_async_copy(k_hbm.at[:, pl.ds(i * ROWS, ROWS)], buf.at[slot], sem.at[slot])

    for i in range(BUFFERS - 1):
        copy(i).start()

    def step(i, carry):
        slot = lax.rem(i, BUFFERS)
        copy(i).wait()

        @pl.when(i + BUFFERS - 1 < steps)
        def _():
            copy(i + BUFFERS - 1).start()

        for r in range(0, ROWS, 2):
            x = jnp.concatenate([buf[slot, c, r + j] for j in range(2) for c in range(2)], axis=0)
            for chunk in range(freqs // LANES):
                o = x[:, chunk * LANES:(chunk + 1) * LANES].T.astype(f32)
                for j in range(2):
                    for h in range(2):
                        rows = pl.ds(chunk * HALF * PITCH + r + j, HALF, stride=PITCH)
                        stage[h, rows, :] = o[h * HALF:(h + 1) * HALF, j * LANES:(j + 1) * LANES]
        rows = pl.ds(pl.multiple_of(i * ROWS, ROWS), ROWS)
        for h in range(2):
            block = stage[h].reshape(freqs // 2, PITCH, LANES)[:, :ROWS]
            out_ref[:, rows, h * LANES:(h + 1) * LANES] = block.astype(bf16)
        return carry

    lax.fori_loop(0, steps, step, 0)


def relayout(kernel):
    _, sensors, sources, freqs = kernel.shape
    return pl.pallas_call(
        relayout_body,
        in_specs=[pl.BlockSpec(memory_space=pl.ANY)],
        out_specs=VM,
        out_shape=pltpu.VMEM((freqs // 2, sensors, 4 * sources), bf16),
        scratch_shapes=[
            pltpu.VMEM((BUFFERS, 2, ROWS, sources, freqs), bf16),
            pltpu.VMEM((2, freqs // 2 * PITCH, LANES), f32),
            pltpu.SemaphoreType.DMA((BUFFERS,)),
        ],
        compiler_params=params(12),
        name="relayout",
    )(kernel)


def pack_body(p_ref, rig_ref, o_ref):
    rows, length = p_ref.shape
    o_ref[:, :length] = p_ref[...]
    same = lax.broadcasted_iota(jnp.int32, (rows, rows), 0) == lax.broadcasted_iota(jnp.int32, (rows, rows), 1)
    column = jnp.sum(jnp.where(same, jnp.broadcast_to(rig_ref[...], (rows, rows)), 0.0), axis=1, keepdims=True)
    o_ref[:, length:] = jnp.broadcast_to(column, (rows, LANES))


def pack(slip_param, rigidity):
    rows, length = slip_param.shape
    return pl.pallas_call(
        pack_body, in_specs=[VM] * 2, out_specs=VM,
        out_shape=jax.ShapeDtypeStruct((rows, length + LANES), f32),
        compiler_params=params(4), name="pack",
    )(slip_param, rigidity.reshape(1, rows))


def pair_row(chunk, h, m):
    return pl.ds(chunk * HALF * 8 + 4 * h + m, HALF, stride=8)


def contract(k_ref, lhs, res, dims):
    pairs = k_ref.shape[0]

    def step(i, carry):
        for u in range(UNROLL):
            pair = i * UNROLL + u
            rows = pl.ds(pl.multiple_of(pair * 8, 8), 8)
            a = jnp.concatenate([lhs[0, rows, :], lhs[1, rows, :]], axis=1).astype(bf16)
            o = mm(a, k_ref[pair], dims)
            res[0, rows, :] = o[:, :LANES]
            res[1, rows, :] = o[:, LANES:]
        return carry

    lax.fori_loop(0, pairs // UNROLL, step, 0)


def forward_core(param, scale_rows, k_ref, t_ref, keep_ref, send_ref, lhs, res, terms):
    freqs, sources = param.shape[1], param.shape[0]
    slip = scale_rows * jax.nn.softplus(param)
    z = mm3((t_ref[0], t_ref[1]), split(jnp.concatenate([slip, slip], axis=0)), NT)
    low = lax.broadcasted_iota(jnp.int32, (freqs, LANES), 1) < sources
    real, imag = z[:freqs], z[freqs:]
    zero = jnp.zeros((HALF, LANES), f32)
    for m, x in enumerate((jnp.where(low, real, -imag), jnp.where(low, imag, real))):
        high = x.astype(bf16).astype(f32)
        for n, v in enumerate((high, x - high)):
            for chunk in range(freqs // LANES):
                for h in range(2):
                    first = chunk * LANES + h * HALF
                    lhs[h, pair_row(chunk, h, 2 * n + m), :] = v[first:first + HALF]
                    lhs[1 - h, pair_row(chunk, h, 2 * n + m), :] = zero
    contract(k_ref, lhs, res, NT)
    w = row_weights(freqs)
    halves = []
    for m in range(2):
        parts = []
        for chunk in range(freqs // LANES):
            for h in range(2):
                high, rest = pair_row(chunk, h, m), pair_row(chunk, h, 2 + m)
                parts.append(jnp.concatenate([res[c, high, :] + res[c, rest, :] for c in range(2)], axis=1))
        halves.append(jnp.concatenate(parts, axis=0) * w)
    spectrum = jnp.concatenate(halves, axis=0).T
    terms[...] = mm3(split(spectrum), (t_ref[0], t_ref[1]), NN).reshape(terms.shape)
    core = lax.axis_index("core")
    keep_ref[...] = terms[:, core]
    send_ref[...] = terms[:, terms.shape[1] - 1 - core]


def forward_first_body(k_ref, mine_ref, other_ref, t_ref, new_ref, rig_ref, keep_ref, send_ref, lhs, res, terms, both):
    sens = lax.axis_index("sens")
    both[sens] = mine_ref[...]
    both[1 - sens] = other_ref[...]
    packed = both[...].reshape(-1, both.shape[2])
    length = new_ref.shape[1]
    new_ref[...] = packed[:, :length]
    rig_ref[...] = packed[:, length:]
    forward_core(packed[:, :length], packed[:, length:length + 1], k_ref, t_ref, keep_ref, send_ref, lhs, res, terms)


def moved(param, gradient, sums, entries):
    square_sum = jnp.sum(sums[:, 0:1], axis=0, keepdims=True)
    root_mean = jnp.sqrt(square_sum / entries + epsilon)
    return param - step_rate * gradient / root_mean


def forward_next_body(entries, k_ref, p_ref, g_ref, q_ref, rig_ref, t_ref, new_ref, keep_ref, send_ref, lhs, res, terms):
    param = moved(p_ref[...], g_ref[...], q_ref[...], entries)
    new_ref[...] = param
    forward_core(param, rig_ref[:, 0:1], k_ref, t_ref, keep_ref, send_ref, lhs, res, terms)


def forward_spaces(k2, length, chips, cores):
    pairs, sensors, _ = k2.shape
    rows = sensors // (chips * cores)
    outs = [jax.ShapeDtypeStruct((chips, rows, length), f32)] * 2
    scratch = [
        pltpu.VMEM((2, pairs * 8, LANES), f32),
        pltpu.VMEM((2, pairs * 8, LANES), f32),
        pltpu.VMEM((chips, cores, rows, length), f32),
    ]
    return outs, scratch


def forward_first(k2, mine, other, table, chips, cores):
    sources, length = 2 * mine.shape[0], table.shape[2]
    outs, scratch = forward_spaces(k2, length, chips, cores)
    return pl.pallas_call(
        forward_first_body, in_specs=[VM] * 4, out_specs=[VM] * 4,
        out_shape=[jax.ShapeDtypeStruct((sources, length), f32), jax.ShapeDtypeStruct((sources, LANES), f32)] + outs,
        scratch_shapes=scratch + [pltpu.VMEM((2, *mine.shape), f32)],
        compiler_params=params(12), name="forward_first",
    )(k2, mine, other, table)


def forward_next(k2, param, gradient, sums, scale_rows, table, chips, cores, entries):
    outs, scratch = forward_spaces(k2, param.shape[1], chips, cores)
    return pl.pallas_call(
        functools.partial(forward_next_body, entries), in_specs=[VM] * 6, out_specs=[VM] * 3,
        out_shape=[jax.ShapeDtypeStruct(param.shape, f32)] + outs,
        scratch_shapes=scratch, compiler_params=params(12), name="forward_next",
    )(k2, param, gradient, sums, scale_rows, table)


def misfit_body(parts_ref, obs_ref, m_ref, spread_ref):
    chips, rows, _ = parts_ref.shape
    first = (lax.axis_index("chip") * lax.axis_size("core") + lax.axis_index("core")) * rows
    total = parts_ref[0]
    for c in range(1, chips):
        total = total + parts_ref[c]
    misfit = total - obs_ref[pl.ds(pl.multiple_of(first, 8), rows), :]
    m_ref[...] = misfit
    for c in range(chips):
        spread_ref[c] = misfit


def misfit_and_spread(parts, observed):
    return pl.pallas_call(
        misfit_body, in_specs=[VM] * 2, out_specs=[VM] * 2,
        out_shape=[jax.ShapeDtypeStruct(parts.shape[1:], f32), jax.ShapeDtypeStruct(parts.shape, f32)],
        compiler_params=params(4), name="misfit",
    )(parts, observed)


def finish_body(entries, p_ref, g_ref, q_ref, o_ref):
    rows = o_ref.shape[0]
    own = pl.ds(pl.multiple_of(lax.axis_index("sens") * rows, 8), rows)
    o_ref[...] = moved(p_ref[own, :], g_ref[own, :], q_ref[...], entries)


def finish(param, gradient, sums, entries):
    return pl.pallas_call(
        functools.partial(finish_body, entries), in_specs=[VM] * 3, out_specs=VM,
        out_shape=jax.ShapeDtypeStruct((param.shape[0] // 2, param.shape[1]), f32),
        compiler_params=params(4), name="finish",
    )(param, gradient, sums)


def adjoint_body(k_ref, mine_ref, other_ref, t_ref, o_ref, lhs, res, full):
    freqs, sources = t_ref.shape[2], k_ref.shape[2] // 4
    core = lax.axis_index("core")
    full[:, core] = mine_ref[...]
    full[:, full.shape[1] - 1 - core] = other_ref[...]
    misfit = full[...].reshape(k_ref.shape[1], freqs)
    spectrum = mm3((t_ref[0], t_ref[1]), split(misfit), NT)
    w = row_weights(freqs)
    for m in range(2):
        x = spectrum[m * freqs:(m + 1) * freqs] * w
        high = x.astype(bf16).astype(f32)
        for n, v in enumerate((high, x - high)):
            for chunk in range(freqs // LANES):
                for h in range(2):
                    first = chunk * LANES + h * HALF
                    for c in range(2):
                        lhs[c, pair_row(chunk, h, 2 * n + m), :] = v[first:first + HALF, c * LANES:(c + 1) * LANES]
    contract(k_ref, lhs, res, NN)
    low = lax.broadcasted_iota(jnp.int32, (HALF, LANES), 1) < sources
    parts = []
    for chunk in range(freqs // LANES):
        for h in range(2):
            real, imag = [res[h, pair_row(chunk, h, m), :] + res[h, pair_row(chunk, h, 2 + m), :] for m in range(2)]
            parts.append(jnp.where(low, real, -real) + pltpu.roll(imag, sources, 1))
    back = jnp.concatenate(parts, axis=0).T
    o_ref[...] = mm3(split(back[:sources]), (t_ref[0, :freqs], t_ref[1, :freqs]), NN) + mm3(
        split(back[sources:]), (t_ref[0, freqs:], t_ref[1, freqs:]), NN
    )


def adjoint(k2, mine, other, table):
    pairs, sensors, width = k2.shape
    chips, rows, length = mine.shape
    return pl.pallas_call(
        adjoint_body, in_specs=[VM] * 4, out_specs=VM,
        out_shape=jax.ShapeDtypeStruct((width // 4, length), f32),
        scratch_shapes=[
            pltpu.VMEM((2, pairs * 8, LANES), f32),
            pltpu.VMEM((2, pairs * 8, LANES), f32),
            pltpu.VMEM((chips, sensors // (chips * rows), rows, length), f32),
        ],
        compiler_params=params(12), name="adjoint",
    )(k2, mine, other, table)


def gradient_body(a_ref, b_ref, p_ref, rig_ref, g_ref, q_ref):
    gradient = (a_ref[...] + b_ref[...]) * rig_ref[:, 0:1] * jax.nn.sigmoid(p_ref[...])
    g_ref[...] = gradient
    total = jnp.sum(jnp.sum(gradient * gradient, axis=0, keepdims=True), axis=1, keepdims=True)
    q_ref[...] = jnp.broadcast_to(total, q_ref.shape)


def gradient_and_square(own, received, param, scale_rows, peers):
    return pl.pallas_call(
        gradient_body, in_specs=[VM] * 4, out_specs=[VM] * 2,
        out_shape=[jax.ShapeDtypeStruct(param.shape, f32), jax.ShapeDtypeStruct((peers, LANES), f32)],
        compiler_params=params(4), name="gradient",
    )(own, received, param, scale_rows)


def swap(x, axis):
    return lax.ppermute(x, axis, [(0, 1), (1, 0)])


def to_chips(x):
    return lax.all_to_all(x, "chip", 0, 0)


def exchange_scalars(sums):
    return lax.all_to_all(sums, ("chip", "core"), 0, 0, tiled=True)


def plain_forward(kernel, slip):
    length = slip.shape[1]
    table = sum(table_parts(length).astype(f32))
    spectra = lax.dot_general(slip, table, (NT, ((), ())), precision=highest)
    real, imag = spectra[None, :, :length], spectra[None, :, length:]
    k_real, k_imag = kernel[0].astype(f32), kernel[1].astype(f32)
    out_real = jnp.sum(k_real * real - k_imag * imag, axis=1)
    out_imag = jnp.sum(k_real * imag + k_imag * real, axis=1)
    w = jnp.tile(row_weights(length), (2, 1))
    return jnp.dot(jnp.concatenate([out_real, out_imag], axis=1), table * w, precision=highest)


def plain_adjoint(kernel, residual):
    length = residual.shape[1]
    table = sum(table_parts(length).astype(f32))
    w = jnp.tile(row_weights(length), (2, 1))
    spectrum = lax.dot_general(residual, table * w, (NT, ((), ())), precision=highest)
    real, imag = spectrum[:, None, :length], spectrum[:, None, length:]
    k_real, k_imag = kernel[0].astype(f32), kernel[1].astype(f32)
    back_real = jnp.sum(k_real * real + k_imag * imag, axis=0)
    back_imag = jnp.sum(k_real * imag - k_imag * real, axis=0)
    return jnp.dot(jnp.concatenate([back_real, back_imag], axis=1), table, precision=highest)


def plain_iterations(slip_param, rigidity, kernel, observed, entries):
    chips, cores = lax.axis_size("chip"), lax.axis_size("core")
    own_sources, length = slip_param.shape
    own_count = kernel.shape[1] // (chips * cores)
    src_index = lax.axis_index("chip") * cores + lax.axis_index("core")
    own_observed = lax.dynamic_slice_in_dim(observed, src_index * own_count, own_count, 0)
    param = lax.all_gather(slip_param, "sens", axis=0, tiled=True)
    scale_rows = lax.all_gather(rigidity[:, None], "sens", axis=0, tiled=True)
    misfit = own_observed
    for _ in range(ITERS):
        terms = plain_forward(kernel, scale_rows * jax.nn.softplus(param)).reshape(chips, cores, -1, length)
        partial = lax.psum_scatter(terms, "core", scatter_dimension=1, tiled=False)
        misfit = jnp.sum(to_chips(partial), axis=0) - own_observed
        spread = to_chips(jnp.broadcast_to(misfit[None], (chips, *misfit.shape)))
        residual = lax.all_gather(spread, "core", axis=1, tiled=False)
        back = plain_adjoint(kernel, residual.reshape(-1, length))
        gradient = lax.psum(back, "sens") * scale_rows * jax.nn.sigmoid(param)
        sums = jnp.broadcast_to(jnp.sum(gradient * gradient), (chips * cores, LANES))
        param = moved(param, gradient, exchange_scalars(sums), entries)
    return lax.dynamic_slice_in_dim(param, lax.axis_index("sens") * own_sources, own_sources, 0), misfit


def iterations(slip_param, rigidity, kernel, observed, entries):
    chips, cores = lax.axis_size("chip"), lax.axis_size("core")
    table = table_parts(slip_param.shape[1])
    mine = pack(slip_param, rigidity)
    other = swap(mine, "sens")
    k2 = relayout(kernel)
    param, scale_rows, keep, send = forward_first(k2, mine, other, table, chips, cores)
    for iteration in range(ITERS):
        if iteration:
            param, keep, send = forward_next(k2, param, gradient, sums, scale_rows, table, chips, cores, entries)
        misfit, spread = misfit_and_spread(to_chips(keep + swap(send, "core")), observed)
        near = to_chips(spread)
        back = adjoint(k2, near, swap(near, "core"), table)
        gradient, sums = gradient_and_square(back, swap(back, "sens"), param, scale_rows, chips * cores)
        sums = exchange_scalars(sums)
    return finish(param, gradient, sums, entries), misfit


def local(slip_param, rigidity, kernel, observed):
    own_sources, length = slip_param.shape
    chips, cores, sens = lax.axis_size("chip"), lax.axis_size("core"), lax.axis_size("sens")
    own_count = kernel.shape[1] // (chips * cores)
    entries = own_sources * sens * chips * cores * length
    fits = (
        sens == 2 and cores == 2 and kernel.shape[2] == HALF and kernel.shape[1] == 2 * LANES
        and length % LANES == 0 and (length // 2) % UNROLL == 0 and own_count % 8 == 0
    )
    run = iterations if fits else plain_iterations
    return run(slip_param, rigidity, kernel, observed, entries)


def solution(mesh):
    sens, src = mesh.shape["sens"], mesh.shape["src"]
    cores = 2 if src % 2 == 0 else 1
    split_mesh = Mesh(mesh.devices.reshape(sens, src // cores, cores), ("sens", "chip", "core"))
    in_specs = (
        P(("chip", "core", "sens"), None),
        P(("chip", "core", "sens")),
        P(None, "sens", ("chip", "core"), None),
        P("sens", None),
    )
    out_specs = (P(("chip", "core", "sens"), None), P(("sens", "chip", "core"), None))
    return jax.shard_map(local, mesh=split_mesh, in_specs=in_specs, out_specs=out_specs, check_vma=False)
```

```python
import functools
import math

import jax
import jax.numpy as jnp
import numpy as np
from jax import lax
from jax.experimental import pallas as pl
from jax.experimental.pallas import tpu as pltpu
from jax.sharding import Mesh, PartitionSpec as P

ITERS = 3

highest = lax.Precision.HIGHEST
step_rate = 0.3
epsilon = 1e-06
f32, bf16 = jnp.float32, jnp.bfloat16
LANES = 128
HALF = LANES // 2
NN, NT = ((1,), (0,)), ((1,), (1,))
VM = pl.BlockSpec(memory_space=pltpu.VMEM)
ROWS = 16
PITCH = 196
BUFFERS = 6
UNROLL = 96


def table_parts(length):
    padded = 2 * length
    phases = np.outer(np.arange(length), np.arange(length)) % padded * (2.0 * math.pi / padded)
    table = np.concatenate([np.cos(phases), -np.sin(phases)], axis=0).astype(np.float32)
    high = table.astype(jnp.bfloat16)
    return jnp.asarray(np.stack([high, (table - high.astype(np.float32)).astype(jnp.bfloat16)]))


def row_weights(length):
    row = lax.broadcasted_iota(jnp.int32, (length, 1), 0)
    return jnp.where(row == 0, 0.5 / length, 1.0 / length).astype(f32)


def params(mib):
    return pltpu.CompilerParams(vmem_limit_bytes=mib << 20)


def mm(a, b, dims):
    return lax.dot_general(a, b, (dims, ((), ())), preferred_element_type=f32)


def split(x):
    high = x.astype(bf16)
    return high, (x - high.astype(f32)).astype(bf16)


def mm3(a, b, dims):
    return mm(a[0], b[0], dims) + (mm(a[0], b[1], dims) + mm(a[1], b[0], dims))


def relayout_body(k_hbm, out_ref, buf, stage, sem):
    freqs = k_hbm.shape[3]
    pairs = freqs // 2
    steps = k_hbm.shape[1] // ROWS
    same = lax.broadcasted_iota(jnp.int32, (LANES, LANES), 0) == lax.broadcasted_iota(jnp.int32, (LANES, LANES), 1)
    eye = same.astype(f32).astype(bf16)

    def copies(i):
        slot = lax.rem(i, BUFFERS)
        rows = pl.ds(i * ROWS, ROWS)
        return [pltpu.make_async_copy(k_hbm.at[c, rows], buf.at[slot, c], sem.at[slot, c]) for c in range(2)]

    def start(i):
        for copy in copies(i):
            copy.start()

    for i in range(BUFFERS - 1):
        start(i)

    def step(i, carry):
        slot = lax.rem(i, BUFFERS)
        for copy in copies(i):
            copy.wait()

        @pl.when(i + BUFFERS - 1 < steps)
        def _():
            start(i + BUFFERS - 1)

        for r in range(0, ROWS, 2):
            x = jnp.concatenate([buf[slot, c, r + j] for j in range(2) for c in range(2)], axis=0)
            for chunk in range(freqs // LANES):
                part = x[:, chunk * LANES:(chunk + 1) * LANES]
                o = mm(eye, part, NT) if r % 4 == 0 else part.T.astype(f32)
                for j in range(2):
                    for h in range(2):
                        rows = pl.ds((r + j) * PITCH + chunk * HALF, HALF)
                        stage[h, rows, :] = o[h * HALF:(h + 1) * HALF, j * LANES:(j + 1) * LANES]
        rows = pl.ds(pl.multiple_of(i * ROWS, ROWS), ROWS)
        for h in range(2):
            for pair in range(pairs):
                out_ref[h, pair, rows, :] = stage[h, pl.ds(pair, ROWS, stride=PITCH), :].astype(bf16)
        return carry

    lax.fori_loop(0, steps, step, 0)


def relayout(kernel):
    _, sensors, sources, freqs = kernel.shape
    return pl.pallas_call(
        relayout_body,
        in_specs=[pl.BlockSpec(memory_space=pl.ANY)],
        out_specs=VM,
        out_shape=pltpu.VMEM((2, freqs // 2, sensors, 2 * sources), bf16),
        scratch_shapes=[
            pltpu.VMEM((BUFFERS, 2, ROWS, sources, freqs), bf16),
            pltpu.VMEM((2, ROWS * PITCH, LANES), f32),
            pltpu.SemaphoreType.DMA((BUFFERS, 2)),
        ],
        compiler_params=params(16),
        name="relayout",
    )(kernel)


def pack_body(p_ref, rig_ref, o_ref):
    rows, length = p_ref.shape
    o_ref[:, :length] = p_ref[...]
    same = lax.broadcasted_iota(jnp.int32, (rows, rows), 0) == lax.broadcasted_iota(jnp.int32, (rows, rows), 1)
    column = jnp.sum(jnp.where(same, jnp.broadcast_to(rig_ref[...], (rows, rows)), 0.0), axis=1, keepdims=True)
    o_ref[:, length:] = jnp.broadcast_to(column, (rows, LANES))


def pack(slip_param, rigidity):
    rows, length = slip_param.shape
    return pl.pallas_call(
        pack_body, in_specs=[VM] * 2, out_specs=VM,
        out_shape=jax.ShapeDtypeStruct((rows, length + LANES), f32),
        compiler_params=params(4), name="pack",
    )(slip_param, rigidity.reshape(1, rows))


def pair_row(chunk, h, m):
    return pl.ds(chunk * HALF * 8 + 4 * h + m, HALF, stride=8)


def contract(k_ref, lhs, res, dims):
    pairs = k_ref.shape[1]

    def tile(pair):
        return jnp.concatenate([k_ref[0, pair], k_ref[1, pair]], axis=1)

    def turned(pair):
        blocks = [[k_ref[h, pair, c * LANES:(c + 1) * LANES, :].T for c in range(2)] for h in range(2)]
        return jnp.concatenate([jnp.concatenate(row, axis=1) for row in blocks], axis=0)

    def step(i, carry):
        for u in range(UNROLL):
            pair = i * UNROLL + u
            rows = pl.ds(pl.multiple_of(pair * 8, 8), 8)
            a = jnp.concatenate([lhs[0, rows, :], lhs[1, rows, :]], axis=1).astype(bf16)
            o = mm(a, turned(pair), NN) if dims == NT and u % 3 else mm(a, tile(pair), dims)
            res[0, rows, :] = o[:, :LANES]
            res[1, rows, :] = o[:, LANES:]
        return carry

    lax.fori_loop(0, pairs // UNROLL, step, 0)


def forward_core(param, scale_rows, k_ref, t_ref, keep_ref, send_ref, lhs, res, terms):
    freqs, sources = param.shape[1], param.shape[0]
    slip = scale_rows * jax.nn.softplus(param)
    z = mm3((t_ref[0], t_ref[1]), split(jnp.concatenate([slip, slip], axis=0)), NT)
    low = lax.broadcasted_iota(jnp.int32, (freqs, LANES), 1) < sources
    real, imag = z[:freqs], z[freqs:]
    zero = jnp.zeros((HALF, LANES), f32)
    for m, x in enumerate((jnp.where(low, real, -imag), jnp.where(low, imag, real))):
        high = x.astype(bf16).astype(f32)
        for n, v in enumerate((high, x - high)):
            for chunk in range(freqs // LANES):
                for h in range(2):
                    first = chunk * LANES + h * HALF
                    lhs[h, pair_row(chunk, h, 2 * n + m), :] = v[first:first + HALF]
                    lhs[1 - h, pair_row(chunk, h, 2 * n + m), :] = zero
    contract(k_ref, lhs, res, NT)
    w = row_weights(freqs)
    halves = []
    for m in range(2):
        parts = []
        for chunk in range(freqs // LANES):
            for h in range(2):
                high, rest = pair_row(chunk, h, m), pair_row(chunk, h, 2 + m)
                parts.append(jnp.concatenate([res[c, high, :] + res[c, rest, :] for c in range(2)], axis=1))
        halves.append(jnp.concatenate(parts, axis=0) * w)
    spectrum = jnp.concatenate(halves, axis=0).T
    terms[...] = mm3(split(spectrum), (t_ref[0], t_ref[1]), NN).reshape(terms.shape)
    core = lax.axis_index("core")
    keep_ref[...] = terms[:, core]
    send_ref[...] = terms[:, terms.shape[1] - 1 - core]


def forward_first_body(k_ref, mine_ref, other_ref, t_ref, new_ref, rig_ref, keep_ref, send_ref, lhs, res, terms, both):
    sens = lax.axis_index("sens")
    both[sens] = mine_ref[...]
    both[1 - sens] = other_ref[...]
    packed = both[...].reshape(-1, both.shape[2])
    length = new_ref.shape[1]
    new_ref[...] = packed[:, :length]
    rig_ref[...] = packed[:, length:]
    forward_core(packed[:, :length], packed[:, length:length + 1], k_ref, t_ref, keep_ref, send_ref, lhs, res, terms)


def moved(param, gradient, sums, entries):
    square_sum = jnp.sum(sums[:, 0:1], axis=0, keepdims=True)
    root_mean = jnp.sqrt(square_sum / entries + epsilon)
    return param - step_rate * gradient / root_mean


def forward_next_body(entries, k_ref, p_ref, g_ref, q_ref, rig_ref, t_ref, new_ref, keep_ref, send_ref, lhs, res, terms):
    param = moved(p_ref[...], g_ref[...], q_ref[...], entries)
    new_ref[...] = param
    forward_core(param, rig_ref[:, 0:1], k_ref, t_ref, keep_ref, send_ref, lhs, res, terms)


def forward_spaces(k2, length, chips, cores):
    _, pairs, sensors, _ = k2.shape
    rows = sensors // (chips * cores)
    outs = [jax.ShapeDtypeStruct((chips, rows, length), f32)] * 2
    scratch = [
        pltpu.VMEM((2, pairs * 8, LANES), f32),
        pltpu.VMEM((2, pairs * 8, LANES), f32),
        pltpu.VMEM((chips, cores, rows, length), f32),
    ]
    return outs, scratch


def forward_first(k2, mine, other, table, chips, cores):
    sources, length = 2 * mine.shape[0], table.shape[2]
    outs, scratch = forward_spaces(k2, length, chips, cores)
    return pl.pallas_call(
        forward_first_body, in_specs=[VM] * 4, out_specs=[VM] * 4,
        out_shape=[jax.ShapeDtypeStruct((sources, length), f32), jax.ShapeDtypeStruct((sources, LANES), f32)] + outs,
        scratch_shapes=scratch + [pltpu.VMEM((2, *mine.shape), f32)],
        compiler_params=params(12), name="forward_first",
    )(k2, mine, other, table)


def forward_next(k2, param, gradient, sums, scale_rows, table, chips, cores, entries):
    outs, scratch = forward_spaces(k2, param.shape[1], chips, cores)
    return pl.pallas_call(
        functools.partial(forward_next_body, entries), in_specs=[VM] * 6, out_specs=[VM] * 3,
        out_shape=[jax.ShapeDtypeStruct(param.shape, f32)] + outs,
        scratch_shapes=scratch, compiler_params=params(12), name="forward_next",
    )(k2, param, gradient, sums, scale_rows, table)


def misfit_body(parts_ref, obs_ref, m_ref, spread_ref):
    chips, rows, _ = parts_ref.shape
    first = (lax.axis_index("chip") * lax.axis_size("core") + lax.axis_index("core")) * rows
    total = parts_ref[0]
    for c in range(1, chips):
        total = total + parts_ref[c]
    misfit = total - obs_ref[pl.ds(pl.multiple_of(first, 8), rows), :]
    m_ref[...] = misfit
    for c in range(chips):
        spread_ref[c] = misfit


def misfit_and_spread(parts, observed):
    return pl.pallas_call(
        misfit_body, in_specs=[VM] * 2, out_specs=[VM] * 2,
        out_shape=[jax.ShapeDtypeStruct(parts.shape[1:], f32), jax.ShapeDtypeStruct(parts.shape, f32)],
        compiler_params=params(4), name="misfit",
    )(parts, observed)


def finish_body(entries, p_ref, g_ref, q_ref, o_ref):
    rows = o_ref.shape[0]
    own = pl.ds(pl.multiple_of(lax.axis_index("sens") * rows, 8), rows)
    o_ref[...] = moved(p_ref[own, :], g_ref[own, :], q_ref[...], entries)


def finish(param, gradient, sums, entries):
    return pl.pallas_call(
        functools.partial(finish_body, entries), in_specs=[VM] * 3, out_specs=VM,
        out_shape=jax.ShapeDtypeStruct((param.shape[0] // 2, param.shape[1]), f32),
        compiler_params=params(4), name="finish",
    )(param, gradient, sums)


def adjoint_body(k_ref, mine_ref, other_ref, t_ref, o_ref, lhs, res, full):
    freqs, sources = t_ref.shape[2], k_ref.shape[3] // 2
    core = lax.axis_index("core")
    full[:, core] = mine_ref[...]
    full[:, full.shape[1] - 1 - core] = other_ref[...]
    misfit = full[...].reshape(k_ref.shape[2], freqs)
    spectrum = mm3((t_ref[0], t_ref[1]), split(misfit), NT)
    w = row_weights(freqs)
    for m in range(2):
        x = spectrum[m * freqs:(m + 1) * freqs] * w
        high = x.astype(bf16).astype(f32)
        for n, v in enumerate((high, x - high)):
            for chunk in range(freqs // LANES):
                for h in range(2):
                    first = chunk * LANES + h * HALF
                    for c in range(2):
                        lhs[c, pair_row(chunk, h, 2 * n + m), :] = v[first:first + HALF, c * LANES:(c + 1) * LANES]
    contract(k_ref, lhs, res, NN)
    low = lax.broadcasted_iota(jnp.int32, (HALF, LANES), 1) < sources
    parts = []
    for chunk in range(freqs // LANES):
        for h in range(2):
            real, imag = [res[h, pair_row(chunk, h, m), :] + res[h, pair_row(chunk, h, 2 + m), :] for m in range(2)]
            parts.append(jnp.where(low, real, -real) + pltpu.roll(imag, sources, 1))
    back = jnp.concatenate(parts, axis=0).T
    o_ref[...] = mm3(split(back[:sources]), (t_ref[0, :freqs], t_ref[1, :freqs]), NN) + mm3(
        split(back[sources:]), (t_ref[0, freqs:], t_ref[1, freqs:]), NN
    )


def adjoint(k2, mine, other, table):
    _, pairs, sensors, width = k2.shape
    chips, rows, length = mine.shape
    return pl.pallas_call(
        adjoint_body, in_specs=[VM] * 4, out_specs=VM,
        out_shape=jax.ShapeDtypeStruct((width // 2, length), f32),
        scratch_shapes=[
            pltpu.VMEM((2, pairs * 8, LANES), f32),
            pltpu.VMEM((2, pairs * 8, LANES), f32),
            pltpu.VMEM((chips, sensors // (chips * rows), rows, length), f32),
        ],
        compiler_params=params(12), name="adjoint",
    )(k2, mine, other, table)


def gradient_body(a_ref, b_ref, p_ref, rig_ref, g_ref, q_ref):
    gradient = (a_ref[...] + b_ref[...]) * rig_ref[:, 0:1] * jax.nn.sigmoid(p_ref[...])
    g_ref[...] = gradient
    total = jnp.sum(jnp.sum(gradient * gradient, axis=0, keepdims=True), axis=1, keepdims=True)
    q_ref[...] = jnp.broadcast_to(total, q_ref.shape)


def gradient_and_square(own, received, param, scale_rows, peers):
    return pl.pallas_call(
        gradient_body, in_specs=[VM] * 4, out_specs=[VM] * 2,
        out_shape=[jax.ShapeDtypeStruct(param.shape, f32), jax.ShapeDtypeStruct((peers, LANES), f32)],
        compiler_params=params(4), name="gradient",
    )(own, received, param, scale_rows)


def swap(x, axis):
    return lax.ppermute(x, axis, [(0, 1), (1, 0)])


def to_chips(x):
    return lax.all_to_all(x, "chip", 0, 0)


def exchange_scalars(sums):
    return lax.all_to_all(sums, ("chip", "core"), 0, 0, tiled=True)


def plain_forward(kernel, slip):
    length = slip.shape[1]
    table = sum(table_parts(length).astype(f32))
    spectra = lax.dot_general(slip, table, (NT, ((), ())), precision=highest)
    real, imag = spectra[None, :, :length], spectra[None, :, length:]
    k_real, k_imag = kernel[0].astype(f32), kernel[1].astype(f32)
    out_real = jnp.sum(k_real * real - k_imag * imag, axis=1)
    out_imag = jnp.sum(k_real * imag + k_imag * real, axis=1)
    w = jnp.tile(row_weights(length), (2, 1))
    return jnp.dot(jnp.concatenate([out_real, out_imag], axis=1), table * w, precision=highest)


def plain_adjoint(kernel, residual):
    length = residual.shape[1]
    table = sum(table_parts(length).astype(f32))
    w = jnp.tile(row_weights(length), (2, 1))
    spectrum = lax.dot_general(residual, table * w, (NT, ((), ())), precision=highest)
    real, imag = spectrum[:, None, :length], spectrum[:, None, length:]
    k_real, k_imag = kernel[0].astype(f32), kernel[1].astype(f32)
    back_real = jnp.sum(k_real * real + k_imag * imag, axis=0)
    back_imag = jnp.sum(k_real * imag - k_imag * real, axis=0)
    return jnp.dot(jnp.concatenate([back_real, back_imag], axis=1), table, precision=highest)


def plain_iterations(slip_param, rigidity, kernel, observed, entries):
    chips, cores = lax.axis_size("chip"), lax.axis_size("core")
    own_sources, length = slip_param.shape
    own_count = kernel.shape[1] // (chips * cores)
    src_index = lax.axis_index("chip") * cores + lax.axis_index("core")
    own_observed = lax.dynamic_slice_in_dim(observed, src_index * own_count, own_count, 0)
    param = lax.all_gather(slip_param, "sens", axis=0, tiled=True)
    scale_rows = lax.all_gather(rigidity[:, None], "sens", axis=0, tiled=True)
    misfit = own_observed
    for _ in range(ITERS):
        terms = plain_forward(kernel, scale_rows * jax.nn.softplus(param)).reshape(chips, cores, -1, length)
        partial = lax.psum_scatter(terms, "core", scatter_dimension=1, tiled=False)
        misfit = jnp.sum(to_chips(partial), axis=0) - own_observed
        spread = to_chips(jnp.broadcast_to(misfit[None], (chips, *misfit.shape)))
        residual = lax.all_gather(spread, "core", axis=1, tiled=False)
        back = plain_adjoint(kernel, residual.reshape(-1, length))
        gradient = lax.psum(back, "sens") * scale_rows * jax.nn.sigmoid(param)
        sums = jnp.broadcast_to(jnp.sum(gradient * gradient), (chips * cores, LANES))
        param = moved(param, gradient, exchange_scalars(sums), entries)
    return lax.dynamic_slice_in_dim(param, lax.axis_index("sens") * own_sources, own_sources, 0), misfit


def iterations(slip_param, rigidity, kernel, observed, entries):
    chips, cores = lax.axis_size("chip"), lax.axis_size("core")
    table = table_parts(slip_param.shape[1])
    mine = pack(slip_param, rigidity)
    other = swap(mine, "sens")
    k2 = relayout(kernel)
    param, scale_rows, keep, send = forward_first(k2, mine, other, table, chips, cores)
    for iteration in range(ITERS):
        if iteration:
            param, keep, send = forward_next(k2, param, gradient, sums, scale_rows, table, chips, cores, entries)
        misfit, spread = misfit_and_spread(to_chips(keep + swap(send, "core")), observed)
        near = to_chips(spread)
        back = adjoint(k2, near, swap(near, "core"), table)
        gradient, sums = gradient_and_square(back, swap(back, "sens"), param, scale_rows, chips * cores)
        sums = exchange_scalars(sums)
    return finish(param, gradient, sums, entries), misfit


def local(slip_param, rigidity, kernel, observed):
    own_sources, length = slip_param.shape
    chips, cores, sens = lax.axis_size("chip"), lax.axis_size("core"), lax.axis_size("sens")
    own_count = kernel.shape[1] // (chips * cores)
    entries = own_sources * sens * chips * cores * length
    fits = (
        sens == 2 and cores == 2 and kernel.shape[2] == HALF and kernel.shape[1] == 2 * LANES
        and length % LANES == 0 and (length // 2) % UNROLL == 0 and own_count % 8 == 0
    )
    run = iterations if fits else plain_iterations
    return run(slip_param, rigidity, kernel, observed, entries)


def solution(mesh):
    sens, src = mesh.shape["sens"], mesh.shape["src"]
    cores = 2 if src % 2 == 0 else 1
    split_mesh = Mesh(mesh.devices.reshape(sens, src // cores, cores), ("sens", "chip", "core"))
    in_specs = (
        P(("chip", "core", "sens"), None),
        P(("chip", "core", "sens")),
        P(None, "sens", ("chip", "core"), None),
        P("sens", None),
    )
    out_specs = (P(("chip", "core", "sens"), None), P(("sens", "chip", "core"), None))
    return jax.shard_map(local, mesh=split_mesh, in_specs=in_specs, out_specs=out_specs, check_vma=False)
```

```python
import functools
import math

import jax
import jax.numpy as jnp
import numpy as np
from jax import lax
from jax.experimental import pallas as pl
from jax.experimental.pallas import tpu as pltpu
from jax.sharding import Mesh, PartitionSpec as P

ITERS = 3

highest = lax.Precision.HIGHEST
step_rate = 0.3
epsilon = 1e-06
f32, bf16 = jnp.float32, jnp.bfloat16
LANES = 128
HALF = LANES // 2
NN, NT = ((1,), (0,)), ((1,), (1,))
VM = pl.BlockSpec(memory_space=pltpu.VMEM)
ROWS = 16
PITCH = 196
BUFFERS = 6
UNROLL = 96


def table_parts(length):
    padded = 2 * length
    phases = np.outer(np.arange(length), np.arange(length)) % padded * (2.0 * math.pi / padded)
    table = np.concatenate([np.cos(phases), -np.sin(phases)], axis=0).astype(np.float32)
    high = table.astype(jnp.bfloat16)
    return jnp.asarray(np.stack([high, (table - high.astype(np.float32)).astype(jnp.bfloat16)]))


def row_weights(length):
    row = lax.broadcasted_iota(jnp.int32, (length, 1), 0)
    return jnp.where(row == 0, 0.5 / length, 1.0 / length).astype(f32)


def params(mib):
    return pltpu.CompilerParams(vmem_limit_bytes=mib << 20)


def mm(a, b, dims):
    return lax.dot_general(a, b, (dims, ((), ())), preferred_element_type=f32)


def split(x):
    high = x.astype(bf16)
    return high, (x - high.astype(f32)).astype(bf16)


def mm3(a, b, dims):
    return mm(a[0], b[0], dims) + (mm(a[0], b[1], dims) + mm(a[1], b[0], dims))


def relayout_body(k_hbm, out_ref, buf, stage, sem):
    freqs = k_hbm.shape[3]
    pairs = freqs // 2
    steps = k_hbm.shape[1] // ROWS
    same = lax.broadcasted_iota(jnp.int32, (LANES, LANES), 0) == lax.broadcasted_iota(jnp.int32, (LANES, LANES), 1)
    eye = same.astype(f32).astype(bf16)

    def copies(i):
        slot = lax.rem(i, BUFFERS)
        rows = pl.ds(i * ROWS, ROWS)
        return [pltpu.make_async_copy(k_hbm.at[c, rows], buf.at[slot, c], sem.at[slot, c]) for c in range(2)]

    def start(i):
        for copy in copies(i):
            copy.start()

    for i in range(BUFFERS - 1):
        start(i)

    def step(i, carry):
        slot = lax.rem(i, BUFFERS)
        for copy in copies(i):
            copy.wait()

        @pl.when(i + BUFFERS - 1 < steps)
        def _():
            start(i + BUFFERS - 1)

        for r in range(0, ROWS, 2):
            x = jnp.concatenate([buf[slot, c, r + j] for j in range(2) for c in range(2)], axis=0)
            for chunk in range(freqs // LANES):
                part = x[:, chunk * LANES:(chunk + 1) * LANES]
                o = mm(eye, part, NT) if r % 4 == 0 else part.T.astype(f32)
                for j in range(2):
                    for h in range(2):
                        rows = pl.ds((r + j) * PITCH + chunk * HALF, HALF)
                        stage[h, rows, :] = o[h * HALF:(h + 1) * HALF, j * LANES:(j + 1) * LANES]
        rows = pl.ds(pl.multiple_of(i * ROWS, ROWS), ROWS)
        for h in range(2):
            for pair in range(pairs):
                out_ref[h, pair, rows, :] = stage[h, pl.ds(pair, ROWS, stride=PITCH), :].astype(bf16)
        return carry

    lax.fori_loop(0, steps, step, 0)


def relayout(kernel):
    _, sensors, sources, freqs = kernel.shape
    return pl.pallas_call(
        relayout_body,
        in_specs=[pl.BlockSpec(memory_space=pl.ANY)],
        out_specs=VM,
        out_shape=pltpu.VMEM((2, freqs // 2, sensors, 2 * sources), bf16),
        scratch_shapes=[
            pltpu.VMEM((BUFFERS, 2, ROWS, sources, freqs), bf16),
            pltpu.VMEM((2, ROWS * PITCH, LANES), f32),
            pltpu.SemaphoreType.DMA((BUFFERS, 2)),
        ],
        compiler_params=params(16),
        name="relayout",
    )(kernel)


def pair_row(chunk, h, m):
    return pl.ds(chunk * HALF * 8 + 4 * h + m, HALF, stride=8)


def tile(k_ref, pair):
    return jnp.concatenate([k_ref[0, pair], k_ref[1, pair]], axis=1)


def turned(k_ref, pair):
    blocks = [[k_ref[h, pair, c * LANES:(c + 1) * LANES, :].T for c in range(2)] for h in range(2)]
    return jnp.concatenate([jnp.concatenate(row, axis=1) for row in blocks], axis=0)


def each_pair(pairs, body):
    first = lax.broadcasted_iota(jnp.int32, (8, LANES), 0) < 4

    def step(i, carry):
        for u in range(UNROLL):
            pair = i * UNROLL + u
            body(u, pair, pl.ds(pl.multiple_of(pair * 8, 8), 8), first)
        return carry

    lax.fori_loop(0, pairs // UNROLL, step, 0)


def forward_core(param, scale_rows, k_ref, t_ref, keep_ref, send_ref, lhs, res, terms):
    freqs, sources = param.shape[1], param.shape[0]
    high, rest = split(scale_rows * jax.nn.softplus(param))
    z = mm(t_ref[0], jnp.concatenate([high, high, rest, rest], axis=0), NT)
    z = z[:, :LANES] + (z[:, LANES:] + mm(t_ref[1], jnp.concatenate([high, high], axis=0), NT))
    low = lax.broadcasted_iota(jnp.int32, (freqs, LANES), 1) < sources
    real, imag = z[:freqs], z[freqs:]
    for m, x in enumerate((jnp.where(low, real, -imag), jnp.where(low, imag, real))):
        high = x.astype(bf16).astype(f32)
        for n, v in enumerate((high, x - high)):
            for chunk in range(freqs // LANES):
                for h in range(2):
                    first = chunk * LANES + h * HALF
                    lhs[pair_row(chunk, h, 2 * n + m), :] = v[first:first + HALF]

    def body(u, pair, rows, first):
        v = lhs[rows, :]
        a = jnp.concatenate([jnp.where(first, v, 0.0), jnp.where(first, 0.0, v)], axis=1).astype(bf16)
        o = mm(a, turned(k_ref, pair), NN) if u % 3 else mm(a, tile(k_ref, pair), NT)
        res[0, rows, :] = o[:, :LANES]
        res[1, rows, :] = o[:, LANES:]

    each_pair(k_ref.shape[1], body)
    w = row_weights(freqs)
    halves = []
    for m in range(2):
        parts = []
        for chunk in range(freqs // LANES):
            for h in range(2):
                high, rest = pair_row(chunk, h, m), pair_row(chunk, h, 2 + m)
                parts.append(jnp.concatenate([res[c, high, :] + res[c, rest, :] for c in range(2)], axis=1))
        halves.append(jnp.concatenate(parts, axis=0) * w)
    spectrum = jnp.concatenate(halves, axis=0).T
    terms[...] = mm3(split(spectrum), (t_ref[0], t_ref[1]), NN).reshape(terms.shape)
    core = lax.axis_index("core")
    keep_ref[...] = terms[:, core]
    send_ref[...] = terms[:, terms.shape[1] - 1 - core]


def forward_first_body(k_ref, mine_ref, other_ref, rig_mine_ref, rig_other_ref, t_ref, new_ref, rig_ref, keep_ref, send_ref, lhs, res, terms, both, scales):
    sens = lax.axis_index("sens")
    rows = mine_ref.shape[0]
    same = lax.broadcasted_iota(jnp.int32, (rows, rows), 0) == lax.broadcasted_iota(jnp.int32, (rows, rows), 1)
    for place, p_ref, r_ref in ((sens, mine_ref, rig_mine_ref), (1 - sens, other_ref, rig_other_ref)):
        both[place] = p_ref[...]
        column = jnp.sum(jnp.where(same, jnp.broadcast_to(r_ref[...], (rows, rows)), 0.0), axis=1, keepdims=True)
        scales[place] = jnp.broadcast_to(column, (rows, LANES))
    param = both[...].reshape(new_ref.shape)
    scale_rows = scales[...].reshape(rig_ref.shape)
    new_ref[...] = param
    rig_ref[...] = scale_rows
    forward_core(param, scale_rows[:, 0:1], k_ref, t_ref, keep_ref, send_ref, lhs, res, terms)


def moved(param, gradient, sums, entries):
    square_sum = jnp.sum(sums[:, 0:1], axis=0, keepdims=True)
    root_mean = jnp.sqrt(square_sum / entries + epsilon)
    return param - step_rate * gradient / root_mean


def forward_next_body(entries, k_ref, p_ref, g_ref, q_ref, rig_ref, t_ref, new_ref, keep_ref, send_ref, lhs, res, terms):
    param = moved(p_ref[...], g_ref[...], q_ref[...], entries)
    new_ref[...] = param
    forward_core(param, rig_ref[:, 0:1], k_ref, t_ref, keep_ref, send_ref, lhs, res, terms)


def forward_spaces(k2, length, chips, cores):
    _, pairs, sensors, _ = k2.shape
    rows = sensors // (chips * cores)
    outs = [jax.ShapeDtypeStruct((chips, rows, length), f32)] * 2
    scratch = [
        pltpu.VMEM((pairs * 8, LANES), f32),
        pltpu.VMEM((2, pairs * 8, LANES), f32),
        pltpu.VMEM((chips, cores, rows, length), f32),
    ]
    return outs, scratch


def forward_first(k2, mine, other, rig_mine, rig_other, table, chips, cores):
    sources, length = 2 * mine.shape[0], table.shape[2]
    outs, scratch = forward_spaces(k2, length, chips, cores)
    return pl.pallas_call(
        forward_first_body, in_specs=[VM] * 6, out_specs=[VM] * 4,
        out_shape=[jax.ShapeDtypeStruct((sources, length), f32), jax.ShapeDtypeStruct((sources, LANES), f32)] + outs,
        scratch_shapes=scratch + [pltpu.VMEM((2, *mine.shape), f32), pltpu.VMEM((2, mine.shape[0], LANES), f32)],
        compiler_params=params(12), name="forward_first",
    )(k2, mine, other, rig_mine, rig_other, table)


def forward_next(k2, param, gradient, sums, scale_rows, table, chips, cores, entries):
    outs, scratch = forward_spaces(k2, param.shape[1], chips, cores)
    return pl.pallas_call(
        functools.partial(forward_next_body, entries), in_specs=[VM] * 6, out_specs=[VM] * 3,
        out_shape=[jax.ShapeDtypeStruct(param.shape, f32)] + outs,
        scratch_shapes=scratch, compiler_params=params(12), name="forward_next",
    )(k2, param, gradient, sums, scale_rows, table)


def misfit_body(parts_ref, obs_ref, m_ref, spread_ref):
    chips, rows, _ = parts_ref.shape
    first = (lax.axis_index("chip") * lax.axis_size("core") + lax.axis_index("core")) * rows
    total = parts_ref[0]
    for c in range(1, chips):
        total = total + parts_ref[c]
    misfit = total - obs_ref[pl.ds(pl.multiple_of(first, 8), rows), :]
    m_ref[...] = misfit
    for c in range(chips):
        spread_ref[c] = misfit


def misfit_and_spread(parts, observed, last):
    space = jax.ShapeDtypeStruct if last else pltpu.VMEM
    return pl.pallas_call(
        misfit_body, in_specs=[VM] * 2, out_specs=[VM] * 2,
        out_shape=[space(parts.shape[1:], f32), jax.ShapeDtypeStruct(parts.shape, f32)],
        compiler_params=params(4), name="misfit",
    )(parts, observed)


def finish_body(entries, p_ref, g_ref, q_ref, o_ref):
    rows = o_ref.shape[0]
    own = pl.ds(pl.multiple_of(lax.axis_index("sens") * rows, 8), rows)
    o_ref[...] = moved(p_ref[own, :], g_ref[own, :], q_ref[...], entries)


def finish(param, gradient, sums, entries):
    return pl.pallas_call(
        functools.partial(finish_body, entries), in_specs=[VM] * 3, out_specs=VM,
        out_shape=jax.ShapeDtypeStruct((param.shape[0] // 2, param.shape[1]), f32),
        compiler_params=params(4), name="finish",
    )(param, gradient, sums)


def adjoint_body(k_ref, mine_ref, other_ref, t_ref, o_ref, lhs, res, full):
    freqs, sources = t_ref.shape[2], k_ref.shape[3] // 2
    core = lax.axis_index("core")
    full[:, core] = mine_ref[...]
    full[:, full.shape[1] - 1 - core] = other_ref[...]
    misfit = full[...].reshape(k_ref.shape[2], freqs)
    spectrum = mm3((t_ref[0], t_ref[1]), split(misfit), NT)
    w = row_weights(freqs)
    for m in range(2):
        x = spectrum[m * freqs:(m + 1) * freqs] * w
        high = x.astype(bf16).astype(f32)
        for n, v in enumerate((high, x - high)):
            for chunk in range(freqs // LANES):
                for h in range(2):
                    first = chunk * LANES + h * HALF
                    for c in range(2):
                        lhs[c, pair_row(chunk, h, 2 * n + m), :] = v[first:first + HALF, c * LANES:(c + 1) * LANES]

    def body(u, pair, rows, first):
        a = jnp.concatenate([lhs[0, rows, :], lhs[1, rows, :]], axis=1).astype(bf16)
        o = mm(a, tile(k_ref, pair), NN)
        res[rows, :] = jnp.where(first, o[:, :LANES], o[:, LANES:])

    each_pair(k_ref.shape[1], body)
    low = lax.broadcasted_iota(jnp.int32, (HALF, LANES), 1) < sources
    parts = []
    for chunk in range(freqs // LANES):
        for h in range(2):
            real, imag = [res[pair_row(chunk, h, m), :] + res[pair_row(chunk, h, 2 + m), :] for m in range(2)]
            parts.append(jnp.where(low, real, -real) + pltpu.roll(imag, sources, 1))
    back = jnp.concatenate(parts, axis=0).T
    o_ref[...] = mm3(split(back[:sources]), (t_ref[0, :freqs], t_ref[1, :freqs]), NN) + mm3(
        split(back[sources:]), (t_ref[0, freqs:], t_ref[1, freqs:]), NN
    )


def adjoint(k2, mine, other, table):
    _, pairs, sensors, width = k2.shape
    chips, rows, length = mine.shape
    return pl.pallas_call(
        adjoint_body, in_specs=[VM] * 4, out_specs=VM,
        out_shape=jax.ShapeDtypeStruct((width // 2, length), f32),
        scratch_shapes=[
            pltpu.VMEM((2, pairs * 8, LANES), f32),
            pltpu.VMEM((pairs * 8, LANES), f32),
            pltpu.VMEM((chips, sensors // (chips * rows), rows, length), f32),
        ],
        compiler_params=params(12), name="adjoint",
    )(k2, mine, other, table)


def gradient_body(a_ref, b_ref, p_ref, rig_ref, g_ref, q_ref):
    gradient = (a_ref[...] + b_ref[...]) * rig_ref[:, 0:1] * jax.nn.sigmoid(p_ref[...])
    g_ref[...] = gradient
    total = jnp.sum(jnp.sum(gradient * gradient, axis=0, keepdims=True), axis=1, keepdims=True)
    q_ref[...] = jnp.broadcast_to(total, q_ref.shape)


def gradient_and_square(own, received, param, scale_rows, peers):
    return pl.pallas_call(
        gradient_body, in_specs=[VM] * 4, out_specs=[VM] * 2,
        out_shape=[jax.ShapeDtypeStruct(param.shape, f32), jax.ShapeDtypeStruct((peers, LANES), f32)],
        compiler_params=params(4), name="gradient",
    )(own, received, param, scale_rows)


def swap(x, axis):
    return lax.ppermute(x, axis, [(0, 1), (1, 0)])


def to_chips(x):
    return lax.all_to_all(x, "chip", 0, 0)


def exchange_scalars(sums):
    return lax.all_to_all(sums, ("chip", "core"), 0, 0, tiled=True)


def plain_forward(kernel, slip):
    length = slip.shape[1]
    table = sum(table_parts(length).astype(f32))
    spectra = lax.dot_general(slip, table, (NT, ((), ())), precision=highest)
    real, imag = spectra[None, :, :length], spectra[None, :, length:]
    k_real, k_imag = kernel[0].astype(f32), kernel[1].astype(f32)
    out_real = jnp.sum(k_real * real - k_imag * imag, axis=1)
    out_imag = jnp.sum(k_real * imag + k_imag * real, axis=1)
    w = jnp.tile(row_weights(length), (2, 1))
    return jnp.dot(jnp.concatenate([out_real, out_imag], axis=1), table * w, precision=highest)


def plain_adjoint(kernel, residual):
    length = residual.shape[1]
    table = sum(table_parts(length).astype(f32))
    w = jnp.tile(row_weights(length), (2, 1))
    spectrum = lax.dot_general(residual, table * w, (NT, ((), ())), precision=highest)
    real, imag = spectrum[:, None, :length], spectrum[:, None, length:]
    k_real, k_imag = kernel[0].astype(f32), kernel[1].astype(f32)
    back_real = jnp.sum(k_real * real + k_imag * imag, axis=0)
    back_imag = jnp.sum(k_real * imag - k_imag * real, axis=0)
    return jnp.dot(jnp.concatenate([back_real, back_imag], axis=1), table, precision=highest)


def plain_iterations(slip_param, rigidity, kernel, observed, entries):
    chips, cores = lax.axis_size("chip"), lax.axis_size("core")
    own_sources, length = slip_param.shape
    own_count = kernel.shape[1] // (chips * cores)
    src_index = lax.axis_index("chip") * cores + lax.axis_index("core")
    own_observed = lax.dynamic_slice_in_dim(observed, src_index * own_count, own_count, 0)
    param = lax.all_gather(slip_param, "sens", axis=0, tiled=True)
    scale_rows = lax.all_gather(rigidity[:, None], "sens", axis=0, tiled=True)
    misfit = own_observed
    for _ in range(ITERS):
        terms = plain_forward(kernel, scale_rows * jax.nn.softplus(param)).reshape(chips, cores, -1, length)
        partial = lax.psum_scatter(terms, "core", scatter_dimension=1, tiled=False)
        misfit = jnp.sum(to_chips(partial), axis=0) - own_observed
        spread = to_chips(jnp.broadcast_to(misfit[None], (chips, *misfit.shape)))
        residual = lax.all_gather(spread, "core", axis=1, tiled=False)
        back = plain_adjoint(kernel, residual.reshape(-1, length))
        gradient = lax.psum(back, "sens") * scale_rows * jax.nn.sigmoid(param)
        sums = jnp.broadcast_to(jnp.sum(gradient * gradient), (chips * cores, LANES))
        param = moved(param, gradient, exchange_scalars(sums), entries)
    return lax.dynamic_slice_in_dim(param, lax.axis_index("sens") * own_sources, own_sources, 0), misfit


def iterations(slip_param, rigidity, kernel, observed, entries):
    chips, cores = lax.axis_size("chip"), lax.axis_size("core")
    table = table_parts(slip_param.shape[1])
    scales = rigidity.reshape(1, -1)
    others, other_scales = swap(slip_param, "sens"), swap(scales, "sens")
    k2 = relayout(kernel)
    param, scale_rows, keep, send = forward_first(k2, slip_param, others, scales, other_scales, table, chips, cores)
    for iteration in range(ITERS):
        if iteration:
            param, keep, send = forward_next(k2, param, gradient, sums, scale_rows, table, chips, cores, entries)
        misfit, spread = misfit_and_spread(to_chips(keep + swap(send, "core")), observed, iteration == ITERS - 1)
        near = to_chips(spread)
        back = adjoint(k2, near, swap(near, "core"), table)
        gradient, sums = gradient_and_square(back, swap(back, "sens"), param, scale_rows, chips * cores)
        sums = exchange_scalars(sums)
    return finish(param, gradient, sums, entries), misfit


def local(slip_param, rigidity, kernel, observed):
    own_sources, length = slip_param.shape
    chips, cores, sens = lax.axis_size("chip"), lax.axis_size("core"), lax.axis_size("sens")
    own_count = kernel.shape[1] // (chips * cores)
    entries = own_sources * sens * chips * cores * length
    fits = (
        sens == 2 and cores == 2 and kernel.shape[2] == HALF and kernel.shape[1] == 2 * LANES
        and length % LANES == 0 and (length // 2) % UNROLL == 0 and own_count % 8 == 0
    )
    run = iterations if fits else plain_iterations
    return run(slip_param, rigidity, kernel, observed, entries)


def solution(mesh):
    sens, src = mesh.shape["sens"], mesh.shape["src"]
    cores = 2 if src % 2 == 0 else 1
    split_mesh = Mesh(mesh.devices.reshape(sens, src // cores, cores), ("sens", "chip", "core"))
    in_specs = (
        P(("chip", "core", "sens"), None),
        P(("chip", "core", "sens")),
        P(None, "sens", ("chip", "core"), None),
        P("sens", None),
    )
    out_specs = (P(("chip", "core", "sens"), None), P(("sens", "chip", "core"), None))
    return jax.shard_map(local, mesh=split_mesh, in_specs=in_specs, out_specs=out_specs, check_vma=False)
```

```python
import functools
import math

import jax
import jax.numpy as jnp
import numpy as np
from jax import lax
from jax.experimental import pallas as pl
from jax.experimental.pallas import tpu as pltpu
from jax.sharding import Mesh, PartitionSpec as P

ITERS = 3

highest = lax.Precision.HIGHEST
step_rate = 0.3
epsilon = 1e-06
f32, bf16 = jnp.float32, jnp.bfloat16
LANES = 128
HALF = LANES // 2
NN, NT = ((1,), (0,)), ((1,), (1,))
VM = pl.BlockSpec(memory_space=pltpu.VMEM)
ROWS = 16
PITCH = 196
BUFFERS = 6
UNROLL = 96


def table_parts(length):
    padded = 2 * length
    phases = np.outer(np.arange(length), np.arange(length)) % padded * (2.0 * math.pi / padded)
    table = np.concatenate([np.cos(phases), -np.sin(phases)], axis=0).astype(np.float32)
    high = table.astype(jnp.bfloat16)
    return jnp.asarray(np.stack([high, (table - high.astype(np.float32)).astype(jnp.bfloat16)]))


def row_weights(length):
    row = lax.broadcasted_iota(jnp.int32, (length, 1), 0)
    return jnp.where(row == 0, 0.5 / length, 1.0 / length).astype(f32)


def params(mib):
    return pltpu.CompilerParams(vmem_limit_bytes=mib << 20)


def mm(a, b, dims):
    return lax.dot_general(a, b, (dims, ((), ())), preferred_element_type=f32)


def split(x):
    high = x.astype(bf16)
    return high, (x - high.astype(f32)).astype(bf16)


def mm3(a, b, dims):
    return mm(a[0], b[0], dims) + (mm(a[0], b[1], dims) + mm(a[1], b[0], dims))


def relayout_body(cores, k_hbm, out_ref, buf, stage, sem):
    freqs = k_hbm.shape[3]
    pairs = freqs // 2
    steps = k_hbm.shape[1] // ROWS
    chips = steps // cores
    same = lax.broadcasted_iota(jnp.int32, (LANES, LANES), 0) == lax.broadcasted_iota(jnp.int32, (LANES, LANES), 1)
    eye = same.astype(f32).astype(bf16)

    def copies(i):
        slot = lax.rem(i, BUFFERS)
        rows = pl.ds((lax.rem(i, chips) * cores + lax.div(i, chips)) * ROWS, ROWS)
        return [pltpu.make_async_copy(k_hbm.at[c, rows], buf.at[slot, c], sem.at[slot, c]) for c in range(2)]

    def start(i):
        for copy in copies(i):
            copy.start()

    for i in range(BUFFERS - 1):
        start(i)

    def step(i, carry):
        slot = lax.rem(i, BUFFERS)
        for copy in copies(i):
            copy.wait()

        @pl.when(i + BUFFERS - 1 < steps)
        def _():
            start(i + BUFFERS - 1)

        for r in range(0, ROWS, 2):
            x = jnp.concatenate([buf[slot, c, r + j] for j in range(2) for c in range(2)], axis=0)
            for chunk in range(freqs // LANES):
                part = x[:, chunk * LANES:(chunk + 1) * LANES]
                o = mm(eye, part, NT) if r % 4 == 0 else part.T.astype(f32)
                for j in range(2):
                    for h in range(2):
                        rows = pl.ds((r + j) * PITCH + chunk * HALF, HALF)
                        stage[h, rows, :] = o[h * HALF:(h + 1) * HALF, j * LANES:(j + 1) * LANES]
        rows = pl.ds(pl.multiple_of(i * ROWS, ROWS), ROWS)
        for h in range(2):
            for pair in range(pairs):
                out_ref[h, pair, rows, :] = stage[h, pl.ds(pair, ROWS, stride=PITCH), :].astype(bf16)
        return carry

    lax.fori_loop(0, steps, step, 0)


def relayout(kernel, cores):
    _, sensors, sources, freqs = kernel.shape
    return pl.pallas_call(
        functools.partial(relayout_body, cores),
        in_specs=[pl.BlockSpec(memory_space=pl.ANY)],
        out_specs=VM,
        out_shape=pltpu.VMEM((2, freqs // 2, sensors, 2 * sources), bf16),
        scratch_shapes=[
            pltpu.VMEM((BUFFERS, 2, ROWS, sources, freqs), bf16),
            pltpu.VMEM((2, ROWS * PITCH, LANES), f32),
            pltpu.SemaphoreType.DMA((BUFFERS, 2)),
        ],
        compiler_params=params(16),
        name="relayout",
    )(kernel)


def pair_row(chunk, h, m):
    return pl.ds(chunk * HALF * 8 + 4 * h + m, HALF, stride=8)


def tile(k_ref, pair):
    return jnp.concatenate([k_ref[0, pair], k_ref[1, pair]], axis=1)


def turned(k_ref, pair):
    blocks = [[k_ref[h, pair, c * LANES:(c + 1) * LANES, :].T for c in range(2)] for h in range(2)]
    return jnp.concatenate([jnp.concatenate(row, axis=1) for row in blocks], axis=0)


def each_pair(pairs, body):
    first = lax.broadcasted_iota(jnp.int32, (8, LANES), 0) < 4

    def step(i, carry):
        for u in range(UNROLL):
            pair = i * UNROLL + u
            body(u, pair, pl.ds(pl.multiple_of(pair * 8, 8), 8), first)
        return carry

    lax.fori_loop(0, pairs // UNROLL, step, 0)


def forward_core(param, scale_rows, k_ref, t_ref, keep_ref, send_ref, lhs, res, terms):
    freqs, sources = param.shape[1], param.shape[0]
    high, rest = split(scale_rows * jax.nn.softplus(param))
    z = mm(t_ref[0], jnp.concatenate([high, high, rest, rest], axis=0), NT)
    z = z[:, :LANES] + (z[:, LANES:] + mm(t_ref[1], jnp.concatenate([high, high], axis=0), NT))
    low = lax.broadcasted_iota(jnp.int32, (freqs, LANES), 1) < sources
    real, imag = z[:freqs], z[freqs:]
    for m, x in enumerate((jnp.where(low, real, -imag), jnp.where(low, imag, real))):
        high = x.astype(bf16).astype(f32)
        for n, v in enumerate((high, x - high)):
            for chunk in range(freqs // LANES):
                for h in range(2):
                    first = chunk * LANES + h * HALF
                    lhs[pair_row(chunk, h, 2 * n + m), :] = v[first:first + HALF]

    def body(u, pair, rows, first):
        v = lhs[rows, :]
        a = jnp.concatenate([jnp.where(first, v, 0.0), jnp.where(first, 0.0, v)], axis=1).astype(bf16)
        o = mm(a, turned(k_ref, pair), NN) if u % 3 else mm(a, tile(k_ref, pair), NT)
        res[0, rows, :] = o[:, :LANES]
        res[1, rows, :] = o[:, LANES:]

    each_pair(k_ref.shape[1], body)
    w = row_weights(freqs)
    halves = []
    for m in range(2):
        parts = []
        for chunk in range(freqs // LANES):
            for h in range(2):
                high, rest = pair_row(chunk, h, m), pair_row(chunk, h, 2 + m)
                parts.append(jnp.concatenate([res[c, high, :] + res[c, rest, :] for c in range(2)], axis=1))
        halves.append(jnp.concatenate(parts, axis=0) * w)
    spectrum = jnp.concatenate(halves, axis=0).T
    terms[...] = mm3(split(spectrum), (t_ref[0], t_ref[1]), NN).reshape(terms.shape)
    core = lax.axis_index("core")
    keep_ref[...] = terms[core]
    send_ref[...] = terms[1 - core]


def forward_first_body(k_ref, mine_ref, other_ref, rig_mine_ref, rig_other_ref, t_ref, new_ref, rig_ref, keep_ref, send_ref, lhs, res, terms, both, scales):
    sens = lax.axis_index("sens")
    rows = mine_ref.shape[0]
    same = lax.broadcasted_iota(jnp.int32, (rows, rows), 0) == lax.broadcasted_iota(jnp.int32, (rows, rows), 1)
    for place, p_ref, r_ref in ((sens, mine_ref, rig_mine_ref), (1 - sens, other_ref, rig_other_ref)):
        both[place] = p_ref[...]
        column = jnp.sum(jnp.where(same, jnp.broadcast_to(r_ref[...], (rows, rows)), 0.0), axis=1, keepdims=True)
        scales[place] = jnp.broadcast_to(column, (rows, LANES))
    param = both[...].reshape(new_ref.shape)
    scale_rows = scales[...].reshape(rig_ref.shape)
    new_ref[...] = param
    rig_ref[...] = scale_rows
    forward_core(param, scale_rows[:, 0:1], k_ref, t_ref, keep_ref, send_ref, lhs, res, terms)


def moved(param, gradient, sums, entries):
    square_sum = jnp.sum(sums[:, 0:1], axis=0, keepdims=True)
    root_mean = jnp.sqrt(square_sum / entries + epsilon)
    return param - step_rate * gradient / root_mean


def forward_next_body(entries, k_ref, p_ref, g_ref, q_ref, rig_ref, t_ref, new_ref, keep_ref, send_ref, lhs, res, terms):
    param = moved(p_ref[...], g_ref[...], q_ref[...], entries)
    new_ref[...] = param
    forward_core(param, rig_ref[:, 0:1], k_ref, t_ref, keep_ref, send_ref, lhs, res, terms)


def forward_spaces(k2, length, chips, cores):
    _, pairs, sensors, _ = k2.shape
    rows = sensors // (chips * cores)
    outs = [jax.ShapeDtypeStruct((chips, rows, length), f32)] * 2
    scratch = [
        pltpu.VMEM((pairs * 8, LANES), f32),
        pltpu.VMEM((2, pairs * 8, LANES), f32),
        pltpu.VMEM((cores, chips, rows, length), f32),
    ]
    return outs, scratch


def forward_first(k2, mine, other, rig_mine, rig_other, table, chips, cores):
    sources, length = 2 * mine.shape[0], table.shape[2]
    outs, scratch = forward_spaces(k2, length, chips, cores)
    return pl.pallas_call(
        forward_first_body, in_specs=[VM] * 6, out_specs=[VM] * 4,
        out_shape=[jax.ShapeDtypeStruct((sources, length), f32), jax.ShapeDtypeStruct((sources, LANES), f32)] + outs,
        scratch_shapes=scratch + [pltpu.VMEM((2, *mine.shape), f32), pltpu.VMEM((2, mine.shape[0], LANES), f32)],
        compiler_params=params(12), name="forward_first",
    )(k2, mine, other, rig_mine, rig_other, table)


def forward_next(k2, param, gradient, sums, scale_rows, table, chips, cores, entries):
    outs, scratch = forward_spaces(k2, param.shape[1], chips, cores)
    return pl.pallas_call(
        functools.partial(forward_next_body, entries), in_specs=[VM] * 6, out_specs=[VM] * 3,
        out_shape=[jax.ShapeDtypeStruct(param.shape, f32)] + outs,
        scratch_shapes=scratch, compiler_params=params(12), name="forward_next",
    )(k2, param, gradient, sums, scale_rows, table)


def misfit_body(parts_ref, obs_ref, spread_ref, m_ref=None):
    chips, rows, _ = parts_ref.shape
    first = (lax.axis_index("chip") * lax.axis_size("core") + lax.axis_index("core")) * rows
    total = parts_ref[0]
    for c in range(1, chips):
        total = total + parts_ref[c]
    misfit = total - obs_ref[pl.ds(pl.multiple_of(first, 8), rows), :]
    for c in range(chips):
        spread_ref[c] = misfit
    if m_ref is not None:
        m_ref[...] = misfit


def misfit_and_spread(parts, observed, last):
    outs = [jax.ShapeDtypeStruct(parts.shape, f32)]
    if last:
        outs.append(jax.ShapeDtypeStruct(parts.shape[1:], f32))
    return pl.pallas_call(
        misfit_body, in_specs=[VM] * 2, out_specs=[VM] * len(outs), out_shape=outs,
        compiler_params=params(4), name="misfit",
    )(parts, observed)


def finish_body(entries, p_ref, g_ref, q_ref, o_ref):
    rows = o_ref.shape[0]
    own = pl.ds(pl.multiple_of(lax.axis_index("sens") * rows, 8), rows)
    o_ref[...] = moved(p_ref[own, :], g_ref[own, :], q_ref[...], entries)


def finish(param, gradient, sums, entries):
    return pl.pallas_call(
        functools.partial(finish_body, entries), in_specs=[VM] * 3, out_specs=VM,
        out_shape=jax.ShapeDtypeStruct((param.shape[0] // 2, param.shape[1]), f32),
        compiler_params=params(4), name="finish",
    )(param, gradient, sums)


def adjoint_half(core, m_ref, k_ref, t_ref, lhs, store):
    freqs = t_ref.shape[2]
    sensors = k_ref.shape[2] // 2
    high, rest = split(m_ref[...].reshape(sensors, freqs))
    both = mm(t_ref[0], jnp.concatenate([high, rest], axis=0), NT)
    spectrum = both[:, :LANES] + (both[:, LANES:] + mm(t_ref[1], high, NT))
    w = row_weights(freqs)
    for m in range(2):
        x = spectrum[m * freqs:(m + 1) * freqs] * w
        high = x.astype(bf16).astype(f32)
        for n, v in enumerate((high, x - high)):
            for chunk in range(freqs // LANES):
                for h in range(2):
                    first = chunk * LANES + h * HALF
                    lhs[pair_row(chunk, h, 2 * n + m), :] = v[first:first + HALF]
    own = pl.ds(pl.multiple_of(core * sensors, LANES), sensors)

    def body(u, pair, rows, first):
        k = jnp.concatenate([k_ref[0, pair, own, :], k_ref[1, pair, own, :]], axis=1)
        o = mm(lhs[rows, :].astype(bf16), k, NN)
        store(rows, jnp.where(first, o[:, :LANES], o[:, LANES:]))

    each_pair(k_ref.shape[1], body)


def adjoint_mine_body(k_ref, m_ref, t_ref, part_ref, lhs):
    def store(rows, value):
        part_ref[rows, :] = value

    adjoint_half(lax.axis_index("core"), m_ref, k_ref, t_ref, lhs, store)


def adjoint_other_body(k_ref, m_ref, part_ref, t_ref, o_ref, lhs, res):
    freqs, sources = t_ref.shape[2], k_ref.shape[3] // 2

    def store(rows, value):
        res[rows, :] = part_ref[rows, :] + value

    adjoint_half(1 - lax.axis_index("core"), m_ref, k_ref, t_ref, lhs, store)
    low = lax.broadcasted_iota(jnp.int32, (HALF, LANES), 1) < sources
    parts = []
    for chunk in range(freqs // LANES):
        for h in range(2):
            real, imag = [res[pair_row(chunk, h, m), :] + res[pair_row(chunk, h, 2 + m), :] for m in range(2)]
            parts.append(jnp.where(low, real, -real) + pltpu.roll(imag, sources, 1))
    back = jnp.concatenate(parts, axis=0).T
    o_ref[...] = mm3(split(back[:sources]), (t_ref[0, :freqs], t_ref[1, :freqs]), NN) + mm3(
        split(back[sources:]), (t_ref[0, freqs:], t_ref[1, freqs:]), NN
    )


def adjoint_mine(k2, mine, table):
    _, pairs, sensors, width = k2.shape
    spent = pl.CostEstimate(flops=16 * pairs * sensors * width, bytes_accessed=2 * pairs * sensors * width, transcendentals=0)
    return pl.pallas_call(
        adjoint_mine_body, in_specs=[VM] * 3, out_specs=VM,
        out_shape=pltpu.VMEM((pairs * 8, LANES), f32),
        scratch_shapes=[pltpu.VMEM((pairs * 8, LANES), f32)],
        cost_estimate=spent, compiler_params=params(8), name="adjoint_mine",
    )(k2, mine, table)


def adjoint_other(k2, other, part, table):
    _, pairs, _, width = k2.shape
    return pl.pallas_call(
        adjoint_other_body, in_specs=[VM] * 4, out_specs=VM,
        out_shape=jax.ShapeDtypeStruct((width // 2, table.shape[2]), f32),
        scratch_shapes=[pltpu.VMEM((pairs * 8, LANES), f32), pltpu.VMEM((pairs * 8, LANES), f32)],
        compiler_params=params(8), name="adjoint_other",
    )(k2, other, part, table)


def gradient_body(a_ref, b_ref, p_ref, rig_ref, g_ref, q_ref):
    gradient = (a_ref[...] + b_ref[...]) * rig_ref[:, 0:1] * jax.nn.sigmoid(p_ref[...])
    g_ref[...] = gradient
    total = jnp.sum(jnp.sum(gradient * gradient, axis=0, keepdims=True), axis=1, keepdims=True)
    q_ref[...] = jnp.broadcast_to(total, q_ref.shape)


def gradient_and_square(own, received, param, scale_rows, peers):
    return pl.pallas_call(
        gradient_body, in_specs=[VM] * 4, out_specs=[VM] * 2,
        out_shape=[jax.ShapeDtypeStruct(param.shape, f32), jax.ShapeDtypeStruct((peers, LANES), f32)],
        compiler_params=params(4), name="gradient",
    )(own, received, param, scale_rows)


def swap(x, axis):
    return lax.ppermute(x, axis, [(0, 1), (1, 0)])


def to_chips(x):
    return lax.all_to_all(x, "chip", 0, 0)


def exchange_scalars(sums):
    return lax.all_to_all(sums, ("chip", "core"), 0, 0, tiled=True)


def plain_forward(kernel, slip):
    length = slip.shape[1]
    table = sum(table_parts(length).astype(f32))
    spectra = lax.dot_general(slip, table, (NT, ((), ())), precision=highest)
    real, imag = spectra[None, :, :length], spectra[None, :, length:]
    k_real, k_imag = kernel[0].astype(f32), kernel[1].astype(f32)
    out_real = jnp.sum(k_real * real - k_imag * imag, axis=1)
    out_imag = jnp.sum(k_real * imag + k_imag * real, axis=1)
    w = jnp.tile(row_weights(length), (2, 1))
    return jnp.dot(jnp.concatenate([out_real, out_imag], axis=1), table * w, precision=highest)


def plain_adjoint(kernel, residual):
    length = residual.shape[1]
    table = sum(table_parts(length).astype(f32))
    w = jnp.tile(row_weights(length), (2, 1))
    spectrum = lax.dot_general(residual, table * w, (NT, ((), ())), precision=highest)
    real, imag = spectrum[:, None, :length], spectrum[:, None, length:]
    k_real, k_imag = kernel[0].astype(f32), kernel[1].astype(f32)
    back_real = jnp.sum(k_real * real + k_imag * imag, axis=0)
    back_imag = jnp.sum(k_real * imag - k_imag * real, axis=0)
    return jnp.dot(jnp.concatenate([back_real, back_imag], axis=1), table, precision=highest)


def plain_iterations(slip_param, rigidity, kernel, observed, entries):
    chips, cores = lax.axis_size("chip"), lax.axis_size("core")
    own_sources, length = slip_param.shape
    own_count = kernel.shape[1] // (chips * cores)
    src_index = lax.axis_index("chip") * cores + lax.axis_index("core")
    own_observed = lax.dynamic_slice_in_dim(observed, src_index * own_count, own_count, 0)
    param = lax.all_gather(slip_param, "sens", axis=0, tiled=True)
    scale_rows = lax.all_gather(rigidity[:, None], "sens", axis=0, tiled=True)
    misfit = own_observed
    for _ in range(ITERS):
        terms = plain_forward(kernel, scale_rows * jax.nn.softplus(param)).reshape(chips, cores, -1, length)
        partial = lax.psum_scatter(terms, "core", scatter_dimension=1, tiled=False)
        misfit = jnp.sum(to_chips(partial), axis=0) - own_observed
        spread = to_chips(jnp.broadcast_to(misfit[None], (chips, *misfit.shape)))
        residual = lax.all_gather(spread, "core", axis=1, tiled=False)
        back = plain_adjoint(kernel, residual.reshape(-1, length))
        gradient = lax.psum(back, "sens") * scale_rows * jax.nn.sigmoid(param)
        sums = jnp.broadcast_to(jnp.sum(gradient * gradient), (chips * cores, LANES))
        param = moved(param, gradient, exchange_scalars(sums), entries)
    return lax.dynamic_slice_in_dim(param, lax.axis_index("sens") * own_sources, own_sources, 0), misfit


def iterations(slip_param, rigidity, kernel, observed, entries):
    chips, cores = lax.axis_size("chip"), lax.axis_size("core")
    table = table_parts(slip_param.shape[1])
    scales = rigidity.reshape(1, -1)
    others, other_scales = swap(slip_param, "sens"), swap(scales, "sens")
    k2 = relayout(kernel, cores)
    param, scale_rows, keep, send = forward_first(k2, slip_param, others, scales, other_scales, table, chips, cores)
    for iteration in range(ITERS):
        if iteration:
            param, keep, send = forward_next(k2, param, gradient, sums, scale_rows, table, chips, cores, entries)
        spread, *misfit = misfit_and_spread(to_chips(keep + swap(send, "core")), observed, iteration == ITERS - 1)
        near = to_chips(spread)
        far = swap(near, "core")
        back = adjoint_other(k2, far, adjoint_mine(k2, near, table), table)
        gradient, sums = gradient_and_square(back, swap(back, "sens"), param, scale_rows, chips * cores)
        sums = exchange_scalars(sums)
    return finish(param, gradient, sums, entries), misfit[0]


def local(slip_param, rigidity, kernel, observed):
    own_sources, length = slip_param.shape
    chips, cores, sens = lax.axis_size("chip"), lax.axis_size("core"), lax.axis_size("sens")
    own_count = kernel.shape[1] // (chips * cores)
    entries = own_sources * sens * chips * cores * length
    fits = (
        sens == 2 and cores == 2 and kernel.shape[2] == HALF and kernel.shape[1] == 2 * LANES
        and length % LANES == 0 and (length // 2) % UNROLL == 0 and own_count == ROWS
    )
    run = iterations if fits else plain_iterations
    return run(slip_param, rigidity, kernel, observed, entries)


def solution(mesh):
    sens, src = mesh.shape["sens"], mesh.shape["src"]
    cores = 2 if src % 2 == 0 else 1
    split_mesh = Mesh(mesh.devices.reshape(sens, src // cores, cores), ("sens", "chip", "core"))
    in_specs = (
        P(("chip", "core", "sens"), None),
        P(("chip", "core", "sens")),
        P(None, "sens", ("chip", "core"), None),
        P("sens", None),
    )
    out_specs = (P(("chip", "core", "sens"), None), P(("sens", "chip", "core"), None))
    return jax.shard_map(local, mesh=split_mesh, in_specs=in_specs, out_specs=out_specs, check_vma=False)
```

```python
import functools
import math

import jax
import jax.numpy as jnp
import numpy as np
from jax import lax
from jax.experimental import pallas as pl
from jax.experimental.pallas import tpu as pltpu
from jax.sharding import Mesh, PartitionSpec as P

ITERS = 3

highest = lax.Precision.HIGHEST
step_rate = 0.3
epsilon = 1e-06
f32, bf16 = jnp.float32, jnp.bfloat16
LANES = 128
HALF = LANES // 2
NN, NT = ((1,), (0,)), ((1,), (1,))
VM = pl.BlockSpec(memory_space=pltpu.VMEM)
ROWS = 16
PITCH = 196
BUFFERS = 6
UNROLL = 96
ADJOINT_UNROLL = 64


def table_parts(length):
    padded = 2 * length
    phases = np.outer(np.arange(length), np.arange(length)) % padded * (2.0 * math.pi / padded)
    table = np.concatenate([np.cos(phases), -np.sin(phases)], axis=0).astype(np.float32)
    high = table.astype(jnp.bfloat16)
    return jnp.asarray(np.stack([high, (table - high.astype(np.float32)).astype(jnp.bfloat16)]))


def row_weights(length):
    row = lax.broadcasted_iota(jnp.int32, (length, 1), 0)
    return jnp.where(row == 0, 0.5 / length, 1.0 / length).astype(f32)


def params(mib):
    return pltpu.CompilerParams(vmem_limit_bytes=mib << 20)


def mm(a, b, dims):
    return lax.dot_general(a, b, (dims, ((), ())), preferred_element_type=f32)


def split(x):
    high = x.astype(bf16)
    return high, (x - high.astype(f32)).astype(bf16)


def mm3(a, b, dims):
    return mm(a[0], b[0], dims) + (mm(a[0], b[1], dims) + mm(a[1], b[0], dims))


def relayout_body(cores, k_hbm, out_ref, buf, stage, sem):
    freqs = k_hbm.shape[3]
    pairs = freqs // 2
    steps = k_hbm.shape[1] // ROWS
    chips = steps // cores
    same = lax.broadcasted_iota(jnp.int32, (LANES, LANES), 0) == lax.broadcasted_iota(jnp.int32, (LANES, LANES), 1)
    eye = same.astype(f32).astype(bf16)

    def copies(i):
        slot = lax.rem(i, BUFFERS)
        rows = pl.ds((lax.rem(i, chips) * cores + lax.div(i, chips)) * ROWS, ROWS)
        return [pltpu.make_async_copy(k_hbm.at[c, rows], buf.at[slot, c], sem.at[slot, c]) for c in range(2)]

    def start(i):
        for copy in copies(i):
            copy.start()

    for i in range(BUFFERS - 1):
        start(i)

    def step(i, carry):
        slot = lax.rem(i, BUFFERS)
        for copy in copies(i):
            copy.wait()

        @pl.when(i + BUFFERS - 1 < steps)
        def _():
            start(i + BUFFERS - 1)

        for r in range(0, ROWS, 2):
            x = jnp.concatenate([buf[slot, c, r + j] for j in range(2) for c in range(2)], axis=0)
            for chunk in range(freqs // LANES):
                part = x[:, chunk * LANES:(chunk + 1) * LANES]
                o = mm(eye, part, NT) if r % 4 == 0 else part.T.astype(f32)
                for j in range(2):
                    for h in range(2):
                        rows = pl.ds((r + j) * PITCH + chunk * HALF, HALF)
                        stage[h, rows, :] = o[h * HALF:(h + 1) * HALF, j * LANES:(j + 1) * LANES]
        rows = pl.ds(pl.multiple_of(i * ROWS, ROWS), ROWS)
        for h in range(2):
            for pair in range(pairs):
                out_ref[h, pair, rows, :] = stage[h, pl.ds(pair, ROWS, stride=PITCH), :].astype(bf16)
        return carry

    lax.fori_loop(0, steps, step, 0)


def relayout(kernel, cores):
    _, sensors, sources, freqs = kernel.shape
    return pl.pallas_call(
        functools.partial(relayout_body, cores),
        in_specs=[pl.BlockSpec(memory_space=pl.ANY)],
        out_specs=VM,
        out_shape=pltpu.VMEM((2, freqs // 2, sensors, 2 * sources), bf16),
        scratch_shapes=[
            pltpu.VMEM((BUFFERS, 2, ROWS, sources, freqs), bf16),
            pltpu.VMEM((2, ROWS * PITCH, LANES), f32),
            pltpu.SemaphoreType.DMA((BUFFERS, 2)),
        ],
        compiler_params=params(16),
        name="relayout",
    )(kernel)


def pair_row(chunk, h, m):
    return pl.ds(chunk * HALF * 8 + 4 * h + m, HALF, stride=8)


def tile(k_ref, pair):
    return jnp.concatenate([k_ref[0, pair], k_ref[1, pair]], axis=1)


def turned(k_ref, pair):
    blocks = [[k_ref[h, pair, c * LANES:(c + 1) * LANES, :].T for c in range(2)] for h in range(2)]
    return jnp.concatenate([jnp.concatenate(row, axis=1) for row in blocks], axis=0)


def each_pair(pairs, unroll, body):
    first = lax.broadcasted_iota(jnp.int32, (8, LANES), 0) < 4

    def step(i, carry):
        for u in range(unroll):
            pair = i * unroll + u
            body(u, pair, pl.ds(pl.multiple_of(pair * 8, 8), 8), first)
        return carry

    lax.fori_loop(0, pairs // unroll, step, 0)


def forward_core(param, scale_rows, k_ref, t_ref, res, send_ref, lhs):
    freqs, sources = param.shape[1], param.shape[0]
    high, rest = split(scale_rows * jax.nn.softplus(param))
    z = mm(t_ref[0], jnp.concatenate([high, high, rest, rest], axis=0), NT)
    z = z[:, :LANES] + (z[:, LANES:] + mm(t_ref[1], jnp.concatenate([high, high], axis=0), NT))
    low = lax.broadcasted_iota(jnp.int32, (freqs, LANES), 1) < sources
    real, imag = z[:freqs], z[freqs:]
    for m, x in enumerate((jnp.where(low, real, -imag), jnp.where(low, imag, real))):
        high = x.astype(bf16).astype(f32)
        for n, v in enumerate((high, x - high)):
            for chunk in range(freqs // LANES):
                for h in range(2):
                    first = chunk * LANES + h * HALF
                    lhs[pair_row(chunk, h, 2 * n + m), :] = v[first:first + HALF]

    def body(u, pair, rows, first):
        v = lhs[rows, :]
        a = jnp.concatenate([jnp.where(first, v, 0.0), jnp.where(first, 0.0, v)], axis=1).astype(bf16)
        o = mm(a, turned(k_ref, pair), NN) if u % 3 else mm(a, tile(k_ref, pair), NT)
        res[0, rows, :] = o[:, :LANES]
        res[1, rows, :] = o[:, LANES:]

    each_pair(k_ref.shape[1], UNROLL, body)
    send_ref[...] = predicted(res, 1 - lax.axis_index("core"), t_ref).reshape(send_ref.shape)


def predicted(res, core, t_ref):
    freqs = t_ref.shape[2]
    w = row_weights(freqs)
    halves = []
    for m in range(2):
        parts = []
        for chunk in range(freqs // LANES):
            for h in range(2):
                parts.append(res[core, pair_row(chunk, h, m), :] + res[core, pair_row(chunk, h, 2 + m), :])
        halves.append(jnp.concatenate(parts, axis=0) * w)
    spectrum = jnp.concatenate(halves, axis=0).T
    return mm3(split(spectrum), (t_ref[0], t_ref[1]), NN)


def keep_body(res_ref, t_ref, keep_ref):
    keep_ref[...] = predicted(res_ref, lax.axis_index("core"), t_ref).reshape(keep_ref.shape)


def kept_terms(res, send, table):
    spent = pl.CostEstimate(flops=12 * res.size * table.shape[2], bytes_accessed=8 * res.size, transcendentals=0)
    return pl.pallas_call(
        keep_body, in_specs=[VM] * 2, out_specs=VM, out_shape=jax.ShapeDtypeStruct(send.shape, f32),
        cost_estimate=spent, compiler_params=params(4), name="keep",
    )(res, table)


def forward_first_body(k_ref, mine_ref, other_ref, rig_mine_ref, rig_other_ref, t_ref, new_ref, rig_ref, res, send_ref, lhs, both, scales):
    sens = lax.axis_index("sens")
    rows = mine_ref.shape[0]
    same = lax.broadcasted_iota(jnp.int32, (rows, rows), 0) == lax.broadcasted_iota(jnp.int32, (rows, rows), 1)
    for place, p_ref, r_ref in ((sens, mine_ref, rig_mine_ref), (1 - sens, other_ref, rig_other_ref)):
        both[place] = p_ref[...]
        column = jnp.sum(jnp.where(same, jnp.broadcast_to(r_ref[...], (rows, rows)), 0.0), axis=1, keepdims=True)
        scales[place] = jnp.broadcast_to(column, (rows, LANES))
    param = both[...].reshape(new_ref.shape)
    scale_rows = scales[...].reshape(rig_ref.shape)
    new_ref[...] = param
    rig_ref[...] = scale_rows
    forward_core(param, scale_rows[:, 0:1], k_ref, t_ref, res, send_ref, lhs)


def moved(param, gradient, sums, entries):
    square_sum = jnp.sum(sums[:, 0:1], axis=0, keepdims=True)
    root_mean = jnp.sqrt(square_sum / entries + epsilon)
    return param - step_rate * gradient / root_mean


def forward_next_body(entries, k_ref, p_ref, g_ref, q_ref, rig_ref, t_ref, new_ref, res, send_ref, lhs):
    param = moved(p_ref[...], g_ref[...], q_ref[...], entries)
    new_ref[...] = param
    forward_core(param, rig_ref[:, 0:1], k_ref, t_ref, res, send_ref, lhs)


def forward_spaces(k2, length, chips, cores):
    _, pairs, sensors, _ = k2.shape
    rows = sensors // (chips * cores)
    outs = [pltpu.VMEM((2, pairs * 8, LANES), f32), jax.ShapeDtypeStruct((chips, rows, length), f32)]
    scratch = [pltpu.VMEM((pairs * 8, LANES), f32)]
    return outs, scratch


def forward_first(k2, mine, other, rig_mine, rig_other, table, chips, cores):
    sources, length = 2 * mine.shape[0], table.shape[2]
    outs, scratch = forward_spaces(k2, length, chips, cores)
    return pl.pallas_call(
        forward_first_body, in_specs=[VM] * 6, out_specs=[VM] * 4,
        out_shape=[jax.ShapeDtypeStruct((sources, length), f32), jax.ShapeDtypeStruct((sources, LANES), f32)] + outs,
        scratch_shapes=scratch + [pltpu.VMEM((2, *mine.shape), f32), pltpu.VMEM((2, mine.shape[0], LANES), f32)],
        compiler_params=params(12), name="forward_first",
    )(k2, mine, other, rig_mine, rig_other, table)


def forward_next(k2, param, gradient, sums, scale_rows, table, chips, cores, entries):
    outs, scratch = forward_spaces(k2, param.shape[1], chips, cores)
    return pl.pallas_call(
        functools.partial(forward_next_body, entries), in_specs=[VM] * 6, out_specs=[VM] * 3,
        out_shape=[jax.ShapeDtypeStruct(param.shape, f32)] + outs,
        scratch_shapes=scratch, compiler_params=params(12), name="forward_next",
    )(k2, param, gradient, sums, scale_rows, table)


def misfit_body(parts_ref, obs_ref, spread_ref, m_ref=None):
    chips, rows, _ = parts_ref.shape
    first = (lax.axis_index("chip") * lax.axis_size("core") + lax.axis_index("core")) * rows
    total = parts_ref[0]
    for c in range(1, chips):
        total = total + parts_ref[c]
    misfit = total - obs_ref[pl.ds(pl.multiple_of(first, 8), rows), :]
    for c in range(chips):
        spread_ref[c] = misfit
    if m_ref is not None:
        m_ref[...] = misfit


def misfit_and_spread(parts, observed, last):
    outs = [jax.ShapeDtypeStruct(parts.shape, f32)]
    if last:
        outs.append(jax.ShapeDtypeStruct(parts.shape[1:], f32))
    return pl.pallas_call(
        misfit_body, in_specs=[VM] * 2, out_specs=[VM] * len(outs), out_shape=outs,
        compiler_params=params(4), name="misfit",
    )(parts, observed)


def finish_body(entries, p_ref, g_ref, q_ref, o_ref):
    rows = o_ref.shape[0]
    own = pl.ds(pl.multiple_of(lax.axis_index("sens") * rows, 8), rows)
    o_ref[...] = moved(p_ref[own, :], g_ref[own, :], q_ref[...], entries)


def finish(param, gradient, sums, entries):
    return pl.pallas_call(
        functools.partial(finish_body, entries), in_specs=[VM] * 3, out_specs=VM,
        out_shape=jax.ShapeDtypeStruct((param.shape[0] // 2, param.shape[1]), f32),
        compiler_params=params(4), name="finish",
    )(param, gradient, sums)


def adjoint_half(core, m_ref, k_ref, t_ref, lhs, store):
    freqs = t_ref.shape[2]
    sensors = k_ref.shape[2] // 2
    high, rest = split(m_ref[...].reshape(sensors, freqs))
    both = mm(t_ref[0], jnp.concatenate([high, rest], axis=0), NT)
    spectrum = both[:, :LANES] + (both[:, LANES:] + mm(t_ref[1], high, NT))
    w = row_weights(freqs)
    for m in range(2):
        x = spectrum[m * freqs:(m + 1) * freqs] * w
        high = x.astype(bf16).astype(f32)
        for n, v in enumerate((high, x - high)):
            for chunk in range(freqs // LANES):
                for h in range(2):
                    first = chunk * LANES + h * HALF
                    lhs[pair_row(chunk, h, 2 * n + m), :] = v[first:first + HALF]
    own = pl.ds(pl.multiple_of(core * sensors, LANES), sensors)

    def body(u, pair, rows, first):
        k = jnp.concatenate([k_ref[0, pair, own, :], k_ref[1, pair, own, :]], axis=1)
        o = mm(lhs[rows, :].astype(bf16), k, NN)
        store(rows, jnp.where(first, o[:, :LANES], o[:, LANES:]))

    each_pair(k_ref.shape[1], ADJOINT_UNROLL, body)


def adjoint_mine_body(k_ref, m_ref, t_ref, part_ref, lhs):
    def store(rows, value):
        part_ref[rows, :] = value

    adjoint_half(lax.axis_index("core"), m_ref, k_ref, t_ref, lhs, store)


def adjoint_other_body(k_ref, m_ref, part_ref, t_ref, o_ref, lhs, res):
    freqs, sources = t_ref.shape[2], k_ref.shape[3] // 2

    def store(rows, value):
        res[rows, :] = part_ref[rows, :] + value

    adjoint_half(1 - lax.axis_index("core"), m_ref, k_ref, t_ref, lhs, store)
    low = lax.broadcasted_iota(jnp.int32, (HALF, LANES), 1) < sources
    parts = []
    for chunk in range(freqs // LANES):
        for h in range(2):
            real, imag = [res[pair_row(chunk, h, m), :] + res[pair_row(chunk, h, 2 + m), :] for m in range(2)]
            parts.append(jnp.where(low, real, -real) + pltpu.roll(imag, sources, 1))
    back = jnp.concatenate(parts, axis=0).T
    o_ref[...] = mm3(split(back[:sources]), (t_ref[0, :freqs], t_ref[1, :freqs]), NN) + mm3(
        split(back[sources:]), (t_ref[0, freqs:], t_ref[1, freqs:]), NN
    )


def adjoint_mine(k2, mine, table):
    _, pairs, sensors, width = k2.shape
    spent = pl.CostEstimate(flops=16 * pairs * sensors * width, bytes_accessed=2 * pairs * sensors * width, transcendentals=0)
    return pl.pallas_call(
        adjoint_mine_body, in_specs=[VM] * 3, out_specs=VM,
        out_shape=pltpu.VMEM((pairs * 8, LANES), f32),
        scratch_shapes=[pltpu.VMEM((pairs * 8, LANES), f32)],
        cost_estimate=spent, compiler_params=params(8), name="adjoint_mine",
    )(k2, mine, table)


def adjoint_other(k2, other, part, table):
    _, pairs, _, width = k2.shape
    return pl.pallas_call(
        adjoint_other_body, in_specs=[VM] * 4, out_specs=VM,
        out_shape=jax.ShapeDtypeStruct((width // 2, table.shape[2]), f32),
        scratch_shapes=[pltpu.VMEM((pairs * 8, LANES), f32), pltpu.VMEM((pairs * 8, LANES), f32)],
        compiler_params=params(8), name="adjoint_other",
    )(k2, other, part, table)


def gradient_body(a_ref, b_ref, p_ref, rig_ref, g_ref, q_ref):
    gradient = (a_ref[...] + b_ref[...]) * rig_ref[:, 0:1] * jax.nn.sigmoid(p_ref[...])
    g_ref[...] = gradient
    total = jnp.sum(jnp.sum(gradient * gradient, axis=0, keepdims=True), axis=1, keepdims=True)
    q_ref[...] = jnp.broadcast_to(total, q_ref.shape)


def gradient_and_square(own, received, param, scale_rows, peers):
    return pl.pallas_call(
        gradient_body, in_specs=[VM] * 4, out_specs=[VM] * 2,
        out_shape=[jax.ShapeDtypeStruct(param.shape, f32), jax.ShapeDtypeStruct((peers, LANES), f32)],
        compiler_params=params(4), name="gradient",
    )(own, received, param, scale_rows)


def swap(x, axis):
    return lax.ppermute(x, axis, [(0, 1), (1, 0)])


def to_chips(x):
    return lax.all_to_all(x, "chip", 0, 0)


def exchange_scalars(sums):
    return lax.all_to_all(sums, ("chip", "core"), 0, 0, tiled=True)


def plain_forward(kernel, slip):
    length = slip.shape[1]
    table = sum(table_parts(length).astype(f32))
    spectra = lax.dot_general(slip, table, (NT, ((), ())), precision=highest)
    real, imag = spectra[None, :, :length], spectra[None, :, length:]
    k_real, k_imag = kernel[0].astype(f32), kernel[1].astype(f32)
    out_real = jnp.sum(k_real * real - k_imag * imag, axis=1)
    out_imag = jnp.sum(k_real * imag + k_imag * real, axis=1)
    w = jnp.tile(row_weights(length), (2, 1))
    return jnp.dot(jnp.concatenate([out_real, out_imag], axis=1), table * w, precision=highest)


def plain_adjoint(kernel, residual):
    length = residual.shape[1]
    table = sum(table_parts(length).astype(f32))
    w = jnp.tile(row_weights(length), (2, 1))
    spectrum = lax.dot_general(residual, table * w, (NT, ((), ())), precision=highest)
    real, imag = spectrum[:, None, :length], spectrum[:, None, length:]
    k_real, k_imag = kernel[0].astype(f32), kernel[1].astype(f32)
    back_real = jnp.sum(k_real * real + k_imag * imag, axis=0)
    back_imag = jnp.sum(k_real * imag - k_imag * real, axis=0)
    return jnp.dot(jnp.concatenate([back_real, back_imag], axis=1), table, precision=highest)


def plain_iterations(slip_param, rigidity, kernel, observed, entries):
    chips, cores = lax.axis_size("chip"), lax.axis_size("core")
    own_sources, length = slip_param.shape
    own_count = kernel.shape[1] // (chips * cores)
    src_index = lax.axis_index("chip") * cores + lax.axis_index("core")
    own_observed = lax.dynamic_slice_in_dim(observed, src_index * own_count, own_count, 0)
    param = lax.all_gather(slip_param, "sens", axis=0, tiled=True)
    scale_rows = lax.all_gather(rigidity[:, None], "sens", axis=0, tiled=True)
    misfit = own_observed
    for _ in range(ITERS):
        terms = plain_forward(kernel, scale_rows * jax.nn.softplus(param)).reshape(chips, cores, -1, length)
        partial = lax.psum_scatter(terms, "core", scatter_dimension=1, tiled=False)
        misfit = jnp.sum(to_chips(partial), axis=0) - own_observed
        spread = to_chips(jnp.broadcast_to(misfit[None], (chips, *misfit.shape)))
        residual = lax.all_gather(spread, "core", axis=1, tiled=False)
        back = plain_adjoint(kernel, residual.reshape(-1, length))
        gradient = lax.psum(back, "sens") * scale_rows * jax.nn.sigmoid(param)
        sums = jnp.broadcast_to(jnp.sum(gradient * gradient), (chips * cores, LANES))
        param = moved(param, gradient, exchange_scalars(sums), entries)
    return lax.dynamic_slice_in_dim(param, lax.axis_index("sens") * own_sources, own_sources, 0), misfit


def iterations(slip_param, rigidity, kernel, observed, entries):
    chips, cores = lax.axis_size("chip"), lax.axis_size("core")
    table = table_parts(slip_param.shape[1])
    scales = rigidity.reshape(1, -1)
    others, other_scales = swap(slip_param, "sens"), swap(scales, "sens")
    k2 = relayout(kernel, cores)
    param, scale_rows, res, send = forward_first(k2, slip_param, others, scales, other_scales, table, chips, cores)
    for iteration in range(ITERS):
        if iteration:
            param, res, send = forward_next(k2, param, gradient, sums, scale_rows, table, chips, cores, entries)
        spread, *misfit = misfit_and_spread(to_chips(kept_terms(res, send, table) + swap(send, "core")), observed, iteration == ITERS - 1)
        near = to_chips(spread)
        far = swap(near, "core")
        back = adjoint_other(k2, far, adjoint_mine(k2, near, table), table)
        gradient, sums = gradient_and_square(back, swap(back, "sens"), param, scale_rows, chips * cores)
        sums = exchange_scalars(sums)
    return finish(param, gradient, sums, entries), misfit[0]


def local(slip_param, rigidity, kernel, observed):
    own_sources, length = slip_param.shape
    chips, cores, sens = lax.axis_size("chip"), lax.axis_size("core"), lax.axis_size("sens")
    own_count = kernel.shape[1] // (chips * cores)
    entries = own_sources * sens * chips * cores * length
    fits = (
        sens == 2 and cores == 2 and kernel.shape[2] == HALF and kernel.shape[1] == 2 * LANES
        and length % LANES == 0 and (length // 2) % UNROLL == 0 and (length // 2) % ADJOINT_UNROLL == 0 and own_count == ROWS
    )
    run = iterations if fits else plain_iterations
    return run(slip_param, rigidity, kernel, observed, entries)


def solution(mesh):
    sens, src = mesh.shape["sens"], mesh.shape["src"]
    cores = 2 if src % 2 == 0 else 1
    split_mesh = Mesh(mesh.devices.reshape(sens, src // cores, cores), ("sens", "chip", "core"))
    in_specs = (
        P(("chip", "core", "sens"), None),
        P(("chip", "core", "sens")),
        P(None, "sens", ("chip", "core"), None),
        P("sens", None),
    )
    out_specs = (P(("chip", "core", "sens"), None), P(("sens", "chip", "core"), None))
    return jax.shard_map(local, mesh=split_mesh, in_specs=in_specs, out_specs=out_specs, check_vma=False)
```

```python
import functools
import math

import jax
import jax.numpy as jnp
import numpy as np
from jax import lax
from jax.experimental import pallas as pl
from jax.experimental.pallas import tpu as pltpu
from jax.sharding import Mesh, PartitionSpec as P

ITERS = 3

highest = lax.Precision.HIGHEST
step_rate = 0.3
epsilon = 1e-06
f32, bf16 = jnp.float32, jnp.bfloat16
LANES = 128
HALF = LANES // 2
NN, NT = ((1,), (0,)), ((1,), (1,))
VM = pl.BlockSpec(memory_space=pltpu.VMEM)
ROWS = 16
PITCH = 196
BUFFERS = 6
UNROLL = 96
ADJOINT_UNROLL = 64


def table_parts(length):
    padded = 2 * length
    phases = np.outer(np.arange(length), np.arange(length)) % padded * (2.0 * math.pi / padded)
    table = np.concatenate([np.cos(phases), -np.sin(phases)], axis=0).astype(np.float32)
    high = table.astype(jnp.bfloat16)
    return jnp.asarray(np.stack([high, (table - high.astype(np.float32)).astype(jnp.bfloat16)]))


def row_weights(length):
    row = lax.broadcasted_iota(jnp.int32, (length, 1), 0)
    return jnp.where(row == 0, 0.5 / length, 1.0 / length).astype(f32)


def params(mib):
    return pltpu.CompilerParams(vmem_limit_bytes=mib << 20)


def mm(a, b, dims):
    return lax.dot_general(a, b, (dims, ((), ())), preferred_element_type=f32)


def split(x):
    high = x.astype(bf16)
    return high, (x - high.astype(f32)).astype(bf16)


def mm3(a, b, dims):
    return mm(a[0], b[0], dims) + (mm(a[0], b[1], dims) + mm(a[1], b[0], dims))


def relayout_body(cores, k_hbm, out_ref, buf, stage, sem):
    freqs = k_hbm.shape[3]
    pairs = freqs // 2
    steps = k_hbm.shape[1] // ROWS
    chips = steps // cores
    same = lax.broadcasted_iota(jnp.int32, (LANES, LANES), 0) == lax.broadcasted_iota(jnp.int32, (LANES, LANES), 1)
    eye = same.astype(f32).astype(bf16)

    def copies(i):
        slot = lax.rem(i, BUFFERS)
        rows = pl.ds((lax.rem(i, chips) * cores + lax.div(i, chips)) * ROWS, ROWS)
        return [pltpu.make_async_copy(k_hbm.at[c, rows], buf.at[slot, c], sem.at[slot, c]) for c in range(2)]

    def start(i):
        for copy in copies(i):
            copy.start()

    for i in range(BUFFERS - 1):
        start(i)

    def step(i, carry):
        slot = lax.rem(i, BUFFERS)
        for copy in copies(i):
            copy.wait()

        @pl.when(i + BUFFERS - 1 < steps)
        def _():
            start(i + BUFFERS - 1)

        for r in range(0, ROWS, 2):
            x = jnp.concatenate([buf[slot, c, r + j] for j in range(2) for c in range(2)], axis=0)
            for chunk in range(freqs // LANES):
                part = x[:, chunk * LANES:(chunk + 1) * LANES]
                o = mm(eye, part, NT) if r % 4 == 0 else part.T.astype(f32)
                for j in range(2):
                    for h in range(2):
                        rows = pl.ds((r + j) * PITCH + chunk * HALF, HALF)
                        stage[h, rows, :] = o[h * HALF:(h + 1) * HALF, j * LANES:(j + 1) * LANES]
        rows = pl.ds(pl.multiple_of(i * ROWS, ROWS), ROWS)
        for h in range(2):
            for pair in range(pairs):
                out_ref[h, pair, rows, :] = stage[h, pl.ds(pair, ROWS, stride=PITCH), :].astype(bf16)
        return carry

    lax.fori_loop(0, steps, step, 0)


def relayout(kernel, cores):
    _, sensors, sources, freqs = kernel.shape
    return pl.pallas_call(
        functools.partial(relayout_body, cores),
        in_specs=[pl.BlockSpec(memory_space=pl.ANY)],
        out_specs=VM,
        out_shape=pltpu.VMEM((2, freqs // 2, sensors, 2 * sources), bf16),
        scratch_shapes=[
            pltpu.VMEM((BUFFERS, 2, ROWS, sources, freqs), bf16),
            pltpu.VMEM((2, ROWS * PITCH, LANES), f32),
            pltpu.SemaphoreType.DMA((BUFFERS, 2)),
        ],
        compiler_params=params(16),
        name="relayout",
    )(kernel)


def pair_row(chunk, h, m):
    return pl.ds(chunk * HALF * 8 + 4 * h + m, HALF, stride=8)


def tile(k_ref, pair):
    return jnp.concatenate([k_ref[0, pair], k_ref[1, pair]], axis=1)


def turned(k_ref, pair):
    return [[k_ref[h, pair, c * LANES:(c + 1) * LANES, :].T for c in range(2)] for h in range(2)]


def joined(blocks):
    return jnp.concatenate([jnp.concatenate(row, axis=1) for row in blocks], axis=0)


def each_pair(pairs, unroll, body):
    first = lax.broadcasted_iota(jnp.int32, (8, LANES), 0) < 4

    def step(i, carry):
        for u in range(unroll):
            pair = i * unroll + u
            body(u, pair, pl.ds(pl.multiple_of(pair * 8, 8), 8), first)
        return carry

    lax.fori_loop(0, pairs // unroll, step, 0)


def forward_core(param, scale_rows, product, k_ref, t_ref, res, send_ref, lhs):
    freqs, sources = param.shape[1], param.shape[0]
    high, rest = split(scale_rows * jax.nn.softplus(param))
    z = mm(t_ref[0], jnp.concatenate([high, high, rest, rest], axis=0), NT)
    z = z[:, :LANES] + (z[:, LANES:] + mm(t_ref[1], jnp.concatenate([high, high], axis=0), NT))
    low = lax.broadcasted_iota(jnp.int32, (freqs, LANES), 1) < sources
    real, imag = z[:freqs], z[freqs:]
    for m, x in enumerate((jnp.where(low, real, -imag), jnp.where(low, imag, real))):
        high = x.astype(bf16).astype(f32)
        for n, v in enumerate((high, x - high)):
            for chunk in range(freqs // LANES):
                for h in range(2):
                    first = chunk * LANES + h * HALF
                    lhs[pair_row(chunk, h, 2 * n + m), :] = v[first:first + HALF]

    def body(u, pair, rows, first):
        v = lhs[rows, :]
        a = jnp.concatenate([jnp.where(first, v, 0.0), jnp.where(first, 0.0, v)], axis=1).astype(bf16)
        o = product(a, u, pair)
        res[0, rows, :] = o[:, :LANES]
        res[1, rows, :] = o[:, LANES:]

    each_pair(k_ref.shape[1], UNROLL, body)
    send_ref[...] = predicted(res, 1 - lax.axis_index("core"), t_ref).reshape(send_ref.shape)


def predicted(res, core, t_ref):
    freqs = t_ref.shape[2]
    w = row_weights(freqs)
    halves = []
    for m in range(2):
        parts = []
        for chunk in range(freqs // LANES):
            for h in range(2):
                parts.append(res[core, pair_row(chunk, h, m), :] + res[core, pair_row(chunk, h, 2 + m), :])
        halves.append(jnp.concatenate(parts, axis=0) * w)
    spectrum = jnp.concatenate(halves, axis=0).T
    return mm3(split(spectrum), (t_ref[0], t_ref[1]), NN)


def keep_body(res_ref, t_ref, keep_ref):
    keep_ref[...] = predicted(res_ref, lax.axis_index("core"), t_ref).reshape(keep_ref.shape)


def kept_terms(res, send, table):
    spent = pl.CostEstimate(flops=12 * res.size * table.shape[2], bytes_accessed=8 * res.size, transcendentals=0)
    return pl.pallas_call(
        keep_body, in_specs=[VM] * 2, out_specs=VM, out_shape=jax.ShapeDtypeStruct(send.shape, f32),
        cost_estimate=spent, compiler_params=params(4), name="keep",
    )(res, table)


def forward_first_body(k_ref, mine_ref, other_ref, rig_mine_ref, rig_other_ref, t_ref, kept_ref, new_ref, rig_ref, res, send_ref, lhs, both, scales):
    sens = lax.axis_index("sens")
    rows = mine_ref.shape[0]
    same = lax.broadcasted_iota(jnp.int32, (rows, rows), 0) == lax.broadcasted_iota(jnp.int32, (rows, rows), 1)
    for place, p_ref, r_ref in ((sens, mine_ref, rig_mine_ref), (1 - sens, other_ref, rig_other_ref)):
        both[place] = p_ref[...]
        column = jnp.sum(jnp.where(same, jnp.broadcast_to(r_ref[...], (rows, rows)), 0.0), axis=1, keepdims=True)
        scales[place] = jnp.broadcast_to(column, (rows, LANES))
    param = both[...].reshape(new_ref.shape)
    scale_rows = scales[...].reshape(rig_ref.shape)
    new_ref[...] = param
    rig_ref[...] = scale_rows

    def product(a, u, pair):
        if u % 12 in (0, 3, 6, 11):
            return mm(a, tile(k_ref, pair), NT)
        blocks = turned(k_ref, pair)
        if u % 4 == 1:
            for h in range(2):
                for c in range(2):
                    kept_ref[c, pair // 4, h * LANES:(h + 1) * LANES, :] = blocks[h][c]
        return mm(a, joined(blocks), NN)

    forward_core(param, scale_rows[:, 0:1], product, k_ref, t_ref, res, send_ref, lhs)


def moved(param, gradient, sums, entries):
    square_sum = jnp.sum(sums[:, 0:1], axis=0, keepdims=True)
    root_mean = jnp.sqrt(square_sum / entries + epsilon)
    return param - step_rate * gradient / root_mean


def forward_next_body(entries, k_ref, kept_ref, p_ref, g_ref, q_ref, rig_ref, t_ref, new_ref, res, send_ref, lhs):
    param = moved(p_ref[...], g_ref[...], q_ref[...], entries)
    new_ref[...] = param

    def product(a, u, pair):
        if u % 4 == 1:
            return mm(a, tile(kept_ref, pair // 4), NN)
        if u % 6 == 0:
            return mm(a, tile(k_ref, pair), NT)
        return mm(a, joined(turned(k_ref, pair)), NN)

    forward_core(param, rig_ref[:, 0:1], product, k_ref, t_ref, res, send_ref, lhs)


def forward_spaces(k2, length, chips, cores):
    _, pairs, sensors, _ = k2.shape
    rows = sensors // (chips * cores)
    outs = [pltpu.VMEM((2, pairs * 8, LANES), f32), jax.ShapeDtypeStruct((chips, rows, length), f32)]
    scratch = [pltpu.VMEM((pairs * 8, LANES), f32)]
    return outs, scratch


def forward_first(k2, mine, other, rig_mine, rig_other, table, chips, cores):
    sources, length = 2 * mine.shape[0], table.shape[2]
    outs, scratch = forward_spaces(k2, length, chips, cores)
    return pl.pallas_call(
        forward_first_body, in_specs=[VM] * 6, out_specs=[VM] * 5,
        out_shape=[pltpu.VMEM((2, k2.shape[1] // 4, 2 * k2.shape[3], k2.shape[2] // 2), bf16), jax.ShapeDtypeStruct((sources, length), f32), jax.ShapeDtypeStruct((sources, LANES), f32)] + outs,
        scratch_shapes=scratch + [pltpu.VMEM((2, *mine.shape), f32), pltpu.VMEM((2, mine.shape[0], LANES), f32)],
        compiler_params=params(6), name="forward_first",
    )(k2, mine, other, rig_mine, rig_other, table)


def forward_next(k2, kept, param, gradient, sums, scale_rows, table, chips, cores, entries):
    outs, scratch = forward_spaces(k2, param.shape[1], chips, cores)
    return pl.pallas_call(
        functools.partial(forward_next_body, entries), in_specs=[VM] * 7, out_specs=[VM] * 3,
        out_shape=[jax.ShapeDtypeStruct(param.shape, f32)] + outs,
        scratch_shapes=scratch, compiler_params=params(6), name="forward_next",
    )(k2, kept, param, gradient, sums, scale_rows, table)


def misfit_body(parts_ref, obs_ref, spread_ref, m_ref=None):
    chips, rows, _ = parts_ref.shape
    first = (lax.axis_index("chip") * lax.axis_size("core") + lax.axis_index("core")) * rows
    total = parts_ref[0]
    for c in range(1, chips):
        total = total + parts_ref[c]
    misfit = total - obs_ref[pl.ds(pl.multiple_of(first, 8), rows), :]
    for c in range(chips):
        spread_ref[c] = misfit
    if m_ref is not None:
        m_ref[...] = misfit


def misfit_and_spread(parts, observed, last):
    outs = [jax.ShapeDtypeStruct(parts.shape, f32)]
    if last:
        outs.append(jax.ShapeDtypeStruct(parts.shape[1:], f32))
    return pl.pallas_call(
        misfit_body, in_specs=[VM] * 2, out_specs=[VM] * len(outs), out_shape=outs,
        compiler_params=params(4), name="misfit",
    )(parts, observed)


def finish_body(entries, p_ref, g_ref, q_ref, o_ref):
    rows = o_ref.shape[0]
    own = pl.ds(pl.multiple_of(lax.axis_index("sens") * rows, 8), rows)
    o_ref[...] = moved(p_ref[own, :], g_ref[own, :], q_ref[...], entries)


def finish(param, gradient, sums, entries):
    return pl.pallas_call(
        functools.partial(finish_body, entries), in_specs=[VM] * 3, out_specs=VM,
        out_shape=jax.ShapeDtypeStruct((param.shape[0] // 2, param.shape[1]), f32),
        compiler_params=params(4), name="finish",
    )(param, gradient, sums)


def adjoint_half(core, m_ref, k_ref, t_ref, lhs, store):
    freqs = t_ref.shape[2]
    sensors = k_ref.shape[2] // 2
    high, rest = split(m_ref[...].reshape(sensors, freqs))
    both = mm(t_ref[0], jnp.concatenate([high, rest], axis=0), NT)
    spectrum = both[:, :LANES] + (both[:, LANES:] + mm(t_ref[1], high, NT))
    w = row_weights(freqs)
    for m in range(2):
        x = spectrum[m * freqs:(m + 1) * freqs] * w
        high = x.astype(bf16).astype(f32)
        for n, v in enumerate((high, x - high)):
            for chunk in range(freqs // LANES):
                for h in range(2):
                    first = chunk * LANES + h * HALF
                    lhs[pair_row(chunk, h, 2 * n + m), :] = v[first:first + HALF]
    own = pl.ds(pl.multiple_of(core * sensors, LANES), sensors)

    def body(u, pair, rows, first):
        k = jnp.concatenate([k_ref[0, pair, own, :], k_ref[1, pair, own, :]], axis=1)
        o = mm(lhs[rows, :].astype(bf16), k, NN)
        store(rows, jnp.where(first, o[:, :LANES], o[:, LANES:]))

    each_pair(k_ref.shape[1], ADJOINT_UNROLL, body)


def adjoint_mine_body(k_ref, m_ref, t_ref, part_ref, lhs):
    def store(rows, value):
        part_ref[rows, :] = value

    adjoint_half(lax.axis_index("core"), m_ref, k_ref, t_ref, lhs, store)


def adjoint_other_body(k_ref, m_ref, part_ref, t_ref, o_ref, lhs, res):
    freqs, sources = t_ref.shape[2], k_ref.shape[3] // 2

    def store(rows, value):
        res[rows, :] = part_ref[rows, :] + value

    adjoint_half(1 - lax.axis_index("core"), m_ref, k_ref, t_ref, lhs, store)
    low = lax.broadcasted_iota(jnp.int32, (HALF, LANES), 1) < sources
    parts = []
    for chunk in range(freqs // LANES):
        for h in range(2):
            real, imag = [res[pair_row(chunk, h, m), :] + res[pair_row(chunk, h, 2 + m), :] for m in range(2)]
            parts.append(jnp.where(low, real, -real) + pltpu.roll(imag, sources, 1))
    back = jnp.concatenate(parts, axis=0).T
    o_ref[...] = mm3(split(back[:sources]), (t_ref[0, :freqs], t_ref[1, :freqs]), NN) + mm3(
        split(back[sources:]), (t_ref[0, freqs:], t_ref[1, freqs:]), NN
    )


def adjoint_mine(k2, mine, table):
    _, pairs, sensors, width = k2.shape
    spent = pl.CostEstimate(flops=16 * pairs * sensors * width, bytes_accessed=2 * pairs * sensors * width, transcendentals=0)
    return pl.pallas_call(
        adjoint_mine_body, in_specs=[VM] * 3, out_specs=VM,
        out_shape=pltpu.VMEM((pairs * 8, LANES), f32),
        scratch_shapes=[pltpu.VMEM((pairs * 8, LANES), f32)],
        cost_estimate=spent, compiler_params=params(6), name="adjoint_mine",
    )(k2, mine, table)


def adjoint_other(k2, other, part, table):
    _, pairs, _, width = k2.shape
    return pl.pallas_call(
        adjoint_other_body, in_specs=[VM] * 4, out_specs=VM,
        out_shape=jax.ShapeDtypeStruct((width // 2, table.shape[2]), f32),
        scratch_shapes=[pltpu.VMEM((pairs * 8, LANES), f32), pltpu.VMEM((pairs * 8, LANES), f32)],
        compiler_params=params(6), name="adjoint_other",
    )(k2, other, part, table)


def gradient_body(a_ref, b_ref, p_ref, rig_ref, g_ref, q_ref):
    gradient = (a_ref[...] + b_ref[...]) * rig_ref[:, 0:1] * jax.nn.sigmoid(p_ref[...])
    g_ref[...] = gradient
    total = jnp.sum(jnp.sum(gradient * gradient, axis=0, keepdims=True), axis=1, keepdims=True)
    q_ref[...] = jnp.broadcast_to(total, q_ref.shape)


def gradient_and_square(own, received, param, scale_rows, peers):
    return pl.pallas_call(
        gradient_body, in_specs=[VM] * 4, out_specs=[VM] * 2,
        out_shape=[jax.ShapeDtypeStruct(param.shape, f32), jax.ShapeDtypeStruct((peers, LANES), f32)],
        compiler_params=params(4), name="gradient",
    )(own, received, param, scale_rows)


def swap(x, axis):
    return lax.ppermute(x, axis, [(0, 1), (1, 0)])


def to_chips(x):
    return lax.all_to_all(x, "chip", 0, 0)


def exchange_scalars(sums):
    return lax.all_to_all(sums, ("chip", "core"), 0, 0, tiled=True)


def plain_forward(kernel, slip):
    length = slip.shape[1]
    table = sum(table_parts(length).astype(f32))
    spectra = lax.dot_general(slip, table, (NT, ((), ())), precision=highest)
    real, imag = spectra[None, :, :length], spectra[None, :, length:]
    k_real, k_imag = kernel[0].astype(f32), kernel[1].astype(f32)
    out_real = jnp.sum(k_real * real - k_imag * imag, axis=1)
    out_imag = jnp.sum(k_real * imag + k_imag * real, axis=1)
    w = jnp.tile(row_weights(length), (2, 1))
    return jnp.dot(jnp.concatenate([out_real, out_imag], axis=1), table * w, precision=highest)


def plain_adjoint(kernel, residual):
    length = residual.shape[1]
    table = sum(table_parts(length).astype(f32))
    w = jnp.tile(row_weights(length), (2, 1))
    spectrum = lax.dot_general(residual, table * w, (NT, ((), ())), precision=highest)
    real, imag = spectrum[:, None, :length], spectrum[:, None, length:]
    k_real, k_imag = kernel[0].astype(f32), kernel[1].astype(f32)
    back_real = jnp.sum(k_real * real + k_imag * imag, axis=0)
    back_imag = jnp.sum(k_real * imag - k_imag * real, axis=0)
    return jnp.dot(jnp.concatenate([back_real, back_imag], axis=1), table, precision=highest)


def plain_iterations(slip_param, rigidity, kernel, observed, entries):
    chips, cores = lax.axis_size("chip"), lax.axis_size("core")
    own_sources, length = slip_param.shape
    own_count = kernel.shape[1] // (chips * cores)
    src_index = lax.axis_index("chip") * cores + lax.axis_index("core")
    own_observed = lax.dynamic_slice_in_dim(observed, src_index * own_count, own_count, 0)
    param = lax.all_gather(slip_param, "sens", axis=0, tiled=True)
    scale_rows = lax.all_gather(rigidity[:, None], "sens", axis=0, tiled=True)
    misfit = own_observed
    for _ in range(ITERS):
        terms = plain_forward(kernel, scale_rows * jax.nn.softplus(param)).reshape(chips, cores, -1, length)
        partial = lax.psum_scatter(terms, "core", scatter_dimension=1, tiled=False)
        misfit = jnp.sum(to_chips(partial), axis=0) - own_observed
        spread = to_chips(jnp.broadcast_to(misfit[None], (chips, *misfit.shape)))
        residual = lax.all_gather(spread, "core", axis=1, tiled=False)
        back = plain_adjoint(kernel, residual.reshape(-1, length))
        gradient = lax.psum(back, "sens") * scale_rows * jax.nn.sigmoid(param)
        sums = jnp.broadcast_to(jnp.sum(gradient * gradient), (chips * cores, LANES))
        param = moved(param, gradient, exchange_scalars(sums), entries)
    return lax.dynamic_slice_in_dim(param, lax.axis_index("sens") * own_sources, own_sources, 0), misfit


def iterations(slip_param, rigidity, kernel, observed, entries):
    chips, cores = lax.axis_size("chip"), lax.axis_size("core")
    table = table_parts(slip_param.shape[1])
    scales = rigidity.reshape(1, -1)
    others, other_scales = swap(slip_param, "sens"), swap(scales, "sens")
    k2 = relayout(kernel, cores)
    kept, param, scale_rows, res, send = forward_first(k2, slip_param, others, scales, other_scales, table, chips, cores)
    for iteration in range(ITERS):
        if iteration:
            param, res, send = forward_next(k2, kept, param, gradient, sums, scale_rows, table, chips, cores, entries)
        spread, *misfit = misfit_and_spread(to_chips(kept_terms(res, send, table) + swap(send, "core")), observed, iteration == ITERS - 1)
        near = to_chips(spread)
        far = swap(near, "core")
        back = adjoint_other(k2, far, adjoint_mine(k2, near, table), table)
        gradient, sums = gradient_and_square(back, swap(back, "sens"), param, scale_rows, chips * cores)
        sums = exchange_scalars(sums)
    return finish(param, gradient, sums, entries), misfit[0]


def local(slip_param, rigidity, kernel, observed):
    own_sources, length = slip_param.shape
    chips, cores, sens = lax.axis_size("chip"), lax.axis_size("core"), lax.axis_size("sens")
    own_count = kernel.shape[1] // (chips * cores)
    entries = own_sources * sens * chips * cores * length
    fits = (
        sens == 2 and cores == 2 and kernel.shape[2] == HALF and kernel.shape[1] == 2 * LANES
        and length % LANES == 0 and (length // 2) % UNROLL == 0 and (length // 2) % ADJOINT_UNROLL == 0 and own_count == ROWS
    )
    run = iterations if fits else plain_iterations
    return run(slip_param, rigidity, kernel, observed, entries)


def solution(mesh):
    sens, src = mesh.shape["sens"], mesh.shape["src"]
    cores = 2 if src % 2 == 0 else 1
    split_mesh = Mesh(mesh.devices.reshape(sens, src // cores, cores), ("sens", "chip", "core"))
    in_specs = (
        P(("chip", "core", "sens"), None),
        P(("chip", "core", "sens")),
        P(None, "sens", ("chip", "core"), None),
        P("sens", None),
    )
    out_specs = (P(("chip", "core", "sens"), None), P(("sens", "chip", "core"), None))
    return jax.shard_map(local, mesh=split_mesh, in_specs=in_specs, out_specs=out_specs, check_vma=False)
```

```python
import functools
import math

import jax
import jax.numpy as jnp
import numpy as np
from jax import lax
from jax.experimental import pallas as pl
from jax.experimental.pallas import tpu as pltpu
from jax.sharding import Mesh, PartitionSpec as P

ITERS = 3

highest = lax.Precision.HIGHEST
step_rate = 0.3
epsilon = 1e-06
f32, bf16 = jnp.float32, jnp.bfloat16
LANES = 128
HALF = LANES // 2
NN, NT = ((1,), (0,)), ((1,), (1,))
VM = pl.BlockSpec(memory_space=pltpu.VMEM)
ROWS = 16
PITCH = 196
BUFFERS = 6
UNROLL = 96
ADJOINT_UNROLL = 96


def table_parts(length):
    padded = 2 * length
    phases = np.outer(np.arange(length), np.arange(length)) % padded * (2.0 * math.pi / padded)
    table = np.concatenate([np.cos(phases), -np.sin(phases)], axis=0).astype(np.float32)
    high = table.astype(jnp.bfloat16)
    return jnp.asarray(np.stack([high, (table - high.astype(np.float32)).astype(jnp.bfloat16)]))


def row_weights(length):
    row = lax.broadcasted_iota(jnp.int32, (length, 1), 0)
    return jnp.where(row == 0, 0.5 / length, 1.0 / length).astype(f32)


def params(mib):
    return pltpu.CompilerParams(vmem_limit_bytes=mib << 20)


def mm(a, b, dims):
    return lax.dot_general(a, b, (dims, ((), ())), preferred_element_type=f32)


def split(x):
    high = x.astype(bf16)
    return high, (x - high.astype(f32)).astype(bf16)


def mm3(a, b, dims):
    return mm(a[0], b[0], dims) + (mm(a[0], b[1], dims) + mm(a[1], b[0], dims))


def relayout_body(cores, k_hbm, out_ref, buf, stage, sem):
    freqs = k_hbm.shape[3]
    pairs = freqs // 2
    steps = k_hbm.shape[1] // ROWS
    chips = steps // cores
    same = lax.broadcasted_iota(jnp.int32, (LANES, LANES), 0) == lax.broadcasted_iota(jnp.int32, (LANES, LANES), 1)
    eye = same.astype(f32).astype(bf16)

    def copies(i):
        slot = lax.rem(i, BUFFERS)
        rows = pl.ds((lax.rem(i, chips) * cores + lax.div(i, chips)) * ROWS, ROWS)
        return [pltpu.make_async_copy(k_hbm.at[c, rows], buf.at[slot, c], sem.at[slot, c]) for c in range(2)]

    def start(i):
        for copy in copies(i):
            copy.start()

    for i in range(BUFFERS - 1):
        start(i)

    def step(i, carry):
        slot = lax.rem(i, BUFFERS)
        for copy in copies(i):
            copy.wait()

        @pl.when(i + BUFFERS - 1 < steps)
        def _():
            start(i + BUFFERS - 1)

        for r in range(0, ROWS, 2):
            x = jnp.concatenate([buf[slot, c, r + j] for j in range(2) for c in range(2)], axis=0)
            for chunk in range(freqs // LANES):
                part = x[:, chunk * LANES:(chunk + 1) * LANES]
                o = mm(eye, part, NT) if r % 4 == 0 else part.T.astype(f32)
                for j in range(2):
                    for h in range(2):
                        rows = pl.ds((r + j) * PITCH + chunk * HALF, HALF)
                        stage[h, rows, :] = o[h * HALF:(h + 1) * HALF, j * LANES:(j + 1) * LANES]
        rows = pl.ds(pl.multiple_of(i * ROWS, ROWS), ROWS)
        for h in range(2):
            for pair in range(pairs):
                out_ref[h, pair, rows, :] = stage[h, pl.ds(pair, ROWS, stride=PITCH), :].astype(bf16)
        return carry

    lax.fori_loop(0, steps, step, 0)


def relayout(kernel, cores):
    _, sensors, sources, freqs = kernel.shape
    return pl.pallas_call(
        functools.partial(relayout_body, cores),
        in_specs=[pl.BlockSpec(memory_space=pl.ANY)],
        out_specs=VM,
        out_shape=pltpu.VMEM((2, freqs // 2, sensors, 2 * sources), bf16),
        scratch_shapes=[
            pltpu.VMEM((BUFFERS, 2, ROWS, sources, freqs), bf16),
            pltpu.VMEM((2, ROWS * PITCH, LANES), f32),
            pltpu.SemaphoreType.DMA((BUFFERS, 2)),
        ],
        compiler_params=params(16),
        name="relayout",
    )(kernel)


def pair_row(chunk, h, m):
    return pl.ds(chunk * HALF * 8 + 4 * h + m, HALF, stride=8)


def tile(k_ref, pair):
    return jnp.concatenate([k_ref[0, pair], k_ref[1, pair]], axis=1)


def turned(k_ref, pair):
    return [[k_ref[h, pair, c * LANES:(c + 1) * LANES, :].T for c in range(2)] for h in range(2)]


def joined(blocks):
    return jnp.concatenate([jnp.concatenate(row, axis=1) for row in blocks], axis=0)


def each_pair(pairs, unroll, body):
    first = lax.broadcasted_iota(jnp.int32, (8, LANES), 0) < 4

    def step(i, carry):
        for u in range(unroll):
            pair = i * unroll + u
            body(u, pair, pl.ds(pl.multiple_of(pair * 8, 8), 8), first)
        return carry

    lax.fori_loop(0, pairs // unroll, step, 0)


def forward_core(param, scale_rows, product, k_ref, t_ref, res, send_ref, lhs):
    freqs, sources = param.shape[1], param.shape[0]
    high, rest = split(scale_rows * jax.nn.softplus(param))
    z = mm(t_ref[0], jnp.concatenate([high, high, rest, rest], axis=0), NT)
    z = z[:, :LANES] + (z[:, LANES:] + mm(t_ref[1], jnp.concatenate([high, high], axis=0), NT))
    low = lax.broadcasted_iota(jnp.int32, (freqs, LANES), 1) < sources
    real, imag = z[:freqs], z[freqs:]
    for m, x in enumerate((jnp.where(low, real, -imag), jnp.where(low, imag, real))):
        high = x.astype(bf16).astype(f32)
        for n, v in enumerate((high, x - high)):
            for chunk in range(freqs // LANES):
                for h in range(2):
                    first = chunk * LANES + h * HALF
                    lhs[pair_row(chunk, h, 2 * n + m), :] = v[first:first + HALF]

    def body(u, pair, rows, first):
        v = lhs[rows, :]
        a = jnp.concatenate([jnp.where(first, v, 0.0), jnp.where(first, 0.0, v)], axis=1).astype(bf16)
        o = product(a, u, pair)
        res[0, rows, :] = o[:, :LANES]
        res[1, rows, :] = o[:, LANES:]

    each_pair(k_ref.shape[1], UNROLL, body)
    send_ref[...] = predicted(res, 1 - lax.axis_index("core"), t_ref).reshape(send_ref.shape)


def predicted(res, core, t_ref):
    freqs = t_ref.shape[2]
    w = row_weights(freqs)
    halves = []
    for m in range(2):
        parts = []
        for chunk in range(freqs // LANES):
            for h in range(2):
                parts.append(res[core, pair_row(chunk, h, m), :] + res[core, pair_row(chunk, h, 2 + m), :])
        halves.append(jnp.concatenate(parts, axis=0) * w)
    spectrum = jnp.concatenate(halves, axis=0).T
    return mm3(split(spectrum), (t_ref[0], t_ref[1]), NN)


def keep_body(res_ref, t_ref, keep_ref):
    keep_ref[...] = predicted(res_ref, lax.axis_index("core"), t_ref).reshape(keep_ref.shape)


def kept_terms(res, send, table):
    spent = pl.CostEstimate(flops=12 * res.size * table.shape[2], bytes_accessed=8 * res.size, transcendentals=0)
    return pl.pallas_call(
        keep_body, in_specs=[VM] * 2, out_specs=VM, out_shape=jax.ShapeDtypeStruct(send.shape, f32),
        cost_estimate=spent, compiler_params=params(4), name="keep",
    )(res, table)


def forward_first_body(k_ref, mine_ref, other_ref, rig_mine_ref, rig_other_ref, t_ref, kept_ref, new_ref, rig_ref, res, send_ref, lhs, both, scales):
    sens = lax.axis_index("sens")
    rows = mine_ref.shape[0]
    same = lax.broadcasted_iota(jnp.int32, (rows, rows), 0) == lax.broadcasted_iota(jnp.int32, (rows, rows), 1)
    for place, p_ref, r_ref in ((sens, mine_ref, rig_mine_ref), (1 - sens, other_ref, rig_other_ref)):
        both[place] = p_ref[...]
        column = jnp.sum(jnp.where(same, jnp.broadcast_to(r_ref[...], (rows, rows)), 0.0), axis=1, keepdims=True)
        scales[place] = jnp.broadcast_to(column, (rows, LANES))
    param = both[...].reshape(new_ref.shape)
    scale_rows = scales[...].reshape(rig_ref.shape)
    new_ref[...] = param
    rig_ref[...] = scale_rows

    def product(a, u, pair):
        if u % 12 in (0, 3, 6, 11):
            return mm(a, tile(k_ref, pair), NT)
        blocks = turned(k_ref, pair)
        if u % 4 == 1:
            for h in range(2):
                for c in range(2):
                    kept_ref[c, pair // 4, h * LANES:(h + 1) * LANES, :] = blocks[h][c]
        return mm(a, joined(blocks), NN)

    forward_core(param, scale_rows[:, 0:1], product, k_ref, t_ref, res, send_ref, lhs)


def moved(param, gradient, sums, entries):
    square_sum = jnp.sum(sums[:, 0:1], axis=0, keepdims=True)
    root_mean = jnp.sqrt(square_sum / entries + epsilon)
    return param - step_rate * gradient / root_mean


def forward_next_body(entries, k_ref, kept_ref, p_ref, g_ref, q_ref, rig_ref, t_ref, new_ref, res, send_ref, lhs):
    param = moved(p_ref[...], g_ref[...], q_ref[...], entries)
    new_ref[...] = param

    def product(a, u, pair):
        if u % 4 == 1:
            return mm(a, tile(kept_ref, pair // 4), NN)
        if u % 6 == 0:
            return mm(a, tile(k_ref, pair), NT)
        return mm(a, joined(turned(k_ref, pair)), NN)

    forward_core(param, rig_ref[:, 0:1], product, k_ref, t_ref, res, send_ref, lhs)


def forward_spaces(k2, length, chips, cores):
    _, pairs, sensors, _ = k2.shape
    rows = sensors // (chips * cores)
    outs = [pltpu.VMEM((2, pairs * 8, LANES), f32), jax.ShapeDtypeStruct((chips, rows, length), f32)]
    scratch = [pltpu.VMEM((pairs * 8, LANES), f32)]
    return outs, scratch


def forward_first(k2, mine, other, rig_mine, rig_other, table, chips, cores):
    sources, length = 2 * mine.shape[0], table.shape[2]
    outs, scratch = forward_spaces(k2, length, chips, cores)
    return pl.pallas_call(
        forward_first_body, in_specs=[VM] * 6, out_specs=[VM] * 5,
        out_shape=[pltpu.VMEM((2, k2.shape[1] // 4, 2 * k2.shape[3], k2.shape[2] // 2), bf16), jax.ShapeDtypeStruct((sources, length), f32), jax.ShapeDtypeStruct((sources, LANES), f32)] + outs,
        scratch_shapes=scratch + [pltpu.VMEM((2, *mine.shape), f32), pltpu.VMEM((2, mine.shape[0], LANES), f32)],
        compiler_params=params(6), name="forward_first",
    )(k2, mine, other, rig_mine, rig_other, table)


def forward_next(k2, kept, param, gradient, sums, scale_rows, table, chips, cores, entries):
    outs, scratch = forward_spaces(k2, param.shape[1], chips, cores)
    return pl.pallas_call(
        functools.partial(forward_next_body, entries), in_specs=[VM] * 7, out_specs=[VM] * 3,
        out_shape=[jax.ShapeDtypeStruct(param.shape, f32)] + outs,
        scratch_shapes=scratch, compiler_params=params(6), name="forward_next",
    )(k2, kept, param, gradient, sums, scale_rows, table)


def misfit_body(parts_ref, obs_ref, spread_ref, m_ref=None):
    chips, rows, _ = parts_ref.shape
    first = (lax.axis_index("chip") * lax.axis_size("core") + lax.axis_index("core")) * rows
    total = parts_ref[0]
    for c in range(1, chips):
        total = total + parts_ref[c]
    misfit = total - obs_ref[pl.ds(pl.multiple_of(first, 8), rows), :]
    for c in range(chips):
        spread_ref[c] = misfit
    if m_ref is not None:
        m_ref[...] = misfit


def misfit_and_spread(parts, observed, last):
    outs = [jax.ShapeDtypeStruct(parts.shape, f32)]
    if last:
        outs.append(jax.ShapeDtypeStruct(parts.shape[1:], f32))
    return pl.pallas_call(
        misfit_body, in_specs=[VM] * 2, out_specs=[VM] * len(outs), out_shape=outs,
        compiler_params=params(4), name="misfit",
    )(parts, observed)


def finish_body(entries, p_ref, g_ref, q_ref, o_ref):
    rows = o_ref.shape[0]
    own = pl.ds(pl.multiple_of(lax.axis_index("sens") * rows, 8), rows)
    o_ref[...] = moved(p_ref[own, :], g_ref[own, :], q_ref[...], entries)


def finish(param, gradient, sums, entries):
    return pl.pallas_call(
        functools.partial(finish_body, entries), in_specs=[VM] * 3, out_specs=VM,
        out_shape=jax.ShapeDtypeStruct((param.shape[0] // 2, param.shape[1]), f32),
        compiler_params=params(4), name="finish",
    )(param, gradient, sums)


def adjoint_half(core, m_ref, k_ref, t_ref, lhs, store):
    freqs = t_ref.shape[2]
    sensors = k_ref.shape[2] // 2
    high, rest = split(m_ref[...].reshape(sensors, freqs))
    both = mm(t_ref[0], jnp.concatenate([high, rest], axis=0), NT)
    spectrum = both[:, :LANES] + (both[:, LANES:] + mm(t_ref[1], high, NT))
    w = row_weights(freqs)
    for m in range(2):
        x = spectrum[m * freqs:(m + 1) * freqs] * w
        high = x.astype(bf16).astype(f32)
        for n, v in enumerate((high, x - high)):
            for chunk in range(freqs // LANES):
                for h in range(2):
                    first = chunk * LANES + h * HALF
                    lhs[pair_row(chunk, h, 2 * n + m), :] = v[first:first + HALF]
    own = pl.ds(pl.multiple_of(core * sensors, LANES), sensors)

    def body(u, pair, rows, first):
        k = jnp.concatenate([k_ref[0, pair, own, :], k_ref[1, pair, own, :]], axis=1)
        o = mm(lhs[rows, :].astype(bf16), k, NN)
        store(rows, jnp.where(first, o[:, :LANES], o[:, LANES:]))

    each_pair(k_ref.shape[1], ADJOINT_UNROLL, body)


def adjoint_mine_body(k_ref, m_ref, t_ref, part_ref, lhs):
    def store(rows, value):
        part_ref[rows, :] = value

    adjoint_half(lax.axis_index("core"), m_ref, k_ref, t_ref, lhs, store)


def adjoint_other_body(k_ref, m_ref, part_ref, t_ref, o_ref, lhs, res):
    freqs, sources = t_ref.shape[2], k_ref.shape[3] // 2

    def store(rows, value):
        res[rows, :] = part_ref[rows, :] + value

    adjoint_half(1 - lax.axis_index("core"), m_ref, k_ref, t_ref, lhs, store)
    low = lax.broadcasted_iota(jnp.int32, (HALF, LANES), 1) < sources
    parts = []
    for chunk in range(freqs // LANES):
        for h in range(2):
            real, imag = [res[pair_row(chunk, h, m), :] + res[pair_row(chunk, h, 2 + m), :] for m in range(2)]
            parts.append(jnp.where(low, real, -real) + pltpu.roll(imag, sources, 1))
    back = jnp.concatenate(parts, axis=0).T
    o_ref[...] = mm3(split(back[:sources]), (t_ref[0, :freqs], t_ref[1, :freqs]), NN) + mm3(
        split(back[sources:]), (t_ref[0, freqs:], t_ref[1, freqs:]), NN
    )


def adjoint_mine(k2, mine, table):
    _, pairs, sensors, width = k2.shape
    spent = pl.CostEstimate(flops=16 * pairs * sensors * width, bytes_accessed=2 * pairs * sensors * width, transcendentals=0)
    return pl.pallas_call(
        adjoint_mine_body, in_specs=[VM] * 3, out_specs=VM,
        out_shape=pltpu.VMEM((pairs * 8, LANES), f32),
        scratch_shapes=[pltpu.VMEM((pairs * 8, LANES), f32)],
        cost_estimate=spent, compiler_params=params(6), name="adjoint_mine",
    )(k2, mine, table)


def adjoint_other(k2, other, part, table):
    _, pairs, _, width = k2.shape
    return pl.pallas_call(
        adjoint_other_body, in_specs=[VM] * 4, out_specs=VM,
        out_shape=jax.ShapeDtypeStruct((width // 2, table.shape[2]), f32),
        scratch_shapes=[pltpu.VMEM((pairs * 8, LANES), f32), pltpu.VMEM((pairs * 8, LANES), f32)],
        compiler_params=params(6), name="adjoint_other",
    )(k2, other, part, table)


def gradient_body(a_ref, b_ref, p_ref, rig_ref, g_ref, q_ref):
    gradient = (a_ref[...] + b_ref[...]) * rig_ref[:, 0:1] * jax.nn.sigmoid(p_ref[...])
    g_ref[...] = gradient
    total = jnp.sum(jnp.sum(gradient * gradient, axis=0, keepdims=True), axis=1, keepdims=True)
    q_ref[...] = jnp.broadcast_to(total, q_ref.shape)


def gradient_and_square(own, received, param, scale_rows, peers):
    return pl.pallas_call(
        gradient_body, in_specs=[VM] * 4, out_specs=[VM] * 2,
        out_shape=[jax.ShapeDtypeStruct(param.shape, f32), jax.ShapeDtypeStruct((peers, LANES), f32)],
        compiler_params=params(4), name="gradient",
    )(own, received, param, scale_rows)


def swap(x, axis):
    return lax.ppermute(x, axis, [(0, 1), (1, 0)])


def to_chips(x):
    return lax.all_to_all(x, "chip", 0, 0)


def exchange_scalars(sums):
    return lax.all_to_all(sums, ("chip", "core"), 0, 0, tiled=True)


def plain_forward(kernel, slip):
    length = slip.shape[1]
    table = sum(table_parts(length).astype(f32))
    spectra = lax.dot_general(slip, table, (NT, ((), ())), precision=highest)
    real, imag = spectra[None, :, :length], spectra[None, :, length:]
    k_real, k_imag = kernel[0].astype(f32), kernel[1].astype(f32)
    out_real = jnp.sum(k_real * real - k_imag * imag, axis=1)
    out_imag = jnp.sum(k_real * imag + k_imag * real, axis=1)
    w = jnp.tile(row_weights(length), (2, 1))
    return jnp.dot(jnp.concatenate([out_real, out_imag], axis=1), table * w, precision=highest)


def plain_adjoint(kernel, residual):
    length = residual.shape[1]
    table = sum(table_parts(length).astype(f32))
    w = jnp.tile(row_weights(length), (2, 1))
    spectrum = lax.dot_general(residual, table * w, (NT, ((), ())), precision=highest)
    real, imag = spectrum[:, None, :length], spectrum[:, None, length:]
    k_real, k_imag = kernel[0].astype(f32), kernel[1].astype(f32)
    back_real = jnp.sum(k_real * real + k_imag * imag, axis=0)
    back_imag = jnp.sum(k_real * imag - k_imag * real, axis=0)
    return jnp.dot(jnp.concatenate([back_real, back_imag], axis=1), table, precision=highest)


def plain_iterations(slip_param, rigidity, kernel, observed, entries):
    chips, cores = lax.axis_size("chip"), lax.axis_size("core")
    own_sources, length = slip_param.shape
    own_count = kernel.shape[1] // (chips * cores)
    src_index = lax.axis_index("chip") * cores + lax.axis_index("core")
    own_observed = lax.dynamic_slice_in_dim(observed, src_index * own_count, own_count, 0)
    param = lax.all_gather(slip_param, "sens", axis=0, tiled=True)
    scale_rows = lax.all_gather(rigidity[:, None], "sens", axis=0, tiled=True)
    misfit = own_observed
    for _ in range(ITERS):
        terms = plain_forward(kernel, scale_rows * jax.nn.softplus(param)).reshape(chips, cores, -1, length)
        partial = lax.psum_scatter(terms, "core", scatter_dimension=1, tiled=False)
        misfit = jnp.sum(to_chips(partial), axis=0) - own_observed
        spread = to_chips(jnp.broadcast_to(misfit[None], (chips, *misfit.shape)))
        residual = lax.all_gather(spread, "core", axis=1, tiled=False)
        back = plain_adjoint(kernel, residual.reshape(-1, length))
        gradient = lax.psum(back, "sens") * scale_rows * jax.nn.sigmoid(param)
        sums = jnp.broadcast_to(jnp.sum(gradient * gradient), (chips * cores, LANES))
        param = moved(param, gradient, exchange_scalars(sums), entries)
    return lax.dynamic_slice_in_dim(param, lax.axis_index("sens") * own_sources, own_sources, 0), misfit


def iterations(slip_param, rigidity, kernel, observed, entries):
    chips, cores = lax.axis_size("chip"), lax.axis_size("core")
    table = table_parts(slip_param.shape[1])
    scales = rigidity.reshape(1, -1)
    others, other_scales = swap(slip_param, "sens"), swap(scales, "sens")
    k2 = relayout(kernel, cores)
    kept, param, scale_rows, res, send = forward_first(k2, slip_param, others, scales, other_scales, table, chips, cores)
    for iteration in range(ITERS):
        if iteration:
            param, res, send = forward_next(k2, kept, param, gradient, sums, scale_rows, table, chips, cores, entries)
        spread, *misfit = misfit_and_spread(to_chips(kept_terms(res, send, table) + swap(send, "core")), observed, iteration == ITERS - 1)
        near = to_chips(spread)
        far = swap(near, "core")
        back = adjoint_other(k2, far, adjoint_mine(k2, near, table), table)
        gradient, sums = gradient_and_square(back, swap(back, "sens"), param, scale_rows, chips * cores)
        sums = exchange_scalars(sums)
    return finish(param, gradient, sums, entries), misfit[0]


def local(slip_param, rigidity, kernel, observed):
    own_sources, length = slip_param.shape
    chips, cores, sens = lax.axis_size("chip"), lax.axis_size("core"), lax.axis_size("sens")
    own_count = kernel.shape[1] // (chips * cores)
    entries = own_sources * sens * chips * cores * length
    fits = (
        sens == 2 and cores == 2 and kernel.shape[2] == HALF and kernel.shape[1] == 2 * LANES
        and length % LANES == 0 and (length // 2) % UNROLL == 0 and (length // 2) % ADJOINT_UNROLL == 0 and own_count == ROWS
    )
    run = iterations if fits else plain_iterations
    return run(slip_param, rigidity, kernel, observed, entries)


def solution(mesh):
    sens, src = mesh.shape["sens"], mesh.shape["src"]
    cores = 2 if src % 2 == 0 else 1
    split_mesh = Mesh(mesh.devices.reshape(sens, src // cores, cores), ("sens", "chip", "core"))
    in_specs = (
        P(("chip", "core", "sens"), None),
        P(("chip", "core", "sens")),
        P(None, "sens", ("chip", "core"), None),
        P("sens", None),
    )
    out_specs = (P(("chip", "core", "sens"), None), P(("sens", "chip", "core"), None))
    return jax.shard_map(local, mesh=split_mesh, in_specs=in_specs, out_specs=out_specs, check_vma=False)
```
